32 devices in a mesh: groups: 2 (over x), cols: 16 (over z, y, core).
Axes of the slice: x: 2, y: 2, z: 4, core: 2. Of those that a mesh axis runs over, the one named last changes fastest.
Arguments:
- clip_tokens: bfloat16 [14, 32, 64, 512], P('groups', None, 'cols'), parts along dimension 0, may hold values from -6 to 6
- cotangent: bfloat16 [14, 32, 64, 512], P('groups', None, 'cols'), parts along dimension 0, may hold values from -6 to 6
- gain_attn: float32 [512], replicated, may hold values from 0.25 to 1.75
- w_query: bfloat16 [512, 512], replicated, may hold values from -0.25 to 0.25
- w_key: bfloat16 [512, 512], replicated, may hold values from -0.25 to 0.25
- w_value: bfloat16 [512, 512], replicated, may hold values from -0.25 to 0.25
- w_out: bfloat16 [512, 512], replicated, may hold values from -0.25 to 0.25
- gain_first: float32 [512], replicated, may hold values from 0.25 to 1.75
- conv_first: bfloat16 [3, 3, 512, 512], replicated, may hold values from -0.09375 to 0.09375
- gain_second: float32 [512], replicated, may hold values from 0.25 to 1.75
- conv_second: bfloat16 [3, 3, 512, 512], replicated, may hold values from -0.09375 to 0.09375
- matching: int32 [7], replicated, may hold values from 0 to 6, as said below
- block_lists: int32 [7, 16, 2], replicated, may hold values from 0 to 15, as said below
- counts: int32 [7, 16], replicated, may hold values from 1 to 2
Outputs:
- result: bfloat16 [14, 32, 64, 512], P('groups', None, 'cols'), parts along dimension 0
- d_clip: bfloat16 [14, 32, 64, 512], P('groups', None, 'cols'), parts along dimension 0
The draws below stay inside these ranges and needn't reach their ends.
There are 2 independent parts, one for each index of `groups`. The reference program is written for one: setup_inputs(seed, part) draws one part's arguments, and reference() takes and returns one part's arrays. A program takes and returns all parts, laid end to end along the dimension named above; an argument that names none is the same for every part. Nothing has to cross between parts.
Inputs may be any that keep to these rules, and one draw needn't show every extreme that they name: `matching`: each camera's partner is another camera, and every camera is the partner of exactly one camera. At one tile column j, the 14 entries block_lists[c, j, s] over all cameras c and slots s are pairwise distinct.
All inputs are finite; a program needn't handle non-finite values.
Results may differ from the reference program's by a relative error of at most 0.0075.
Values may be sent and summed in bfloat16 or wider, within the bound.
No kernel may reach another device: no remote copies, remote signals or barrier semaphores. Data moves between devices by JAX's collectives and lax.ppermute only.
A program may use at most 320 MiB of HBM per device.

```python
import jax
import jax.numpy as jnp
from jax import lax

HEADS = 8
HEAD_DIM = 64
D = 512
CAMS = 7
ROWS = 32
TILE_W = 4
BLK = 128
TILES = 16
COLS = 64
KSEL = 2
VIEWS = 7


def draw_matching(key, part):
    order = jax.random.permutation(key, CAMS).astype(jnp.int32)
    return jnp.zeros((CAMS,), jnp.int32).at[order].set(jnp.roll(order, -1))


def draw_block_lists(key, part):

    def one_column(column):
        return jax.random.permutation(jax.random.fold_in(key, column), TILES)[:CAMS * KSEL]
    chosen = jax.vmap(one_column)(jnp.arange(TILES))
    return jnp.transpose(chosen.reshape(TILES, CAMS, KSEL), (1, 0, 2)).astype(jnp.int32)


def plant(drawn, key, least, top_value):
    dims = drawn.shape
    place = [jax.random.randint(jax.random.fold_in(key, axis), (), 0, dims[axis]) for axis in range(len(dims))]
    drawn = drawn.at[tuple(place)].set(least)
    longest = dims.index(max(dims))
    place[longest] = (place[longest] + 1) % dims[longest]
    return drawn.at[tuple(place)].set(top_value)


def block_levels(rng, extent, pieces, smallest, top_value):
    gain = 1.0
    for dim, shards_of in pieces:
        heights = jax.random.uniform(jax.random.fold_in(jax.random.fold_in(rng, 6), dim), (shards_of,), jnp.float32, smallest / len(pieces), top_value / len(pieces))
        gain = gain * jnp.repeat(jnp.exp(heights), extent[dim] // shards_of).reshape((-1,) + (1,) * (len(extent) - 1 - dim))
    return gain


def scatter_about(stream_key, extent, deviation, limit, cuts=(), kind=jnp.bfloat16):
    values = deviation * jax.random.normal(stream_key, extent, jnp.float32)
    if cuts:
        values = values * block_levels(stream_key, extent, cuts, -0.22, 0.18)
    return jnp.clip(values, -limit, limit).astype(kind)


def setup_inputs(seed: int = 0, part: int = 0) -> dict:
    key_of = jax.random.split(jax.random.key(seed), 15)
    part_splits = jax.random.split(jax.random.fold_in(key_of[14], part), 15)
    return {
        "clip_tokens": scatter_about(part_splits[0], (VIEWS, ROWS, COLS, D), 1.0, 6.0, ((2, 16),)),
        "cotangent": scatter_about(part_splits[1], (VIEWS, ROWS, COLS, D), 1.0, 6.0, ((2, 16),)),
        "gain_attn": jnp.clip(1.0 + 0.15 * jax.random.normal(key_of[2], (D,), jnp.float32), 0.25, 1.75),
        "w_query": scatter_about(key_of[3], (D, D), D ** -0.5, 0.25),
        "w_key": scatter_about(key_of[4], (D, D), D ** -0.5, 0.25),
        "w_value": scatter_about(key_of[5], (D, D), D ** -0.5, 0.25),
        "w_out": scatter_about(key_of[6], (D, D), D ** -0.5, 0.25),
        "gain_first": jnp.clip(1.0 + 0.15 * jax.random.normal(key_of[7], (D,), jnp.float32), 0.25, 1.75),
        "conv_first": scatter_about(key_of[8], (3, 3, D, D), (9 * D) ** -0.5, 0.09375),
        "gain_second": jnp.clip(1.0 + 0.15 * jax.random.normal(key_of[9], (D,), jnp.float32), 0.25, 1.75),
        "conv_second": scatter_about(key_of[10], (3, 3, D, D), (9 * D) ** -0.5, 0.09375),
        "matching": draw_matching(jax.random.fold_in(key_of[14], 71), part),
        "block_lists": draw_block_lists(jax.random.fold_in(key_of[14], 71), part),
        "counts": plant(jax.random.randint(key_of[13], (CAMS, TILES), 1, KSEL + 1), jax.random.fold_in(key_of[13], 1), 1, KSEL).astype(jnp.int32),
    }


EPSILON = 1e-06

def row_norm(values, gain_vec):
    inv_rms = lax.rsqrt(lax.optimization_barrier(jnp.mean(values * values, axis=-1, keepdims=True)) + EPSILON)
    return (values * inv_rms * gain_vec, inv_rms)

def norm_back(gradient, values, inv_rms, gain_vec):
    weighted = gradient * gain_vec
    cubed = inv_rms * inv_rms * inv_rms
    return inv_rms * weighted - values * cubed * lax.optimization_barrier(jnp.mean(weighted * values, axis=-1, keepdims=True))

def silu_slope(inputs):
    sigmoid = jax.nn.sigmoid(inputs)
    return sigmoid * (1.0 + inputs * (1.0 - sigmoid))

def head_product(tokens, weight):
    product = jnp.dot(tokens, weight, preferred_element_type=jnp.float32)
    return product.reshape(product.shape[0], HEADS, -1)

def conv_forward(activation, kernel):
    view_count, row_count, col_count, model_width = activation.shape
    padded = jnp.pad(activation, ((0, 0), (1, 1), (1, 1), (0, 0)))
    summed = jnp.zeros((view_count * row_count * col_count, kernel.shape[3]), jnp.float32)
    for vertical in range(3):
        for across in range(3):
            window = padded[:, vertical:vertical + row_count, across:across + col_count, :].reshape(-1, model_width)
            summed = summed + jnp.dot(window, kernel[vertical, across], preferred_element_type=jnp.float32)
    return summed

def conv_backward(gradient, kernel):
    view_count, row_count, col_count, model_width = gradient.shape
    padded = jnp.pad(gradient, ((0, 0), (1, 1), (1, 1), (0, 0)))
    summed = jnp.zeros((view_count * row_count * col_count, kernel.shape[2]), jnp.float32)
    for vertical in range(3):
        for across in range(3):
            window = padded[:, 2 - vertical:2 - vertical + row_count, 2 - across:2 - across + col_count, :].reshape(-1, model_width)
            summed = summed + jnp.dot(window, kernel[vertical, across].T, preferred_element_type=jnp.float32)
    return summed

def attention_weights(queries, keys, live_mask):
    head_size = queries.shape[-1]
    raw = jnp.einsum('cqhd,ckhd->chqk', queries.astype(jnp.float32), keys.astype(jnp.float32)) * head_size ** (-0.5)
    grown = jnp.exp(raw) * live_mask[:, None, None, :]
    return grown / lax.optimization_barrier(jnp.sum(grown, axis=-1, keepdims=True))

def to_blocks(flat):
    shaped = flat.reshape(VIEWS, ROWS, TILES, TILE_W, -1)
    return jnp.transpose(shaped, (0, 2, 1, 3, 4)).reshape(VIEWS, TILES, BLK, -1)

def from_blocks(blocks):
    shaped = blocks.reshape(VIEWS, TILES, ROWS, TILE_W, -1)
    return jnp.transpose(shaped, (0, 2, 1, 3, 4)).reshape(VIEWS * ROWS * TILES * TILE_W, -1)

def reference(clip_tokens, cotangent, gain_attn, w_query, w_key, w_value, w_out, gain_first, conv_first, gain_second, conv_second, matching, block_lists, counts):
    model_width = HEADS * HEAD_DIM
    view_ids = jnp.arange(VIEWS, dtype=jnp.int32)
    view_camera = (view_ids % CAMS).astype(jnp.int32)
    partner = (view_ids // CAMS * CAMS + jnp.take(matching, view_camera)).astype(jnp.int32)
    view_lists = jnp.take(block_lists, view_camera, axis=0)
    view_counts = jnp.take(counts, view_camera, axis=0)
    inputs = clip_tokens.astype(jnp.float32).reshape(-1, model_width)
    normed, inv_in = row_norm(inputs, gain_attn)
    rows_in = normed.astype(jnp.bfloat16)
    query_pre = head_product(rows_in, w_query)
    query_hat, query_inv = row_norm(query_pre, 1.0)
    key_pre = head_product(rows_in, w_key)
    key_hat, key_inv = row_norm(key_pre, 1.0)
    values = jnp.dot(rows_in, w_value, preferred_element_type=jnp.float32).astype(jnp.bfloat16)
    query_blocks = to_blocks(query_hat.astype(jnp.bfloat16).reshape(-1, model_width))
    pair_blocks = to_blocks(jnp.concatenate([key_hat.astype(jnp.bfloat16).reshape(-1, model_width), values], axis=-1))
    key_pre_blocks = to_blocks(key_pre.reshape(-1, model_width))
    key_inv_blocks = to_blocks(key_inv.reshape(-1, HEADS))
    columns = jnp.arange(TILES, dtype=jnp.int32)
    slot_ids = jnp.arange(KSEL, dtype=jnp.int32)

    def key_set(column):
        listed = view_lists[:, column]
        far_blocks = pair_blocks[partner[:, None], listed]
        own_block = pair_blocks[:, column][:, None]
        all_blocks = jnp.concatenate([own_block, far_blocks], axis=1).reshape(VIEWS, -1, 2 * model_width)
        live_far = (slot_ids[None, :] < view_counts[:, column][:, None]).astype(jnp.float32)
        live_mask = jnp.repeat(jnp.concatenate([jnp.ones((VIEWS, 1), jnp.float32), live_far], axis=1), BLK, axis=1)
        key_part = all_blocks[..., :model_width].reshape(VIEWS, -1, HEADS, HEAD_DIM)
        value_part = all_blocks[..., model_width:].reshape(VIEWS, -1, HEADS, HEAD_DIM)
        queries = query_blocks[:, column].reshape(VIEWS, BLK, HEADS, HEAD_DIM)
        return (queries, key_part, value_part, live_mask)

    def forward_column(column):
        queries, key_part, value_part, live_mask = key_set(column)
        weights = attention_weights(queries, key_part, live_mask)
        rounded = weights.astype(jnp.bfloat16)
        mixed = jnp.einsum('vhqk,vkhd->vqhd', rounded.astype(jnp.float32), value_part.astype(jnp.float32))
        return mixed.astype(jnp.bfloat16)
    mixed_all = lax.map(forward_column, columns)
    mixed = from_blocks(jnp.transpose(mixed_all, (1, 0, 2, 3, 4)).reshape(VIEWS, TILES, BLK, model_width))
    lifted = (inputs + jnp.dot(mixed, w_out, preferred_element_type=jnp.float32)).astype(jnp.bfloat16)
    lifted_f = lifted.astype(jnp.float32)
    first_in, inv_two = row_norm(lifted_f, gain_first)
    act_one = jax.nn.silu(first_in).astype(jnp.bfloat16)
    conv_one = conv_forward(act_one.reshape(VIEWS, ROWS, COLS, model_width), conv_first)
    second_in, inv_three = row_norm(conv_one, gain_second)
    act_two = jax.nn.silu(second_in).astype(jnp.bfloat16)
    conv_two = conv_forward(act_two.reshape(VIEWS, ROWS, COLS, model_width), conv_second)
    result = (lifted_f + conv_two).astype(jnp.bfloat16)
    grad_out = cotangent.astype(jnp.float32).reshape(-1, model_width)
    d_act_two = conv_backward(cotangent, conv_second)
    d_conv_one = norm_back(d_act_two * silu_slope(second_in), conv_one, inv_three, gain_second).astype(jnp.bfloat16)
    d_act_one = conv_backward(d_conv_one.reshape(VIEWS, ROWS, COLS, model_width), conv_first)
    d_lifted = grad_out + norm_back(d_act_one * silu_slope(first_in), lifted_f, inv_two, gain_first)
    d_mixed = jnp.dot(d_lifted.astype(jnp.bfloat16), w_out.T, preferred_element_type=jnp.float32).astype(jnp.bfloat16)
    d_mixed_blocks = to_blocks(d_mixed)

    def backward_column(column):
        queries, key_part, value_part, live_mask = key_set(column)
        weights = attention_weights(queries, key_part, live_mask)
        rounded = weights.astype(jnp.bfloat16).astype(jnp.float32)
        gradient = d_mixed_blocks[:, column].reshape(VIEWS, BLK, HEADS, HEAD_DIM).astype(jnp.float32)
        slope = jnp.einsum('vqhd,vkhd->vhqk', gradient, value_part.astype(jnp.float32))
        d_score = weights * (slope - lax.optimization_barrier(jnp.sum(weights * slope, axis=-1, keepdims=True)))
        d_scaled = (d_score * HEAD_DIM ** (-0.5)).astype(jnp.bfloat16).astype(jnp.float32)
        d_query = jnp.einsum('vhqk,vkhd->vqhd', d_scaled, key_part.astype(jnp.float32))
        d_keys = jnp.einsum('vhqk,vqhd->vkhd', d_scaled, queries.astype(jnp.float32))
        d_vals = jnp.einsum('vhqk,vqhd->vkhd', rounded, gradient)
        both = jnp.concatenate([d_keys.reshape(VIEWS, -1, model_width), d_vals.reshape(VIEWS, -1, model_width)], axis=-1)
        both = both.reshape(VIEWS, 1 + KSEL, BLK, 2 * model_width)
        far = both[:, 1:].astype(jnp.bfloat16)
        listed = view_lists[:, column]
        target_pre = key_pre_blocks[partner[:, None], listed].reshape(-1, HEADS, HEAD_DIM)
        target_inv = key_inv_blocks[partner[:, None], listed].reshape(-1, HEADS, 1)
        far_keys = far[..., :model_width].astype(jnp.float32).reshape(-1, HEADS, HEAD_DIM)
        listed_keys = norm_back(far_keys, target_pre, target_inv, 1.0).reshape(-1, model_width).astype(jnp.bfloat16)
        share = jnp.dot(listed_keys, w_key.T, preferred_element_type=jnp.float32)
        share = share + jnp.dot(far[..., model_width:].reshape(-1, model_width), w_value.T, preferred_element_type=jnp.float32)
        share = share.astype(jnp.bfloat16).reshape(VIEWS, KSEL, BLK, model_width)
        return (d_query, both[:, 0], share)
    d_query_all, own_all, share_all = lax.map(backward_column, columns)
    own_pairs = from_blocks(jnp.transpose(own_all, (1, 0, 2, 3)))
    summed_shares = jnp.zeros((VIEWS, TILES, BLK, model_width), jnp.float32)
    target_view = jnp.broadcast_to(partner[None, :, None], (TILES, VIEWS, KSEL))
    target_column = jnp.transpose(view_lists, (1, 0, 2))
    summed_shares = summed_shares.at[target_view, target_column].add(share_all.astype(jnp.float32))
    d_query_flat = from_blocks(jnp.transpose(d_query_all, (1, 0, 2, 3, 4)).reshape(VIEWS, TILES, BLK, model_width))
    d_query_pre = norm_back(d_query_flat.reshape(-1, HEADS, HEAD_DIM), query_pre, query_inv, 1.0)
    d_key_pre = norm_back(own_pairs[:, :model_width].reshape(-1, HEADS, HEAD_DIM), key_pre, key_inv, 1.0)
    d_rows = jnp.dot(d_query_pre.reshape(-1, model_width).astype(jnp.bfloat16), w_query.T, preferred_element_type=jnp.float32)
    d_rows = d_rows + jnp.dot(d_key_pre.reshape(-1, model_width).astype(jnp.bfloat16), w_key.T, preferred_element_type=jnp.float32)
    d_rows = d_rows + jnp.dot(own_pairs[:, model_width:].astype(jnp.bfloat16), w_value.T, preferred_element_type=jnp.float32)
    d_rows = d_rows + from_blocks(summed_shares)
    d_clip = (d_lifted + norm_back(d_rows, inputs, inv_in, gain_attn)).astype(jnp.bfloat16)
    shape_out = (VIEWS, ROWS, COLS, model_width)
    return (result.reshape(shape_out), d_clip.reshape(shape_out))
```

```python
import functools

import jax
import jax.numpy as jnp
from jax import lax
from jax.experimental import pallas as pl
from jax.experimental.pallas import tpu as pltpu
from jax.sharding import PartitionSpec as P

HEADS = 8
EPSILON = 1e-06
F32 = jnp.float32
BF16 = jnp.bfloat16
VMEM_LIMIT = 56 * 1024 * 1024


def mm(a, b):
    return lax.dot_general(a, b, (((1,), (0,)), ((), ())), preferred_element_type=F32)


def mm_t(a, b):
    return lax.dot_general(a, b, (((1,), (1,)), ((), ())), preferred_element_type=F32)


def params(sems=None):
    return pltpu.CompilerParams(
        dimension_semantics=sems, vmem_limit_bytes=VMEM_LIMIT
    )


def whole(shape):
    zeros = (0,) * len(shape)
    return pl.BlockSpec(shape, lambda *_: zeros)


def rms(values):
    return lax.rsqrt(jnp.mean(values * values, axis=-1, keepdims=True) + EPSILON)


def silu_parts(u):
    sigmoid = jax.nn.sigmoid(u)
    return u * sigmoid, sigmoid * (1.0 + u * (1.0 - sigmoid))


def head_ones(width, head):
    rows = lax.broadcasted_iota(jnp.int32, (width, width), 0) // head
    cols = lax.broadcasted_iota(jnp.int32, (width, width), 1) // head
    return jnp.where(rows == cols, 1.0, 0.0).astype(BF16)


def head_mean(values, ones, head):
    width = ones.shape[0]
    parts = [
        mm(values[:, i : i + width].astype(BF16), ones)
        for i in range(0, values.shape[1], width)
    ]
    return jnp.concatenate(parts, axis=1) * (1.0 / head)


def prep_kernel(n_cols, own_s, match_s, lists_s, counts_s, clip_ref, gain_ref, rows_ref, send_ref, sem):
    cams = match_s.shape[0]
    picks = lists_s.shape[2]
    own = own_s[0]
    tw, _, nr, width = clip_ref.shape
    for c in range(cams):
        x = clip_ref[:, c].reshape(tw * nr, width).astype(F32)
        rows_ref[c] = (x * rms(x) * gain_ref[...]).astype(BF16)

    def copy(i):
        cam = jnp.int32(0)
        for c in range(cams):
            for s in range(picks):
                hit = (lists_s[c, i, s] == own) & (s < counts_s[c, i])
                cam = jnp.where(hit, match_s[c], cam)
        pltpu.make_async_copy(rows_ref.at[cam], send_ref.at[i], sem.at[i]).start()

    def start(i, carry):
        copy(i)
        return carry

    lax.fori_loop(0, n_cols, start, 0)

    def wait(i, carry):
        pltpu.make_async_copy(rows_ref.at[0], send_ref.at[i], sem.at[i]).wait()
        return carry

    lax.fori_loop(0, n_cols, wait, 0)


def prep(n_cols, own, matching, lists, counts, clip_t, gain):
    tw, cams, nr, width = clip_t.shape
    blk = tw * nr
    return pl.pallas_call(
        functools.partial(prep_kernel, n_cols),
        name="prep",
        out_shape=(
            jax.ShapeDtypeStruct((cams, blk, width), BF16),
            jax.ShapeDtypeStruct((n_cols, blk, width), BF16),
        ),
        grid_spec=pltpu.PrefetchScalarGridSpec(
            num_scalar_prefetch=4,
            grid=(1,),
            in_specs=[whole(clip_t.shape), whole((1, width))],
            out_specs=[whole((cams, blk, width)), pl.BlockSpec(memory_space=pl.ANY)],
            scratch_shapes=[pltpu.SemaphoreType.DMA((n_cols,))],
        ),
        compiler_params=params(),
    )(own, matching, lists, counts, clip_t, gain)


def project_kernel(head, rows_ref, wq_ref, wk_ref, wv_ref, q_ref, k_ref, v_ref, rq_ref, rk_ref):
    rows = rows_ref[...]
    width = rows.shape[1]
    half = width // 2
    ones = head_ones(half, head)
    for n in range(2):
        cols = slice(n * half, (n + 1) * half)
        for w_ref, o_ref, r_ref in ((wq_ref, q_ref, rq_ref), (wk_ref, k_ref, rk_ref)):
            pre = mm(rows, w_ref[:, cols])
            r = lax.rsqrt(head_mean(pre * pre, ones, head) + EPSILON)
            o_ref[:, cols] = (pre * r).astype(BF16)
            r_ref[:, cols] = r
        v_ref[:, cols] = mm(rows, wv_ref[:, cols]).astype(BF16)


def project(rows, wq, wk, wv, head):
    total, width = rows.shape
    full = (total, width)
    return pl.pallas_call(
        functools.partial(project_kernel, head),
        name="project",
        out_shape=(
            jax.ShapeDtypeStruct(full, BF16),
            jax.ShapeDtypeStruct(full, BF16),
            jax.ShapeDtypeStruct(full, BF16),
            jax.ShapeDtypeStruct(full, F32),
            jax.ShapeDtypeStruct(full, F32),
        ),
        compiler_params=params(),
        cost_estimate=pl.CostEstimate(
            flops=6 * total * width * width, bytes_accessed=20 * total * width, transcendentals=0
        ),
    )(rows, wq, wk, wv)


def pair_rows(x, low):
    zero = jnp.zeros_like(x)
    return jnp.concatenate([jnp.where(low, x, zero), jnp.where(low, zero, x)], axis=0)


def attend_kernel(head, picks, own_s, lists_s, counts_s, *refs):
    far = refs[:picks]
    (q_ref, k_ref, v_ref, clip_ref, wk_ref, wv_ref, wo_ref, gain_ref,
     lifted_ref, act_ref, near_ref, farther_ref, kf_ref, vf_ref, rf_ref, kcat, vcat) = refs[picks:]
    c = pl.program_id(0)
    own = own_s[0]
    count = counts_s[c, own]
    blk, width = q_ref.shape[1:]
    half = width // 2
    keys = (1 + picks) * blk
    ones_h = head_ones(half, head)
    rows = jnp.concatenate([f[0] for f in far], axis=0)
    kcat[:blk] = k_ref[0]
    vcat[:blk] = v_ref[0]
    for n in range(2):
        cols = slice(n * half, (n + 1) * half)
        pre = mm(rows, wk_ref[:, cols])
        r = lax.rsqrt(head_mean(pre * pre, ones_h, head) + EPSILON)
        k = (pre * r).astype(BF16)
        v = mm(rows, wv_ref[:, cols]).astype(BF16)
        kcat[blk:, cols] = k
        vcat[blk:, cols] = v
        kf_ref[0, :, cols] = k
        vf_ref[0, :, cols] = v
        rf_ref[0, :, cols] = r
    key_block = lax.broadcasted_iota(jnp.int32, (keys, 1), 0) // blk
    live = jnp.where(key_block <= count, 1.0, 0.0)
    live_ones = jnp.broadcast_to(live, (keys, 128)).astype(BF16)
    low = lax.broadcasted_iota(jnp.int32, (blk, 128), 1) < head
    scale = head ** (-0.5)
    mixed = []
    for h in range(0, width, 128):
        q2 = pair_rows(q_ref[0, :, h : h + 128] * jnp.asarray(scale, BF16), low)
        grown = jnp.exp(mm_t(q2, kcat[:, h : h + 128])).astype(BF16)
        ext = jnp.concatenate([vcat[:, h : h + 128] * live_ones, live_ones], axis=1)
        out = mm(grown, ext)
        out = out[:, :128] / out[:, 128:]
        mixed.append(jnp.where(low, out[:blk], out[blk:]).astype(BF16))
    mixed = jnp.concatenate(mixed, axis=1)
    clip = clip_ref[:, 0].reshape(blk, width).astype(F32)
    lifted = (clip + mm(mixed, wo_ref[...])).astype(BF16)
    lifted_f = lifted.astype(F32)
    act, _ = silu_parts(lifted_f * rms(lifted_f) * gain_ref[...])
    slabs = (clip_ref.shape[0], clip_ref.shape[2], width)
    lifted_ref[:, 0] = lifted.reshape(slabs)
    act = act.astype(BF16).reshape(slabs)
    act_ref[:, 0] = act
    even = lax.rem(own, 2) == 0
    near_ref[0] = jnp.where(even, act[-1], act[0])
    farther_ref[0] = jnp.where(even, act[0], act[-1])


def attend(own, lists, counts, arrived, q, k, v, clip_t, wk, wv, wo, gain, head):
    tw, cams, nr, width = clip_t.shape
    blk = tw * nr
    picks = lists.shape[2]
    slab = pl.BlockSpec((tw, 1, nr, width), lambda c, *_: (0, c, 0, 0))
    block = pl.BlockSpec((1, blk, width), lambda c, *_: (c, 0, 0))
    far_block = pl.BlockSpec((1, picks * blk, width), lambda c, *_: (c, 0, 0))
    edge = pl.BlockSpec((1, nr, width), lambda c, *_: (c, 0, 0))

    def listed(s):
        return pl.BlockSpec(
            (1, blk, width), lambda c, own, lists, counts: (lists[c, own[0], s], 0, 0)
        )

    return pl.pallas_call(
        functools.partial(attend_kernel, head, picks),
        name="attend",
        out_shape=(
            jax.ShapeDtypeStruct(clip_t.shape, BF16),
            jax.ShapeDtypeStruct(clip_t.shape, BF16),
            jax.ShapeDtypeStruct((cams, nr, width), BF16),
            jax.ShapeDtypeStruct((cams, nr, width), BF16),
            jax.ShapeDtypeStruct((cams, picks * blk, width), BF16),
            jax.ShapeDtypeStruct((cams, picks * blk, width), BF16),
            jax.ShapeDtypeStruct((cams, picks * blk, width), F32),
        ),
        grid_spec=pltpu.PrefetchScalarGridSpec(
            num_scalar_prefetch=3,
            grid=(cams,),
            in_specs=[listed(s) for s in range(picks)]
            + [block, block, block, slab]
            + [whole((width, width))] * 3
            + [whole((1, width))],
            out_specs=[slab, slab, edge, edge, far_block, far_block, far_block],
            scratch_shapes=[
                pltpu.VMEM(((1 + picks) * blk, width), BF16),
                pltpu.VMEM(((1 + picks) * blk, width), BF16),
            ],
        ),
        compiler_params=params(("arbitrary",)),
    )(own, lists, counts, *([arrived] * picks), q, k, v, clip_t, wk, wv, wo, gain)


def fill_windows(own_s, act_ref, near_ref, farther_ref, x_ref, edge, total):
    width = act_ref.shape[1]
    even = lax.rem(own_s[0], 2) == 0
    near = near_ref[...]
    farther = farther_ref[...]
    x_ref[:edge, :width] = jnp.where(even, farther, near)
    x_ref[edge:, :width] = act_ref[: total - edge]
    x_ref[:, width : 2 * width] = act_ref[...]
    x_ref[: total - edge, 2 * width :] = act_ref[edge:]
    x_ref[total - edge :, 2 * width :] = jnp.where(even, near, farther)


def conv_step(w_ref, x_ref, y_ref, step, transposed):
    width = w_ref.shape[2]
    if transposed:
        total = None
        for q in range(3):
            cols = slice((2 - q) * width, (3 - q) * width)
            part = mm_t(x_ref[:, cols], w_ref[0, q])
            total = part if total is None else total + part
        y_ref[step] = total
    else:
        y_ref[step] = mm(x_ref[...], w_ref[0].reshape(3 * width, width))


def conv_rows(y_ref, start, size, nr, transposed):
    rows = pl.ds(start, size)
    before, centre, after = (2, 1, 0) if transposed else (0, 1, 2)
    place = lax.broadcasted_iota(jnp.int32, (size, 1), 0) % nr
    up = pltpu.roll(y_ref[before, rows, :], 1, 0)
    down = pltpu.roll(y_ref[after, rows, :], size - 1, 0)
    return (
        jnp.where(place == 0, 0.0, up)
        + y_ref[centre, rows, :]
        + jnp.where(place == nr - 1, 0.0, down)
    )


def conv_kernel(body, n_extra, transposed, nr, own_s, act_ref, near_ref, farther_ref, w_ref, *refs):
    extra, outs, (x_ref, y_ref) = refs[:n_extra], refs[n_extra:-2], refs[-2:]
    step = pl.program_id(0)
    total = act_ref.shape[0]
    edge = near_ref.shape[0]

    @pl.when(step == 0)
    def _():
        fill_windows(own_s, act_ref, near_ref, farther_ref, x_ref, edge, total)

    conv_step(w_ref, x_ref, y_ref, step, transposed)

    @pl.when(step == 2)
    def _():
        even = lax.rem(own_s[0], 2) == 0
        body(lambda start, size: conv_rows(y_ref, start, size, nr, transposed), even, edge, extra, outs)


def conv_call(name, body, own, act, near, farther, weights, extra, outs, nr, transposed):
    total, width = act.shape
    edge = near.shape[0]
    return pl.pallas_call(
        functools.partial(conv_kernel, body, len(extra), transposed, nr),
        name=name,
        out_shape=outs,
        grid_spec=pltpu.PrefetchScalarGridSpec(
            num_scalar_prefetch=1,
            grid=(3,),
            in_specs=[
                whole((total, width)),
                whole((edge, width)),
                whole((edge, width)),
                pl.BlockSpec((1, 3, width, width), lambda p, *_: (p, 0, 0, 0)),
            ]
            + [whole(e.shape) for e in extra],
            out_specs=[whole(o.shape) for o in outs],
            scratch_shapes=[
                pltpu.VMEM((total, 3 * width), BF16),
                pltpu.VMEM((3, total, width), F32),
            ],
        ),
        compiler_params=params(("arbitrary",)),
        cost_estimate=pl.CostEstimate(
            flops=18 * total * width * width, bytes_accessed=18 * width * width, transcendentals=0
        ),
    )(own, act, near, farther, weights, *extra)


CHUNK = 32


def chunks(total, fn):
    def step(i, carry):
        fn(pl.multiple_of(i * CHUNK, CHUNK))
        return carry

    lax.fori_loop(0, total // CHUNK, step, 0)


def grad_two_body(rows_of, even, edge, extra, outs):
    (out,) = outs

    def one(start):
        out[pl.ds(start, CHUNK), :] = rows_of(start, CHUNK)

    chunks(out.shape[0], one)


def copy_edges(even, edge, full, near, farther):
    total = full.shape[0]
    first = full[:edge]
    last = full[total - edge :]
    near[...] = jnp.where(even, last, first)
    farther[...] = jnp.where(even, first, last)


def conv_one_body(rows_of, even, edge, extra, outs):
    grad_ref, gain_ref = extra
    act_ref, act_near, act_far, d_ref, d_near, d_far = outs
    total = act_ref.shape[0]
    gain = gain_ref[...]

    def one(start):
        rows = pl.ds(start, CHUNK)
        conv = rows_of(start, CHUNK)
        r = rms(conv)
        hat = conv * r
        act, slope = silu_parts(hat * gain)
        act_ref[rows, :] = act.astype(BF16)
        g = grad_ref[rows, :] * slope * gain
        d_ref[rows, :] = (r * (g - hat * jnp.mean(g * hat, axis=-1, keepdims=True))).astype(BF16)

    chunks(total, one)
    copy_edges(even, edge, act_ref, act_near, act_far)
    copy_edges(even, edge, d_ref, d_near, d_far)


def conv_two_body(rows_of, even, edge, extra, outs):
    (lifted_ref,) = extra
    (out,) = outs

    def one(start):
        rows = pl.ds(start, CHUNK)
        out[rows, :] = (lifted_ref[rows, :].astype(F32) + rows_of(start, CHUNK)).astype(BF16)

    chunks(out.shape[0], one)


def grad_one_body(rows_of, even, edge, extra, outs):
    lifted_ref, cot_ref, gain_ref, wo_ref = extra
    d_lifted_ref, d_mixed_ref = outs
    gain = gain_ref[...]
    total = d_lifted_ref.shape[0]

    def one(start):
        rows = pl.ds(start, CHUNK)
        lifted = lifted_ref[rows, :].astype(F32)
        r = rms(lifted)
        hat = lifted * r
        _, slope = silu_parts(hat * gain)
        g = rows_of(start, CHUNK) * slope * gain
        back = r * (g - hat * jnp.mean(g * hat, axis=-1, keepdims=True))
        d_lifted_ref[rows, :] = cot_ref[rows, :].astype(F32) + back

    chunks(total, one)
    d_mixed_ref[...] = mm_t(d_lifted_ref[...].astype(BF16), wo_ref[...]).astype(BF16)


def head_norm_back(grad, hat, r, ones, head):
    hat = hat.astype(F32)
    return r * (grad - hat * head_mean(grad * hat, ones, head))


def attend_back_kernel(head, picks, own_s, lists_s, counts_s, *refs):
    (q_ref, k_ref, v_ref, kf_ref, vf_ref, rq_ref, rk_ref, rf_ref, dm_ref, wk_ref, wv_ref,
     dq_ref, dk_ref, dv_ref, send_ref, kcat, vcat, kgrad, vgrad) = refs
    c = pl.program_id(0)
    own = own_s[0]
    count = counts_s[c, own]
    blk, width = q_ref.shape[1:]
    half = width // 2
    keys = (1 + picks) * blk
    tw, nr = dm_ref.shape[0], dm_ref.shape[2]
    scale = head ** (-0.5)

    @pl.when(c == 0)
    def _():
        send_ref[...] = jnp.zeros_like(send_ref)

    kcat[:blk] = k_ref[0]
    kcat[blk:] = kf_ref[0]
    vcat[:blk] = v_ref[0]
    vcat[blk:] = vf_ref[0]
    key_block = lax.broadcasted_iota(jnp.int32, (keys, 1), 0) // blk
    live = jnp.where(key_block <= count, 1.0, 0.0)
    low = lax.broadcasted_iota(jnp.int32, (blk, 128), 1) < head
    ones_h = head_ones(half, head)
    dq = []
    for h in range(0, width, 128):
        cols = slice(h, h + 128)
        kp = kcat[:, cols]
        q2 = pair_rows(q_ref[0, :, cols] * jnp.asarray(scale, BF16), low)
        dm2 = pair_rows(dm_ref[:, 0, :, cols].reshape(blk, 128), low)
        grown = jnp.exp(mm_t(kp, q2)) * live
        inverse = 1.0 / jnp.sum(grown, axis=0, keepdims=True)
        weights = grown * inverse
        slope = mm_t(vcat[:, cols], dm2)
        drift = jnp.sum(weights * slope, axis=0, keepdims=True)
        d_scaled = (weights * (slope - drift)).astype(BF16)
        kgrad[:, cols] = mm(d_scaled, q2)
        vgrad[:, cols] = mm(weights.astype(BF16), dm2)
        dq_t = mm(jnp.transpose(kp), d_scaled) * scale
        dq_t = jnp.concatenate([dq_t[:head, :blk], dq_t[head:, blk:]], axis=0)
        dq.append(jnp.transpose(dq_t))
    dq = jnp.concatenate(dq, axis=1)
    dq_ref[0] = head_norm_back(dq, q_ref[0], rq_ref[0], ones_h, head).astype(BF16)
    dk_ref[0] = head_norm_back(kgrad[:blk], kcat[:blk], rk_ref[0], ones_h, head).astype(BF16)
    dv_ref[0] = vgrad[:blk].astype(BF16)
    far_k = head_norm_back(kgrad[blk:], kcat[blk:], rf_ref[0], ones_h, head).astype(BF16)
    share = mm_t(far_k, wk_ref[...]) + mm_t(vgrad[blk:].astype(BF16), wv_ref[...])
    share = share.astype(BF16)
    for s in range(picks):
        send_ref[lists_s[c, own, s]] = share[s * blk : (s + 1) * blk]


def attend_back(own, lists, counts, n_cols, q, k, v, kf, vf, rq, rk, rf, dm_t, wk, wv, head):
    tw, cams, nr, width = dm_t.shape
    blk = tw * nr
    picks = lists.shape[2]
    slab = pl.BlockSpec((tw, 1, nr, width), lambda c, *_: (0, c, 0, 0))
    block = pl.BlockSpec((1, blk, width), lambda c, *_: (c, 0, 0))
    far_block = pl.BlockSpec((1, picks * blk, width), lambda c, *_: (c, 0, 0))
    keys = (1 + picks) * blk
    return pl.pallas_call(
        functools.partial(attend_back_kernel, head, picks),
        name="attend_back",
        out_shape=(
            jax.ShapeDtypeStruct((cams, blk, width), BF16),
            jax.ShapeDtypeStruct((cams, blk, width), BF16),
            jax.ShapeDtypeStruct((cams, blk, width), BF16),
            jax.ShapeDtypeStruct((n_cols, blk, width), BF16),
        ),
        grid_spec=pltpu.PrefetchScalarGridSpec(
            num_scalar_prefetch=3,
            grid=(cams,),
            in_specs=[block, block, block, far_block, far_block, block, block, far_block, slab]
            + [whole((width, width))] * 2,
            out_specs=[block, block, block, whole((n_cols, blk, width))],
            scratch_shapes=[
                pltpu.VMEM((keys, width), BF16),
                pltpu.VMEM((keys, width), BF16),
                pltpu.VMEM((keys, width), F32),
                pltpu.VMEM((keys, width), F32),
            ],
        ),
        compiler_params=params(("arbitrary",)),
    )(own, lists, counts, q, k, v, kf, vf, rq, rk, rf, dm_t, wk, wv)


def row_grad_kernel(dq_ref, dk_ref, dv_ref, wq_ref, wk_ref, wv_ref, out_ref):
    out_ref[...] = mm_t(dq_ref[...], wq_ref[...])
    out_ref[...] += mm_t(dk_ref[...], wk_ref[...])
    out_ref[...] += mm_t(dv_ref[...], wv_ref[...])


def row_grad(dq, dk, dv, wq, wk, wv):
    total, width = dq.shape
    return pl.pallas_call(
        row_grad_kernel,
        name="row_grad",
        out_shape=jax.ShapeDtypeStruct((total, width), F32),
        compiler_params=params(),
        cost_estimate=pl.CostEstimate(
            flops=6 * total * width * width, bytes_accessed=10 * total * width, transcendentals=0
        ),
    )(dq, dk, dv, wq, wk, wv)


def final_kernel(n_cols, own_s, match_s, lists_s, counts_s, back_ref, rows_ref, clip_ref, dl_ref, gain_ref, out_ref, acc):
    cams = match_s.shape[0]
    picks = lists_s.shape[2]
    own = own_s[0]
    tw, _, nr, width = clip_ref.shape
    blk = tw * nr
    acc[...] = rows_ref[...]

    def add(i, carry):
        cam = jnp.int32(-1)
        for c in range(cams):
            for s in range(picks):
                hit = (lists_s[c, i, s] == own) & (s < counts_s[c, i])
                cam = jnp.where(hit, match_s[c], cam)

        @pl.when(cam >= 0)
        def _():
            acc[cam] += back_ref[i].astype(F32)

        return carry

    lax.fori_loop(0, n_cols, add, 0)
    gain = gain_ref[...]

    def one(c, carry):
        x = clip_ref[:, c].reshape(blk, width).astype(F32)
        r = rms(x)
        hat = x * r
        g = acc[c] * gain
        d = dl_ref[:, c].reshape(blk, width) + r * (
            g - hat * jnp.mean(g * hat, axis=-1, keepdims=True)
        )
        out_ref[:, c] = d.astype(BF16).reshape(tw, nr, width)
        return carry

    lax.fori_loop(0, cams, one, 0)


def final(own, matching, lists, counts, back, rows, clip_t, d_lifted, gain):
    n_cols = back.shape[0]
    return pl.pallas_call(
        functools.partial(final_kernel, n_cols),
        name="final",
        out_shape=jax.ShapeDtypeStruct(clip_t.shape, BF16),
        grid_spec=pltpu.PrefetchScalarGridSpec(
            num_scalar_prefetch=4,
            grid=(1,),
            in_specs=[whole(a.shape) for a in (back, rows, clip_t, d_lifted, gain)],
            out_specs=whole(clip_t.shape),
            scratch_shapes=[pltpu.VMEM(rows.shape, F32)],
        ),
        compiler_params=params(),
    )(own, matching, lists, counts, back, rows, clip_t, d_lifted, gain)


def exchange_edges(near, farther):
    size = lax.axis_size("cols")
    inner = [(i, i ^ 1) for i in range(size)]
    outer = [(i, i + 1 if i % 2 else i - 1) for i in range(1, size - 1)]
    return lax.ppermute(near, "cols", inner), lax.ppermute(farther, "cols", outer)


def local(
    clip_tokens,
    cotangent,
    gain_attn,
    w_query,
    w_key,
    w_value,
    w_out,
    gain_first,
    conv_first,
    gain_second,
    conv_second,
    matching,
    block_lists,
    counts,
):
    views, nr, tw, width = clip_tokens.shape
    head = width // HEADS
    n_cols = lax.axis_size("cols")
    own_index = lax.axis_index("cols").astype(jnp.int32)
    own = own_index.reshape(1)
    total = views * nr * tw
    blk = nr * tw
    flat = (total, width)
    slabs = (tw, views, nr, width)
    gain_attn = gain_attn.reshape(1, width)
    gain_first = gain_first.reshape(1, width)
    gain_second = gain_second.reshape(1, width)

    clip_t = jnp.transpose(clip_tokens, (2, 0, 1, 3))
    cot_t = jnp.transpose(cotangent, (2, 0, 1, 3))
    odd = own_index % 2
    last = (tw - 1) * (1 - odd)
    cot_near = lax.dynamic_index_in_dim(cot_t, last, 0, keepdims=False).reshape(-1, width)
    cot_far = lax.dynamic_index_in_dim(cot_t, tw - 1 - last, 0, keepdims=False).reshape(-1, width)
    cot_near, cot_far = exchange_edges(cot_near, cot_far)

    rows, send = prep(n_cols, own, matching, block_lists, counts, clip_t, gain_attn)
    arrived = lax.all_to_all(send, "cols", split_axis=0, concat_axis=0, tiled=True)

    (d_act_two,) = conv_call(
        "grad_two", grad_two_body, own, cot_t.reshape(flat), cot_near, cot_far, conv_second,
        (), (jax.ShapeDtypeStruct(flat, F32),), nr, True,
    )
    q, k, v, rq, rk = (
        a.reshape(views, blk, width)
        for a in project(rows.reshape(flat), w_query, w_key, w_value, head)
    )
    lifted, act_one, near, farther, kf, vf, rf = attend(
        own, block_lists, counts, arrived, q, k, v, clip_t, w_key, w_value, w_out, gain_first, head
    )
    edge = (views * nr, width)
    near, farther = exchange_edges(near.reshape(edge), farther.reshape(edge))
    flat_bf = jax.ShapeDtypeStruct(flat, BF16)
    edge_bf = jax.ShapeDtypeStruct(edge, BF16)
    act_two, act_near, act_far, d_conv, d_near, d_far = conv_call(
        "conv_one", conv_one_body, own, act_one.reshape(flat), near, farther, conv_first,
        (d_act_two, gain_second),
        (flat_bf, edge_bf, edge_bf, flat_bf, edge_bf, edge_bf), nr, False,
    )
    d_near, d_far = exchange_edges(d_near, d_far)
    d_lifted, d_mixed = conv_call(
        "grad_one", grad_one_body, own, d_conv, d_near, d_far, conv_first,
        (lifted.reshape(flat), cot_t.reshape(flat), gain_first, w_out),
        (jax.ShapeDtypeStruct(flat, F32), flat_bf), nr, True,
    )
    dq, dk, dv, send_back = attend_back(
        own, block_lists, counts, n_cols, q, k, v, kf, vf, rq, rk, rf,
        d_mixed.reshape(slabs), w_key, w_value, head,
    )
    back = lax.all_to_all(send_back, "cols", split_axis=0, concat_axis=0, tiled=True)
    act_near, act_far = exchange_edges(act_near, act_far)
    (result,) = conv_call(
        "conv_two", conv_two_body, own, act_two, act_near, act_far, conv_second,
        (lifted.reshape(flat),), (flat_bf,), nr, False,
    )
    d_rows = row_grad(
        dq.reshape(flat), dk.reshape(flat), dv.reshape(flat), w_query, w_key, w_value
    ).reshape(views, blk, width)
    d_clip = final(own, matching, block_lists, counts, back, d_rows, clip_t, d_lifted.reshape(slabs), gain_attn)
    return (
        jnp.transpose(result.reshape(slabs), (1, 2, 0, 3)),
        jnp.transpose(d_clip, (1, 2, 0, 3)),
    )


def solution(mesh):
    tiles = P("groups", None, "cols", None)
    in_specs = (tiles, tiles) + (P(),) * 12
    return jax.shard_map(
        local, mesh=mesh, in_specs=in_specs, out_specs=(tiles, tiles), check_vma=False
    )
```

```python
import functools

import jax
import jax.numpy as jnp
from jax import lax
from jax.experimental import pallas as pl
from jax.experimental.pallas import tpu as pltpu
from jax.sharding import PartitionSpec as P

HEADS = 8
EPSILON = 1e-06
F32 = jnp.float32
BF16 = jnp.bfloat16


def mm(a, b):
    return lax.dot_general(a, b, (((1,), (0,)), ((), ())), preferred_element_type=F32)


def mm_t(a, b):
    return lax.dot_general(a, b, (((1,), (1,)), ((), ())), preferred_element_type=F32)


def params(mib):
    return pltpu.CompilerParams(vmem_limit_bytes=mib * 1024 * 1024)


def hbm(x):
    return pltpu.with_memory_space_constraint(x, pltpu.HBM)


def vmem(x):
    return pltpu.with_memory_space_constraint(x, pltpu.VMEM)


def whole(shape):
    zeros = (0,) * len(shape)
    return pl.BlockSpec(shape, lambda *_: zeros)


def rms(values):
    return lax.rsqrt(jnp.mean(values * values, axis=-1, keepdims=True) + EPSILON)


def silu_parts(u):
    sigmoid = 0.5 + 0.5 * jnp.tanh(0.5 * u)
    return u * sigmoid, sigmoid * (1.0 + u * (1.0 - sigmoid))


def head_ones(width, head):
    rows = lax.broadcasted_iota(jnp.int32, (width, width), 0) // head
    cols = lax.broadcasted_iota(jnp.int32, (width, width), 1) // head
    return jnp.where(rows == cols, 1.0, 0.0).astype(BF16)


def head_mean(values, ones, head):
    width = ones.shape[0]
    parts = [
        mm(values[:, i : i + width].astype(BF16), ones)
        for i in range(0, values.shape[1], width)
    ]
    return jnp.concatenate(parts, axis=1) * (1.0 / head)


def prep_kernel(n_cols, own_s, match_s, lists_s, counts_s, clip_ref, gain_ref, rows_ref, send_ref, sem):
    cams = match_s.shape[0]
    picks = lists_s.shape[2]
    own = own_s[0]
    tw, _, nr, width = clip_ref.shape
    for c in range(cams):
        x = clip_ref[:, c].reshape(tw * nr, width).astype(F32)
        rows_ref[c] = (x * rms(x) * gain_ref[...]).astype(BF16)

    def copy(i):
        cam = jnp.int32(0)
        for c in range(cams):
            for s in range(picks):
                hit = (lists_s[c, i, s] == own) & (s < counts_s[c, i])
                cam = jnp.where(hit, match_s[c], cam)
        pltpu.make_async_copy(rows_ref.at[cam], send_ref.at[i], sem.at[i]).start()

    def start(i, carry):
        copy(i)
        return carry

    lax.fori_loop(0, n_cols, start, 0)

    def wait(i, carry):
        pltpu.make_async_copy(rows_ref.at[0], send_ref.at[i], sem.at[i]).wait()
        return carry

    lax.fori_loop(0, n_cols, wait, 0)


def prep(n_cols, own, matching, lists, counts, clip_t, gain):
    tw, cams, nr, width = clip_t.shape
    blk = tw * nr
    return pl.pallas_call(
        functools.partial(prep_kernel, n_cols),
        name="prep",
        out_shape=(
            jax.ShapeDtypeStruct((cams, blk, width), BF16),
            pltpu.HBM((n_cols, blk, width), BF16),
        ),
        grid_spec=pltpu.PrefetchScalarGridSpec(
            num_scalar_prefetch=4,
            grid=(1,),
            in_specs=[whole(clip_t.shape), whole((1, width))],
            out_specs=[whole((cams, blk, width)), pl.BlockSpec(memory_space=pltpu.HBM)],
            scratch_shapes=[pltpu.SemaphoreType.DMA((n_cols,))],
        ),
        compiler_params=params(8),
    )(own, matching, lists, counts, clip_t, gain)


def project_kernel(head, blk, rows_ref, wq_ref, wk_ref, wv_ref, wvt_ref, q_ref, k_ref, v_ref, vt_ref, rq_ref, rk_ref):
    rows = rows_ref[...]
    total, width = rows.shape
    half = width // 2
    ones = head_ones(half, head)
    for n in range(2):
        cols = slice(n * half, (n + 1) * half)
        for w_ref, o_ref, r_ref, scale in (
            (wq_ref, q_ref, rq_ref, head ** (-0.5)),
            (wk_ref, k_ref, rk_ref, 1.0),
        ):
            pre = mm(rows, w_ref[:, cols])
            r = lax.rsqrt(head_mean(pre * pre, ones, head) + EPSILON)
            o_ref[:, cols] = (pre * r * scale).astype(BF16)
            r_ref[:, cols] = r
        v_ref[:, cols] = mm(rows, wv_ref[:, cols]).astype(BF16)
    for c in range(total // blk):
        vt_ref[c] = mm_t(wvt_ref[...], rows_ref[c * blk : (c + 1) * blk]).astype(BF16)


def project(rows, wq, wk, wv, wvt, head, blk):
    total, width = rows.shape
    full = (total, width)
    return pl.pallas_call(
        functools.partial(project_kernel, head, blk),
        name="project",
        out_shape=(
            pltpu.VMEM(full, BF16),
            pltpu.VMEM(full, BF16),
            pltpu.VMEM(full, BF16),
            pltpu.VMEM((total // blk, width, blk), BF16),
            pltpu.VMEM(full, F32),
            pltpu.VMEM(full, F32),
        ),
        compiler_params=params(8),
        cost_estimate=pl.CostEstimate(
            flops=8 * total * width * width, bytes_accessed=20 * total * width, transcendentals=0
        ),
    )(rows, wq, wk, wv, wvt)


def pair_rows(x, low):
    zero = jnp.zeros_like(x)
    return jnp.concatenate([jnp.where(low, x, zero), jnp.where(low, zero, x)], axis=0)


PAD = 16


def attend_kernel(head, picks, own_s, lists_s, counts_s, *refs):
    (arrived_ref, q_ref, k_ref, vt_ref, clip_ref, wk_ref, wvt_ref, wo_ref, gain_ref,
     lifted_ref, act_ref, near_ref, farther_ref, kf_ref, rf_ref, e_ref, row_ref, col_ref,
     kcat, vcat) = refs
    c = pl.program_id(0)
    q_ref, k_ref, vt_ref, near_ref, farther_ref, kf_ref, rf_ref, e_ref, row_ref, col_ref = (
        camera(r, c)
        for r in (q_ref, k_ref, vt_ref, near_ref, farther_ref, kf_ref, rf_ref, e_ref, row_ref, col_ref)
    )
    clip_ref, lifted_ref, act_ref = (camera_slabs(r, c) for r in (clip_ref, lifted_ref, act_ref))
    own = own_s[0]
    count = counts_s[c, own]
    blk, width = q_ref.shape[1:]
    half = width // 2
    keys = (1 + picks) * blk
    pairs = width // 128

    @pl.when(c == 0)
    def _():
        vcat[:, 128:] = jnp.ones((pairs, PAD, keys), BF16)

    ones_h = head_ones(half, head)
    rows = jnp.concatenate([arrived_ref[lists_s[c, own, s]] for s in range(picks)], axis=0)
    kcat[:blk] = k_ref[0]
    vcat[:, :128, :blk] = vt_ref[0].reshape(pairs, 128, blk)
    vcat[:, :128, blk:] = mm_t(wvt_ref[...], rows).astype(BF16).reshape(pairs, 128, keys - blk)
    for n in range(2):
        cols = slice(n * half, (n + 1) * half)
        pre = mm(rows, wk_ref[:, cols])
        r = lax.rsqrt(head_mean(pre * pre, ones_h, head) + EPSILON)
        k = (pre * r).astype(BF16)
        kcat[blk:, cols] = k
        kf_ref[0, :, cols] = k
        rf_ref[0, :, cols] = r
    low = lax.broadcasted_iota(jnp.int32, (blk, 128), 1) < head
    live = [jnp.where(s < count, 1.0, 0.0) for s in range(picks)]
    mixed = []
    inverses = []
    for p in range(pairs):
        cols = slice(128 * p, 128 * (p + 1))
        q2 = pair_rows(q_ref[0, :, cols], low)
        grown = jnp.exp(mm_t(kcat[:, cols], q2))
        e_ref[0, p, :blk] = grown[:blk].astype(BF16)
        for s in range(picks):
            part = slice((1 + s) * blk, (2 + s) * blk)
            e_ref[0, p, part] = (grown[part] * live[s]).astype(BF16)
        out = mm(vcat[p], e_ref[0, p])
        inverse = 1.0 / out[128:129]
        inverses += [inverse[:, :blk], inverse[:, blk:]]
        out = out[:128] * inverse
        out = jnp.concatenate([out[:head, :blk], out[head:, blk:]], axis=0)
        mixed.append(jnp.transpose(out).astype(BF16))
    inverses = jnp.concatenate(inverses, axis=0)
    row_ref[0] = inverses
    spread = jnp.concatenate([inverses, jnp.zeros((128 - HEADS, blk), F32)], axis=0)
    col_ref[0] = jnp.transpose(spread)
    mixed = jnp.concatenate(mixed, axis=1)
    clip = clip_ref[:, 0].reshape(blk, width).astype(F32)
    lifted = (clip + mm(mixed, wo_ref[...])).astype(BF16)
    lifted_f = lifted.astype(F32)
    act, _ = silu_parts(lifted_f * rms(lifted_f) * gain_ref[...])
    slabs = (clip_ref.shape[0], clip_ref.shape[2], width)
    lifted_ref[:, 0] = lifted.reshape(slabs)
    act = act.astype(BF16).reshape(slabs)
    act_ref[:, 0] = act
    even = lax.rem(own, 2) == 0
    near_ref[0] = jnp.where(even, act[-1], act[0])
    farther_ref[0] = jnp.where(even, act[0], act[-1])


def camera(ref, c):
    return ref.at[pl.ds(c, 1)]


def camera_slabs(ref, c):
    return ref.at[:, pl.ds(c, 1)]


def attend(own, lists, counts, arrived, q, k, vt, clip_t, wk, wvt, wo, gain, head):
    tw, cams, nr, width = clip_t.shape
    blk = tw * nr
    picks = lists.shape[2]
    keys = (1 + picks) * blk
    pairs = width // 128
    args = (arrived, q, k, vt, clip_t, wk, wvt, wo, gain)
    outs = (
            pltpu.VMEM(clip_t.shape, BF16),
            pltpu.VMEM(clip_t.shape, BF16),
            jax.ShapeDtypeStruct((cams, nr, width), BF16),
            jax.ShapeDtypeStruct((cams, nr, width), BF16),
            pltpu.VMEM((cams, picks * blk, width), BF16),
            pltpu.VMEM((cams, picks * blk, width), F32),
            pltpu.VMEM((cams, pairs, keys, 2 * blk), BF16),
            pltpu.VMEM((cams, HEADS, blk), F32),
            pltpu.VMEM((cams, blk, 128), F32),
        )
    return pl.pallas_call(
        functools.partial(attend_kernel, head, picks),
        name="attend",
        out_shape=outs,
        grid_spec=pltpu.PrefetchScalarGridSpec(
            num_scalar_prefetch=3,
            grid=(cams,),
            in_specs=[whole(x.shape) for x in args],
            out_specs=[whole(x.shape) for x in outs],
            scratch_shapes=[
                pltpu.VMEM((keys, width), BF16),
                pltpu.VMEM((pairs, 128 + PAD, keys), BF16),
            ],
        ),
        compiler_params=params(6 + 2 * picks),
    )(own, lists, counts, *args)


def far_values_kernel(picks, own_s, lists_s, arrived_ref, w_ref, out_ref):
    cams = lists_s.shape[0]
    blk = arrived_ref.shape[1]
    for c in range(cams):
        rows = jnp.concatenate([arrived_ref[lists_s[c, own_s[0], s]] for s in range(picks)], axis=0)
        out_ref[c] = mm(rows, w_ref[...]).astype(BF16)


def far_values(own, lists, arrived, w):
    _, blk, width = arrived.shape
    cams, _, picks = lists.shape
    return pl.pallas_call(
        functools.partial(far_values_kernel, picks),
        name="far_values",
        out_shape=pltpu.VMEM((cams, picks * blk, width), BF16),
        grid_spec=pltpu.PrefetchScalarGridSpec(
            num_scalar_prefetch=2,
            grid=(1,),
            in_specs=[whole(arrived.shape), whole(w.shape)],
            out_specs=whole((cams, picks * blk, width)),
        ),
        compiler_params=params(4 + 2 * picks),
        cost_estimate=pl.CostEstimate(
            flops=2 * cams * picks * blk * width * width,
            bytes_accessed=4 * cams * picks * blk * width,
            transcendentals=0,
        ),
    )(own, lists, arrived, w)


def fill_windows(own_s, act_ref, near_ref, farther_ref, x_ref, edge, total):
    width = act_ref.shape[1]
    even = lax.rem(own_s[0], 2) == 0
    near = near_ref[...]
    farther = farther_ref[...]
    x_ref[:edge, :width] = jnp.where(even, farther, near)
    x_ref[edge:, :width] = act_ref[: total - edge]
    x_ref[:, width : 2 * width] = act_ref[...]
    x_ref[: total - edge, 2 * width :] = act_ref[edge:]
    x_ref[total - edge :, 2 * width :] = jnp.where(even, near, farther)


def conv_step(w_ref, x_ref, y_ref, step, transposed):
    width = w_ref.shape[2]
    if transposed:
        total = None
        for q in range(3):
            cols = slice((2 - q) * width, (3 - q) * width)
            part = mm_t(x_ref[:, cols], w_ref[0, q])
            total = part if total is None else total + part
        y_ref[step] = total
    else:
        y_ref[step] = mm(x_ref[...], w_ref[0].reshape(3 * width, width))


def conv_rows(y_ref, start, size, nr, transposed):
    rows = pl.ds(start, size)
    before, centre, after = (2, 1, 0) if transposed else (0, 1, 2)
    place = lax.broadcasted_iota(jnp.int32, (size, 1), 0) % nr
    up = pltpu.roll(y_ref[before, rows, :], 1, 0)
    down = pltpu.roll(y_ref[after, rows, :], size - 1, 0)
    return (
        jnp.where(place == 0, 0.0, up)
        + y_ref[centre, rows, :]
        + jnp.where(place == nr - 1, 0.0, down)
    )


def conv_kernel(body, n_extra, transposed, nr, own_s, act_ref, near_ref, farther_ref, w_ref, *refs):
    extra, outs, (x_ref, y_ref) = refs[:n_extra], refs[n_extra:-2], refs[-2:]
    step = pl.program_id(0)
    total = act_ref.shape[0]
    edge = near_ref.shape[0]

    @pl.when(step == 0)
    def _():
        fill_windows(own_s, act_ref, near_ref, farther_ref, x_ref, edge, total)

    conv_step(w_ref, x_ref, y_ref, step, transposed)

    @pl.when(step == 2)
    def _():
        even = lax.rem(own_s[0], 2) == 0
        body(lambda start, size: conv_rows(y_ref, start, size, nr, transposed), even, edge, extra, outs)


def conv_call(name, body, own, act, near, farther, weights, extra, outs, nr, transposed):
    total, width = act.shape
    edge = near.shape[0]
    return pl.pallas_call(
        functools.partial(conv_kernel, body, len(extra), transposed, nr),
        name=name,
        out_shape=outs,
        grid_spec=pltpu.PrefetchScalarGridSpec(
            num_scalar_prefetch=1,
            grid=(3,),
            in_specs=[
                whole((total, width)),
                whole((edge, width)),
                whole((edge, width)),
                pl.BlockSpec((1, 3, width, width), lambda p, *_: (p, 0, 0, 0)),
            ]
            + [whole(e.shape) for e in extra],
            out_specs=[whole(o.shape) for o in outs],
            scratch_shapes=[
                pltpu.VMEM((total, 3 * width), BF16),
                pltpu.VMEM((3, total, width), F32),
            ],
        ),
        compiler_params=params(14),
        cost_estimate=pl.CostEstimate(
            flops=18 * total * width * width, bytes_accessed=18 * width * width, transcendentals=0
        ),
    )(own, act, near, farther, weights, *extra)


CHUNK = 128


def chunks(total, fn):
    def step(i, carry):
        fn(pl.multiple_of(i * CHUNK, CHUNK))
        return carry

    lax.fori_loop(0, total // CHUNK, step, 0)


def grad_two_body(rows_of, even, edge, extra, outs):
    (out,) = outs

    def one(start):
        out[pl.ds(start, CHUNK), :] = rows_of(start, CHUNK)

    chunks(out.shape[0], one)


def copy_edges(even, edge, full, near, farther):
    total = full.shape[0]
    first = full[:edge]
    last = full[total - edge :]
    near[...] = jnp.where(even, last, first)
    farther[...] = jnp.where(even, first, last)


def conv_one_body(rows_of, even, edge, extra, outs):
    grad_ref, gain_ref = extra
    act_ref, act_near, act_far, d_ref, d_near, d_far = outs
    total = act_ref.shape[0]
    gain = gain_ref[...]

    def one(start):
        rows = pl.ds(start, CHUNK)
        conv = rows_of(start, CHUNK)
        r = rms(conv)
        hat = conv * r
        act, slope = silu_parts(hat * gain)
        act_ref[rows, :] = act.astype(BF16)
        g = grad_ref[rows, :] * slope * gain
        d_ref[rows, :] = (r * (g - hat * jnp.mean(g * hat, axis=-1, keepdims=True))).astype(BF16)

    chunks(total, one)
    copy_edges(even, edge, act_ref, act_near, act_far)
    copy_edges(even, edge, d_ref, d_near, d_far)


def conv_two_body(rows_of, even, edge, extra, outs):
    (lifted_ref,) = extra
    (out,) = outs

    def one(start):
        rows = pl.ds(start, CHUNK)
        out[rows, :] = (lifted_ref[rows, :].astype(F32) + rows_of(start, CHUNK)).astype(BF16)

    chunks(out.shape[0], one)


def grad_one_body(rows_of, even, edge, extra, outs):
    lifted_ref, cot_ref, gain_ref, wo_ref = extra
    d_lifted_ref, d_mixed_ref = outs
    gain = gain_ref[...]
    total = d_lifted_ref.shape[0]

    def one(start):
        rows = pl.ds(start, CHUNK)
        lifted = lifted_ref[rows, :].astype(F32)
        r = rms(lifted)
        hat = lifted * r
        _, slope = silu_parts(hat * gain)
        g = rows_of(start, CHUNK) * slope * gain
        back = r * (g - hat * jnp.mean(g * hat, axis=-1, keepdims=True))
        d_lifted_ref[rows, :] = cot_ref[rows, :].astype(F32) + back

    chunks(total, one)
    d_mixed_ref[...] = mm_t(d_lifted_ref[...].astype(BF16), wo_ref[...]).astype(BF16)


def head_norm_back(grad, hat, r, ones, head):
    hat = hat.astype(F32)
    return r * (grad - hat * head_mean(grad * hat, ones, head))


def pair_grads(p, head, q_ref, v_ref, vf_ref, e_ref, dm_ref, row_ref, col_ref, low):
    blk = q_ref.shape[1]
    cols = slice(128 * p, 128 * (p + 1))
    row = jnp.concatenate([row_ref[0, 2 * p : 2 * p + 1], row_ref[0, 2 * p + 1 : 2 * p + 2]], axis=1)
    col = jnp.where(low, col_ref[0, :, 2 * p : 2 * p + 1], col_ref[0, :, 2 * p + 1 : 2 * p + 2])
    dm = dm_ref[:, 0, :, cols].reshape(blk, 128).astype(F32)
    q2 = pair_rows(q_ref[0, :, cols], low)
    dm2 = pair_rows((dm * col).astype(BF16), low)
    e = e_ref[0, p].astype(F32)
    slope = jnp.concatenate([mm_t(v_ref[0, :, cols], dm2), mm_t(vf_ref[0, :, cols], dm2)], axis=0)
    drift = jnp.sum(e * slope, axis=0, keepdims=True) * row
    return q2, dm2, (e * (slope - drift)).astype(BF16)


def far_grads_kernel(head, picks, own_s, lists_s, counts_s, q_ref, v_ref, vf_ref, e_ref, dm_ref,
                     row_ref, col_ref, kf_ref, rf_ref, wk_ref, wv_ref, send_ref, kgrad, vgrad, shares, sems):
    c = pl.program_id(0)
    q_ref, v_ref, vf_ref, e_ref, row_ref, col_ref, kf_ref, rf_ref = (
        camera(r, c) for r in (q_ref, v_ref, vf_ref, e_ref, row_ref, col_ref, kf_ref, rf_ref)
    )
    dm_ref = camera_slabs(dm_ref, c)
    own = own_s[0]
    blk, width = q_ref.shape[1:]
    low = lax.broadcasted_iota(jnp.int32, (blk, 128), 1) < head
    ones_h = head_ones(width // 2, head)
    for p in range(width // 128):
        cols = slice(128 * p, 128 * (p + 1))
        q2, dm2, d_scaled = pair_grads(
            p, head, q_ref, v_ref, vf_ref, e_ref, dm_ref, row_ref, col_ref, low
        )
        kgrad[:, cols] = mm(d_scaled[blk:], q2)
        vgrad[:, cols] = mm(e_ref[0, p, blk:], dm2).astype(BF16)
    far_k = head_norm_back(kgrad[...], kf_ref[0], rf_ref[0], ones_h, head).astype(BF16)
    share = mm_t(far_k, wk_ref[...]) + mm_t(vgrad[...], wv_ref[...])
    share = share.astype(BF16)
    for s in range(picks):
        shares[c, s] = share[s * blk : (s + 1) * blk]
        pltpu.make_async_copy(
            shares.at[c, s], send_ref.at[lists_s[c, own, s]], sems.at[c, s]
        ).start()

    @pl.when(c == pl.num_programs(0) - 1)
    def _():
        for i in range(shares.shape[0]):
            for s in range(picks):
                pltpu.make_async_copy(shares.at[i, s], send_ref.at[0], sems.at[i, s]).wait()


def far_grads(own, lists, counts, n_cols, q, v, vf, e, dm_t, row, col, kf, rf, wk, wv, head):
    tw, cams, nr, width = dm_t.shape
    blk = tw * nr
    picks = lists.shape[2]
    args = (q, v, vf, e, dm_t, row, col, kf, rf, wk, wv)
    return pl.pallas_call(
        functools.partial(far_grads_kernel, head, picks),
        name="far_grads",
        out_shape=pltpu.HBM((n_cols, blk, width), BF16),
        grid_spec=pltpu.PrefetchScalarGridSpec(
            num_scalar_prefetch=3,
            grid=(cams,),
            in_specs=[whole(x.shape) for x in args],
            out_specs=pl.BlockSpec(memory_space=pltpu.HBM),
            scratch_shapes=[
                pltpu.VMEM((picks * blk, width), F32),
                pltpu.VMEM((picks * blk, width), BF16),
                pltpu.VMEM((cams, picks, blk, width), BF16),
                pltpu.SemaphoreType.DMA((cams, picks)),
            ],
        ),
        compiler_params=params(6 + 5 * picks),
    )(own, lists, counts, *args)


def own_grads_kernel(head, q_ref, v_ref, vf_ref, e_ref, dm_ref, row_ref, col_ref, k_ref, kf_ref,
                     rq_ref, rk_ref, wq_ref, wk_ref, wv_ref, out_ref):
    c = pl.program_id(0)
    q_ref, v_ref, vf_ref, e_ref, row_ref, col_ref, k_ref, kf_ref, rq_ref, rk_ref, out_ref = (
        camera(r, c)
        for r in (q_ref, v_ref, vf_ref, e_ref, row_ref, col_ref, k_ref, kf_ref, rq_ref, rk_ref, out_ref)
    )
    dm_ref = camera_slabs(dm_ref, c)
    blk, width = q_ref.shape[1:]
    low = lax.broadcasted_iota(jnp.int32, (blk, 128), 1) < head
    ones_h = head_ones(width // 2, head)
    scale = head ** (-0.5)
    dq, dk, dv = [], [], []
    for p in range(width // 128):
        cols = slice(128 * p, 128 * (p + 1))
        q2, dm2, d_scaled = pair_grads(
            p, head, q_ref, v_ref, vf_ref, e_ref, dm_ref, row_ref, col_ref, low
        )
        dk.append(mm(d_scaled[:blk], q2))
        dv.append(mm(e_ref[0, p, :blk], dm2).astype(BF16))
        flipped = jnp.transpose(d_scaled)
        both = mm(flipped[:, :blk], k_ref[0, :, cols]) + mm(flipped[:, blk:], kf_ref[0, :, cols])
        dq.append(jnp.where(low, both[:blk], both[blk:]) * scale)
    dq, dk, dv = (jnp.concatenate(parts, axis=1) for parts in (dq, dk, dv))
    q_hat = q_ref[0].astype(F32) * (1.0 / scale)
    dq = head_norm_back(dq, q_hat, rq_ref[0], ones_h, head).astype(BF16)
    dk = head_norm_back(dk, k_ref[0], rk_ref[0], ones_h, head).astype(BF16)
    out_ref[0] = mm_t(dq, wq_ref[...]) + mm_t(dk, wk_ref[...]) + mm_t(dv, wv_ref[...])


def own_grads(q, v, vf, e, dm_t, row, col, k, kf, rq, rk, wq, wk, wv, head):
    tw, cams, nr, width = dm_t.shape
    blk = tw * nr
    args = (q, v, vf, e, dm_t, row, col, k, kf, rq, rk, wq, wk, wv)
    return pl.pallas_call(
        functools.partial(own_grads_kernel, head),
        name="own_grads",
        out_shape=pltpu.VMEM((cams, blk, width), F32),
        grid_spec=pltpu.PrefetchScalarGridSpec(
            num_scalar_prefetch=0,
            grid=(cams,),
            in_specs=[whole(x.shape) for x in args],
            out_specs=whole((cams, blk, width)),
        ),
        compiler_params=params(12 + e.shape[2] * 8 // 256),
        cost_estimate=pl.CostEstimate(
            flops=20 * cams * blk * width * width, bytes_accessed=4 * e.size, transcendentals=0
        ),
    )(*args)


def final_kernel(own_s, match_s, lists_s, counts_s, back_ref, rows_ref, clip_ref, dl_ref, gain_ref, out_ref, acc):
    cams, n_cols, picks = lists_s.shape
    own = own_s[0]
    me = pl.program_id(0)
    rows_ref = camera(rows_ref, me)
    clip_ref, dl_ref, out_ref = (camera_slabs(r, me) for r in (clip_ref, dl_ref, out_ref))
    tw, _, nr, width = clip_ref.shape
    blk = tw * nr
    source = jnp.int32(0)
    for c in range(cams):
        source = jnp.where(match_s[c] == me, c, source)
    acc[...] = rows_ref[0]
    for i in range(n_cols):
        hit = jnp.bool_(False)
        for s in range(picks):
            hit = hit | ((lists_s[source, i, s] == own) & (s < counts_s[source, i]))

        @pl.when(hit)
        def _():
            acc[...] += back_ref[i].astype(F32)

    x = clip_ref[:, 0].reshape(blk, width).astype(F32)
    r = rms(x)
    hat = x * r
    g = acc[...] * gain_ref[...]
    d = dl_ref[:, 0].reshape(blk, width) + r * (
        g - hat * jnp.mean(g * hat, axis=-1, keepdims=True)
    )
    out_ref[:, 0] = d.astype(BF16).reshape(tw, nr, width)


def final(own, matching, lists, counts, back, rows, clip_t, d_lifted, gain):
    tw, cams, nr, width = clip_t.shape
    blk = tw * nr
    slab = pl.BlockSpec((tw, 1, nr, width), lambda c, *_: (0, c, 0, 0))
    return pl.pallas_call(
        final_kernel,
        name="final",
        out_shape=jax.ShapeDtypeStruct(clip_t.shape, BF16),
        grid_spec=pltpu.PrefetchScalarGridSpec(
            num_scalar_prefetch=4,
            grid=(cams,),
            in_specs=[whole(a.shape) for a in (back, rows, clip_t, d_lifted, gain)],
            out_specs=whole(clip_t.shape),
            scratch_shapes=[pltpu.VMEM((blk, width), F32)],
        ),
        compiler_params=params(8),
    )(own, matching, lists, counts, back, rows, clip_t, d_lifted, gain)


def exchange_edges(near, farther):
    size = lax.axis_size("cols")
    inner = [(i, i ^ 1) for i in range(size)]
    outer = [(i, i + 1 if i % 2 else i - 1) for i in range(1, size - 1)]
    return lax.ppermute(near, "cols", inner), lax.ppermute(farther, "cols", outer)


def local(
    clip_tokens,
    cotangent,
    gain_attn,
    w_query,
    w_key,
    w_value,
    w_out,
    gain_first,
    conv_first,
    gain_second,
    conv_second,
    matching,
    block_lists,
    counts,
):
    views, nr, tw, width = clip_tokens.shape
    head = width // HEADS
    n_cols = lax.axis_size("cols")
    own_index = lax.axis_index("cols").astype(jnp.int32)
    own = own_index.reshape(1)
    total = views * nr * tw
    blk = nr * tw
    flat = (total, width)
    slabs = (tw, views, nr, width)
    gain_attn = gain_attn.reshape(1, width)
    gain_first = gain_first.reshape(1, width)
    gain_second = gain_second.reshape(1, width)

    clip_t = jnp.transpose(clip_tokens, (2, 0, 1, 3))
    cot_t = jnp.transpose(cotangent, (2, 0, 1, 3))
    odd = own_index % 2
    last = (tw - 1) * (1 - odd)
    cot_near = lax.dynamic_index_in_dim(cot_t, last, 0, keepdims=False).reshape(-1, width)
    cot_far = lax.dynamic_index_in_dim(cot_t, tw - 1 - last, 0, keepdims=False).reshape(-1, width)

    rows, send = prep(n_cols, own, matching, block_lists, counts, clip_t, gain_attn)
    arrived = lax.all_to_all(send, "cols", split_axis=0, concat_axis=0, tiled=True)
    w_value_t = w_value.T
    q, k, v, vt, rq, rk = project(rows.reshape(flat), w_query, w_key, w_value, w_value_t, head, blk)
    q, k, v, rq, rk = (a.reshape(views, blk, width) for a in (q, k, v, rq, rk))
    arrived, q, k, v, vt, rq, rk, cot_t, cot_near, cot_far = lax.optimization_barrier(
        (arrived, q, k, v, vt, rq, rk, cot_t, cot_near, cot_far)
    )
    cot_near, cot_far = exchange_edges(cot_near, cot_far)
    lifted, act_one, near, farther, kf, rf, e, row, col = attend(
        own, block_lists, counts, arrived, q, k, vt, clip_t, w_key, w_value_t, w_out, gain_first, head
    )
    edge = (views * nr, width)
    near, farther = exchange_edges(near.reshape(edge), farther.reshape(edge))
    (d_act_two,) = conv_call(
        "grad_two", grad_two_body, own, cot_t.reshape(flat), cot_near, cot_far, conv_second,
        (), (pltpu.VMEM(flat, F32),), nr, True,
    )
    flat_bf = pltpu.VMEM(flat, BF16)
    edge_bf = jax.ShapeDtypeStruct(edge, BF16)
    act_two, act_near, act_far, d_conv, d_near, d_far = conv_call(
        "conv_one", conv_one_body, own, act_one.reshape(flat), near, farther, conv_first,
        (d_act_two, gain_second),
        (flat_bf, edge_bf, edge_bf, flat_bf, edge_bf, edge_bf), nr, False,
    )
    d_near, d_far = exchange_edges(d_near, d_far)
    vf = far_values(own, block_lists, arrived, w_value)
    d_near, d_far, vf = lax.optimization_barrier((d_near, d_far, vf))
    d_lifted, d_mixed = conv_call(
        "grad_one", grad_one_body, own, d_conv, d_near, d_far, conv_first,
        (lifted.reshape(flat), cot_t.reshape(flat), gain_first, w_out),
        (pltpu.VMEM(flat, F32), flat_bf), nr, True,
    )
    d_mixed, act_near, act_far = lax.optimization_barrier((d_mixed, act_near, act_far))
    d_mixed = d_mixed.reshape(slabs)
    act_near, act_far = exchange_edges(act_near, act_far)
    send_back = far_grads(
        own, block_lists, counts, n_cols, q, v, vf, e, d_mixed, row, col, kf, rf, w_key, w_value, head
    )
    send_back, act_near, act_far = lax.optimization_barrier((send_back, act_near, act_far))
    back = lax.all_to_all(send_back, "cols", split_axis=0, concat_axis=0, tiled=True)
    (result,) = conv_call(
        "conv_two", conv_two_body, own, act_two, act_near, act_far, conv_second,
        (lifted.reshape(flat),), (jax.ShapeDtypeStruct(flat, BF16),), nr, False,
    )
    d_rows = own_grads(
        q, v, vf, e, d_mixed, row, col, k, kf, rq, rk, w_query, w_key, w_value, head
    )
    d_clip = final(own, matching, block_lists, counts, back, d_rows, clip_t, d_lifted.reshape(slabs), gain_attn)
    return (
        jnp.transpose(result.reshape(slabs), (1, 2, 0, 3)),
        jnp.transpose(d_clip, (1, 2, 0, 3)),
    )


def solution(mesh):
    tiles = P("groups", None, "cols", None)
    in_specs = (tiles, tiles) + (P(),) * 12
    return jax.shard_map(
        local, mesh=mesh, in_specs=in_specs, out_specs=(tiles, tiles), check_vma=False
    )
```

```python
import functools

import jax
import jax.numpy as jnp
from jax import lax
from jax.experimental import pallas as pl
from jax.experimental.pallas import tpu as pltpu
from jax.sharding import PartitionSpec as P

HEADS = 8
EPSILON = 1e-06
F32 = jnp.float32
BF16 = jnp.bfloat16


def mm(a, b):
    return lax.dot_general(a, b, (((1,), (0,)), ((), ())), preferred_element_type=F32)


def mm_t(a, b):
    return lax.dot_general(a, b, (((1,), (1,)), ((), ())), preferred_element_type=F32)


def params(mib):
    return pltpu.CompilerParams(vmem_limit_bytes=mib * 1024 * 1024)


def hbm(x):
    return pltpu.with_memory_space_constraint(x, pltpu.HBM)


def vmem(x):
    return pltpu.with_memory_space_constraint(x, pltpu.VMEM)


def whole(shape):
    zeros = (0,) * len(shape)
    return pl.BlockSpec(shape, lambda *_: zeros)


def rms(values):
    return lax.rsqrt(jnp.mean(values * values, axis=-1, keepdims=True) + EPSILON)


def silu_parts(u):
    sigmoid = 0.5 + 0.5 * jnp.tanh(0.5 * u)
    return u * sigmoid, sigmoid * (1.0 + u * (1.0 - sigmoid))


def head_ones(width, head):
    rows = lax.broadcasted_iota(jnp.int32, (width, width), 0) // head
    cols = lax.broadcasted_iota(jnp.int32, (width, width), 1) // head
    return jnp.where(rows == cols, 1.0, 0.0).astype(BF16)


def head_mean(values, ones, head):
    width = ones.shape[0]
    parts = [
        mm(values[:, i : i + width].astype(BF16), ones)
        for i in range(0, values.shape[1], width)
    ]
    return jnp.concatenate(parts, axis=1) * (1.0 / head)


def prep_kernel(n_cols, own_s, match_s, lists_s, counts_s, clip_ref, gain_ref, rows_ref, send_ref, sem):
    cams = match_s.shape[0]
    picks = lists_s.shape[2]
    own = own_s[0]
    tw, _, nr, width = clip_ref.shape
    for c in range(cams):
        x = clip_ref[:, c].reshape(tw * nr, width).astype(F32)
        rows_ref[c] = (x * rms(x) * gain_ref[...]).astype(BF16)

    def copy(i):
        cam = jnp.int32(0)
        for c in range(cams):
            for s in range(picks):
                hit = (lists_s[c, i, s] == own) & (s < counts_s[c, i])
                cam = jnp.where(hit, match_s[c], cam)
        pltpu.make_async_copy(rows_ref.at[cam], send_ref.at[i], sem.at[i]).start()

    def start(i, carry):
        copy(i)
        return carry

    lax.fori_loop(0, n_cols, start, 0)

    def wait(i, carry):
        pltpu.make_async_copy(rows_ref.at[0], send_ref.at[i], sem.at[i]).wait()
        return carry

    lax.fori_loop(0, n_cols, wait, 0)


def prep(n_cols, own, matching, lists, counts, clip_t, gain):
    tw, cams, nr, width = clip_t.shape
    blk = tw * nr
    return pl.pallas_call(
        functools.partial(prep_kernel, n_cols),
        name="prep",
        out_shape=(
            jax.ShapeDtypeStruct((cams, blk, width), BF16),
            pltpu.HBM((n_cols, blk, width), BF16),
        ),
        grid_spec=pltpu.PrefetchScalarGridSpec(
            num_scalar_prefetch=4,
            grid=(1,),
            in_specs=[whole(clip_t.shape), whole((1, width))],
            out_specs=[whole((cams, blk, width)), pl.BlockSpec(memory_space=pltpu.HBM)],
            scratch_shapes=[pltpu.SemaphoreType.DMA((n_cols,))],
        ),
        compiler_params=params(8),
    )(own, matching, lists, counts, clip_t, gain)


def project_kernel(head, blk, rows_ref, wq_ref, wk_ref, wv_ref, wvt_ref, q_ref, k_ref, v_ref, vt_ref, rq_ref, rk_ref):
    rows = rows_ref[...]
    total, width = rows.shape
    half = width // 2
    ones = head_ones(half, head)
    for n in range(2):
        cols = slice(n * half, (n + 1) * half)
        for w_ref, o_ref, r_ref, scale in (
            (wq_ref, q_ref, rq_ref, head ** (-0.5)),
            (wk_ref, k_ref, rk_ref, 1.0),
        ):
            pre = mm(rows, w_ref[:, cols])
            r = lax.rsqrt(head_mean(pre * pre, ones, head) + EPSILON)
            o_ref[:, cols] = (pre * r * scale).astype(BF16)
            r_ref[:, cols] = r
        v_ref[:, cols] = mm(rows, wv_ref[:, cols]).astype(BF16)
    for c in range(total // blk):
        vt_ref[c] = mm_t(wvt_ref[...], rows_ref[c * blk : (c + 1) * blk]).astype(BF16)


def project(rows, wq, wk, wv, wvt, head, blk):
    total, width = rows.shape
    full = (total, width)
    return pl.pallas_call(
        functools.partial(project_kernel, head, blk),
        name="project",
        out_shape=(
            pltpu.HBM(full, BF16),
            pltpu.HBM(full, BF16),
            pltpu.HBM(full, BF16),
            pltpu.HBM((total // blk, width, blk), BF16),
            pltpu.HBM(full, F32),
            pltpu.HBM(full, F32),
        ),
        compiler_params=params(12),
        cost_estimate=pl.CostEstimate(
            flops=8 * total * width * width, bytes_accessed=20 * total * width, transcendentals=0
        ),
    )(rows, wq, wk, wv, wvt)


def pair_rows(x, low):
    zero = jnp.zeros_like(x)
    return jnp.concatenate([jnp.where(low, x, zero), jnp.where(low, zero, x)], axis=0)


PAD = 16


def attend_kernel(head, picks, own_s, lists_s, counts_s, *refs):
    (arrived_ref, q_ref, k_ref, vt_ref, clip_ref, wk_ref, wvt_ref, wo_ref, gain_ref,
     lifted_ref, act_ref, near_ref, farther_ref, kf_ref, rf_ref, e_ref, row_ref, col_ref,
     mixed_ref, kcat, vcat) = refs
    c = pl.program_id(0)
    near_ref, farther_ref, kf_ref, rf_ref, e_ref, row_ref, col_ref = (
        r.at[pl.ds(c, 1)] for r in (near_ref, farther_ref, kf_ref, rf_ref, e_ref, row_ref, col_ref)
    )
    lifted_ref, act_ref = (r.at[:, pl.ds(c, 1)] for r in (lifted_ref, act_ref))
    own = own_s[0]
    count = counts_s[c, own]
    blk, width = q_ref.shape[1:]
    half = width // 2
    keys = (1 + picks) * blk
    pairs = width // 128

    @pl.when(c == 0)
    def _():
        vcat[:, 128:] = jnp.ones((pairs, PAD, keys), BF16)

    ones_h = head_ones(half, head)
    rows = jnp.concatenate([arrived_ref[lists_s[c, own, s]] for s in range(picks)], axis=0)
    kcat[:blk] = k_ref[0]
    vcat[:, :128, :blk] = vt_ref[0].reshape(pairs, 128, blk)
    vcat[:, :128, blk:] = mm_t(wvt_ref[...], rows).astype(BF16).reshape(pairs, 128, keys - blk)
    for n in range(2):
        cols = slice(n * half, (n + 1) * half)
        pre = mm(rows, wk_ref[:, cols])
        r = lax.rsqrt(head_mean(pre * pre, ones_h, head) + EPSILON)
        k = (pre * r).astype(BF16)
        kcat[blk:, cols] = k
        kf_ref[0, :, cols] = k
        rf_ref[0, :, cols] = r
    low = lax.broadcasted_iota(jnp.int32, (blk, 128), 1) < head
    live = [jnp.where(s < count, 1.0, 0.0) for s in range(picks)]
    mixed = []
    inverses = []
    for p in range(pairs):
        cols = slice(128 * p, 128 * (p + 1))
        q2 = pair_rows(q_ref[0, :, cols], low)
        grown = jnp.exp(mm_t(kcat[:, cols], q2))
        e_ref[0, p, :blk] = grown[:blk].astype(BF16)
        for s in range(picks):
            part = slice((1 + s) * blk, (2 + s) * blk)
            e_ref[0, p, part] = (grown[part] * live[s]).astype(BF16)
        out = mm(vcat[p], e_ref[0, p])
        inverse = 1.0 / out[128:129]
        inverses += [inverse[:, :blk], inverse[:, blk:]]
        out = out[:128] * inverse
        out = jnp.concatenate([out[:head, :blk], out[head:, blk:]], axis=0)
        mixed.append(jnp.transpose(out).astype(BF16))
    inverses = jnp.concatenate(inverses, axis=0)
    row_ref[0] = inverses
    spread = jnp.concatenate([inverses, jnp.zeros((128 - HEADS, blk), F32)], axis=0)
    col_ref[0] = jnp.transpose(spread)
    mixed = jnp.concatenate(mixed, axis=1)
    mixed_ref[c] = mixed
    clip = clip_ref[:, 0].reshape(blk, width).astype(F32)
    lifted = (clip + mm(mixed, wo_ref[...])).astype(BF16)
    lifted_f = lifted.astype(F32)
    act, _ = silu_parts(lifted_f * rms(lifted_f) * gain_ref[...])
    slabs = (clip_ref.shape[0], clip_ref.shape[2], width)
    lifted_ref[:, 0] = lifted.reshape(slabs)
    act = act.astype(BF16).reshape(slabs)
    act_ref[:, 0] = act
    even = lax.rem(own, 2) == 0
    near_ref[0] = jnp.where(even, act[-1], act[0])
    farther_ref[0] = jnp.where(even, act[0], act[-1])


def per_camera(x):
    zeros = (0,) * (x.ndim - 1)
    return pl.BlockSpec((1,) + x.shape[1:], lambda c, *_: (c,) + zeros)


def attend(own, lists, counts, arrived, q, k, vt, clip_t, wk, wvt, wo, gain, head):
    tw, cams, nr, width = clip_t.shape
    blk = tw * nr
    picks = lists.shape[2]
    keys = (1 + picks) * blk
    pairs = width // 128
    slab = pl.BlockSpec((tw, 1, nr, width), lambda c, *_: (0, c, 0, 0))
    outs = (
        pltpu.VMEM(clip_t.shape, BF16),
        pltpu.VMEM(clip_t.shape, BF16),
        jax.ShapeDtypeStruct((cams, nr, width), BF16),
        jax.ShapeDtypeStruct((cams, nr, width), BF16),
        pltpu.VMEM((cams, picks * blk, width), BF16),
        pltpu.VMEM((cams, picks * blk, width), F32),
        pltpu.VMEM((cams, pairs, keys, 2 * blk), BF16),
        pltpu.VMEM((cams, HEADS, blk), F32),
        pltpu.VMEM((cams, blk, 128), F32),
        pltpu.VMEM((cams, blk, width), BF16),
    )
    weights = (wk, wvt, wo, gain)
    return pl.pallas_call(
        functools.partial(attend_kernel, head, picks),
        name="attend",
        out_shape=outs,
        grid_spec=pltpu.PrefetchScalarGridSpec(
            num_scalar_prefetch=3,
            grid=(cams,),
            in_specs=[whole(arrived.shape), per_camera(q), per_camera(k), per_camera(vt), slab]
            + [whole(x.shape) for x in weights],
            out_specs=[whole(x.shape) for x in outs],
            scratch_shapes=[
                pltpu.VMEM((keys, width), BF16),
                pltpu.VMEM((pairs, 128 + PAD, keys), BF16),
            ],
        ),
        compiler_params=params(10 + picks),
    )(own, lists, counts, arrived, hbm(q), hbm(k), hbm(vt), hbm(clip_t), *weights)


def far_values_kernel(arrived_ref, w_ref, out_ref):
    out_ref[...] = mm(arrived_ref[...], w_ref[...]).astype(BF16)


def far_values(arrived, w):
    total, width = arrived.shape
    return pl.pallas_call(
        far_values_kernel,
        name="far_values",
        out_shape=pltpu.VMEM((total, width), BF16),
        grid=(total // 512,),
        in_specs=[pl.BlockSpec((512, width), lambda i: (i, 0)), whole(w.shape)],
        out_specs=pl.BlockSpec((512, width), lambda i: (i, 0)),
        compiler_params=params(6),
        cost_estimate=pl.CostEstimate(
            flops=2 * total * width * width, bytes_accessed=4 * total * width, transcendentals=0
        ),
    )(arrived, w)


def fill_windows(own_s, act_ref, near_ref, farther_ref, x_ref, edge, total):
    width = act_ref.shape[1]
    even = lax.rem(own_s[0], 2) == 0
    near = near_ref[...]
    farther = farther_ref[...]
    x_ref[:edge, :width] = jnp.where(even, farther, near)
    x_ref[edge:, :width] = act_ref[: total - edge]
    x_ref[:, width : 2 * width] = act_ref[...]
    x_ref[: total - edge, 2 * width :] = act_ref[edge:]
    x_ref[total - edge :, 2 * width :] = jnp.where(even, near, farther)


def conv_step(w_ref, x_ref, y_ref, step, transposed):
    width = w_ref.shape[2]
    if transposed:
        total = None
        for q in range(3):
            cols = slice((2 - q) * width, (3 - q) * width)
            part = mm_t(x_ref[:, cols], w_ref[0, q])
            total = part if total is None else total + part
        y_ref[step] = total
    else:
        y_ref[step] = mm(x_ref[...], w_ref[0].reshape(3 * width, width))


def conv_rows(y_ref, start, size, nr, transposed):
    rows = pl.ds(start, size)
    before, centre, after = (2, 1, 0) if transposed else (0, 1, 2)
    place = lax.broadcasted_iota(jnp.int32, (size, 1), 0) % nr
    up = pltpu.roll(y_ref[before, rows, :], 1, 0)
    down = pltpu.roll(y_ref[after, rows, :], size - 1, 0)
    return (
        jnp.where(place == 0, 0.0, up)
        + y_ref[centre, rows, :]
        + jnp.where(place == nr - 1, 0.0, down)
    )


def conv_kernel(body, n_extra, transposed, nr, own_s, act_ref, near_ref, farther_ref, w_ref, *refs):
    extra, outs, (x_ref, y_ref) = refs[:n_extra], refs[n_extra:-2], refs[-2:]
    step = pl.program_id(0)
    total = act_ref.shape[0]
    edge = near_ref.shape[0]

    @pl.when(step == 0)
    def _():
        fill_windows(own_s, act_ref, near_ref, farther_ref, x_ref, edge, total)

    conv_step(w_ref, x_ref, y_ref, step, transposed)

    @pl.when(step == 2)
    def _():
        even = lax.rem(own_s[0], 2) == 0
        body(lambda start, size: conv_rows(y_ref, start, size, nr, transposed), even, edge, extra, outs)


def conv_call(name, body, own, act, near, farther, weights, extra, outs, nr, transposed):
    total, width = act.shape
    edge = near.shape[0]
    return pl.pallas_call(
        functools.partial(conv_kernel, body, len(extra), transposed, nr),
        name=name,
        out_shape=outs,
        grid_spec=pltpu.PrefetchScalarGridSpec(
            num_scalar_prefetch=1,
            grid=(3,),
            in_specs=[
                whole((total, width)),
                whole((edge, width)),
                whole((edge, width)),
                pl.BlockSpec((1, 3, width, width), lambda p, *_: (p, 0, 0, 0)),
            ]
            + [whole(e.shape) for e in extra],
            out_specs=[whole(o.shape) for o in outs],
            scratch_shapes=[
                pltpu.VMEM((total, 3 * width), BF16),
                pltpu.VMEM((3, total, width), F32),
            ],
        ),
        compiler_params=params(14),
        cost_estimate=pl.CostEstimate(
            flops=18 * total * width * width, bytes_accessed=18 * width * width, transcendentals=0
        ),
    )(own, act, near, farther, weights, *extra)


CHUNK = 128


def chunks(total, fn):
    def step(i, carry):
        fn(pl.multiple_of(i * CHUNK, CHUNK))
        return carry

    lax.fori_loop(0, total // CHUNK, step, 0)


def grad_two_body(rows_of, even, edge, extra, outs):
    (out,) = outs

    def one(start):
        out[pl.ds(start, CHUNK), :] = rows_of(start, CHUNK)

    chunks(out.shape[0], one)


def copy_edges(even, edge, full, near, farther):
    total = full.shape[0]
    first = full[:edge]
    last = full[total - edge :]
    near[...] = jnp.where(even, last, first)
    farther[...] = jnp.where(even, first, last)


def conv_one_body(rows_of, even, edge, extra, outs):
    grad_ref, gain_ref = extra
    act_ref, act_near, act_far, d_ref, d_near, d_far = outs
    total = act_ref.shape[0]
    gain = gain_ref[...]

    def one(start):
        rows = pl.ds(start, CHUNK)
        conv = rows_of(start, CHUNK)
        r = rms(conv)
        hat = conv * r
        act, slope = silu_parts(hat * gain)
        act_ref[rows, :] = act.astype(BF16)
        g = grad_ref[rows, :] * slope * gain
        d_ref[rows, :] = (r * (g - hat * jnp.mean(g * hat, axis=-1, keepdims=True))).astype(BF16)

    chunks(total, one)
    copy_edges(even, edge, act_ref, act_near, act_far)
    copy_edges(even, edge, d_ref, d_near, d_far)


def conv_two_body(rows_of, even, edge, extra, outs):
    (lifted_ref,) = extra
    (out,) = outs

    def one(start):
        rows = pl.ds(start, CHUNK)
        out[rows, :] = (lifted_ref[rows, :].astype(F32) + rows_of(start, CHUNK)).astype(BF16)

    chunks(out.shape[0], one)


def grad_one_body(rows_of, even, edge, extra, outs):
    lifted_ref, cot_ref, gain_ref, wo_ref = extra
    d_lifted_ref, d_mixed_ref = outs
    gain = gain_ref[...]
    total = d_lifted_ref.shape[0]

    def one(start):
        rows = pl.ds(start, CHUNK)
        lifted = lifted_ref[rows, :].astype(F32)
        r = rms(lifted)
        hat = lifted * r
        _, slope = silu_parts(hat * gain)
        g = rows_of(start, CHUNK) * slope * gain
        back = r * (g - hat * jnp.mean(g * hat, axis=-1, keepdims=True))
        d_lifted_ref[rows, :] = cot_ref[rows, :].astype(F32) + back

    chunks(total, one)
    d_mixed_ref[...] = mm_t(d_lifted_ref[...].astype(BF16), wo_ref[...]).astype(BF16)


def head_norm_back(grad, hat, r, ones, head):
    hat = hat.astype(F32)
    return r * (grad - hat * head_mean(grad * hat, ones, head))


def drift_rows(head, dm, mixed, row):
    width = dm.shape[1]
    lanes = lax.broadcasted_iota(jnp.int32, (PAD, width), 1) // head
    picked = (lanes == lax.broadcasted_iota(jnp.int32, (PAD, width), 0)).astype(BF16)
    product = (dm.astype(F32) * mixed.astype(F32)).astype(BF16)
    return mm_t(picked, product)[:HEADS] * row


def pair_queries(p, q, dm, col, drift, low):
    cols = slice(128 * p, 128 * (p + 1))
    spread = jnp.where(low, col[:, 2 * p : 2 * p + 1], col[:, 2 * p + 1 : 2 * p + 2])
    q2 = pair_rows(q[:, cols], low)
    dm2 = pair_rows((dm[:, cols].astype(F32) * spread).astype(BF16), low)
    shift = jnp.concatenate([drift[2 * p : 2 * p + 1], drift[2 * p + 1 : 2 * p + 2]], axis=1)
    return q2, dm2, shift


def far_grads_kernel(head, picks, own_s, lists_s, counts_s, q_ref, vf_ref, e_ref, dm_ref, mixed_ref,
                     row_ref, col_ref, kf_ref, rf_ref, wk_ref, wv_ref, send_ref, kgrad, vgrad, shares, sems):
    c = pl.program_id(0)
    own = own_s[0]
    cams, blk, width = mixed_ref.shape
    low = lax.broadcasted_iota(jnp.int32, (blk, 128), 1) < head
    q = q_ref[0]
    dm = dm_ref[:, c].reshape(blk, width)
    drift = drift_rows(head, dm, mixed_ref[c], row_ref[c])
    col = col_ref[c]
    for p in range(width // 128):
        cols = slice(128 * p, 128 * (p + 1))
        q2, dm2, shift = pair_queries(p, q, dm, col, drift, low)
        far_v = jnp.concatenate([vf_ref[lists_s[c, own, s], :, cols] for s in range(picks)], axis=0)
        e = e_ref[c, p, blk:]
        d_scaled = (e.astype(F32) * (mm_t(far_v, dm2) - shift)).astype(BF16)
        kgrad[c, :, cols] = mm(d_scaled, q2)
        vgrad[c, :, cols] = mm(e, dm2).astype(BF16)

    @pl.when(c == cams - 1)
    def _():
        ones_h = head_ones(width // 2, head)

        def back(i, carry):
            grad = head_norm_back(kgrad[i], kf_ref[i], rf_ref[i], ones_h, head)
            shares[i] = grad.astype(BF16)
            return carry

        lax.fori_loop(0, cams, back, 0)
        shape = (picks * blk, width)
        for first, last in ((0, (cams + 1) // 2), ((cams + 1) // 2, cams)):
            count = last - first
            share = mm_t(shares[first:last].reshape(count * shape[0], width), wk_ref[...])
            share = share + mm_t(vgrad[first:last].reshape(count * shape[0], width), wv_ref[...])
            shares[first:last] = share.astype(BF16).reshape((count,) + shape)
            for i in range(first, last):
                for s in range(picks):
                    pltpu.make_async_copy(
                        shares.at[i, pl.ds(s * blk, blk)],
                        send_ref.at[lists_s[i, own, s]],
                        sems.at[i, s],
                    ).start()
        for i in range(cams):
            for s in range(picks):
                pltpu.make_async_copy(
                    shares.at[i, pl.ds(s * blk, blk)], send_ref.at[0], sems.at[i, s]
                ).wait()


def far_grads(own, lists, counts, n_cols, q, vf, e, dm_t, mixed, row, col, kf, rf, wk, wv, head):
    cams, blk, width = mixed.shape
    picks = lists.shape[2]
    args = (vf, e, dm_t, mixed, row, col, kf, rf, wk, wv)
    return pl.pallas_call(
        functools.partial(far_grads_kernel, head, picks),
        name="far_grads",
        out_shape=pltpu.HBM((n_cols, blk, width), BF16),
        grid_spec=pltpu.PrefetchScalarGridSpec(
            num_scalar_prefetch=3,
            grid=(cams,),
            in_specs=[per_camera(q)] + [whole(x.shape) for x in args],
            out_specs=pl.BlockSpec(memory_space=pltpu.HBM),
            scratch_shapes=[
                pltpu.VMEM((cams, picks * blk, width), F32),
                pltpu.VMEM((cams, picks * blk, width), BF16),
                pltpu.VMEM((cams, picks * blk, width), BF16),
                pltpu.SemaphoreType.DMA((cams, picks)),
            ],
        ),
        compiler_params=params(4 + 6 * picks),
    )(own, lists, counts, hbm(q), *args)


def own_grads_kernel(head, picks, own_s, lists_s, q_ref, k_ref, v_ref, rq_ref, rk_ref, vf_ref, e_ref, dm_ref,
                     mixed_ref, row_ref, col_ref, kf_ref, wq_ref, wk_ref, wv_ref, out_ref):
    c = pl.program_id(0)
    own = own_s[0]
    cams, blk, width = mixed_ref.shape
    low = lax.broadcasted_iota(jnp.int32, (blk, 128), 1) < head
    ones_h = head_ones(width // 2, head)
    scale = head ** (-0.5)
    q = q_ref[0]
    dm = dm_ref[:, c].reshape(blk, width)
    drift = drift_rows(head, dm, mixed_ref[c], row_ref[c])
    col = col_ref[c]
    listed = [lists_s[c, own, s] for s in range(picks)]
    dq, dk, dv = [], [], []
    for p in range(width // 128):
        cols = slice(128 * p, 128 * (p + 1))
        q2, dm2, shift = pair_queries(p, q, dm, col, drift, low)
        all_v = jnp.concatenate([v_ref[0, :, cols]] + [vf_ref[i, :, cols] for i in listed], axis=0)
        all_k = jnp.concatenate([k_ref[0, :, cols], kf_ref[c, :, cols]], axis=0)
        e = e_ref[c, p]
        d_scaled = (e.astype(F32) * (mm_t(all_v, dm2) - shift)).astype(BF16)
        dk.append(mm(d_scaled[:blk], q2))
        dv.append(mm(e[:blk], dm2).astype(BF16))
        both = mm(jnp.transpose(d_scaled), all_k)
        dq.append(jnp.where(low, both[:blk], both[blk:]) * scale)
    dq, dk, dv = (jnp.concatenate(parts, axis=1) for parts in (dq, dk, dv))
    q_hat = q.astype(F32) * (1.0 / scale)
    dq = head_norm_back(dq, q_hat, rq_ref[0], ones_h, head).astype(BF16)
    dk = head_norm_back(dk, k_ref[0], rk_ref[0], ones_h, head).astype(BF16)
    out_ref[0] = mm_t(dq, wq_ref[...]) + mm_t(dk, wk_ref[...]) + mm_t(dv, wv_ref[...])


def own_grads(own, lists, q, k, v, rq, rk, vf, e, dm_t, mixed, row, col, kf, wq, wk, wv, head):
    cams, blk, width = mixed.shape
    picks = lists.shape[2]
    windows = (q, k, v, rq, rk)
    args = (vf, e, dm_t, mixed, row, col, kf, wq, wk, wv)
    return pl.pallas_call(
        functools.partial(own_grads_kernel, head, picks),
        name="own_grads",
        out_shape=pltpu.HBM((cams, blk, width), F32),
        grid_spec=pltpu.PrefetchScalarGridSpec(
            num_scalar_prefetch=2,
            grid=(cams,),
            in_specs=[per_camera(x) for x in windows] + [whole(x.shape) for x in args],
            out_specs=per_camera(mixed),
        ),
        compiler_params=params(6 + picks),
        cost_estimate=pl.CostEstimate(
            flops=20 * cams * blk * width * width, bytes_accessed=4 * e.size, transcendentals=0
        ),
    )(own, lists, *map(hbm, windows), *args)


def final_kernel(table_s, back_ref, rows_ref, clip_ref, dl_ref, gain_ref, out_ref, acc):
    tw, cams, nr, width = clip_ref.shape
    blk = tw * nr
    acc[...] = rows_ref[...]

    def add(i, carry):
        cam = table_s[i]

        @pl.when(cam >= 0)
        def _():
            acc[cam] += back_ref[i].astype(F32)

        return carry

    lax.fori_loop(0, back_ref.shape[0], add, 0)
    gain = gain_ref[...]

    def one(c, carry):
        x = clip_ref[:, c].reshape(blk, width).astype(F32)
        r = rms(x)
        hat = x * r
        g = acc[c] * gain
        d = dl_ref[:, c].reshape(blk, width) + r * (
            g - hat * jnp.mean(g * hat, axis=-1, keepdims=True)
        )
        out_ref[:, c] = d.astype(BF16).reshape(tw, nr, width)
        return carry

    lax.fori_loop(0, cams, one, 0)


def final(table, back, rows, clip_t, d_lifted, gain):
    args = (back, rows, clip_t, d_lifted, gain)
    return pl.pallas_call(
        final_kernel,
        name="final",
        out_shape=jax.ShapeDtypeStruct(clip_t.shape, BF16),
        grid_spec=pltpu.PrefetchScalarGridSpec(
            num_scalar_prefetch=1,
            grid=(1,),
            in_specs=[whole(x.shape) for x in args],
            out_specs=whole(clip_t.shape),
            scratch_shapes=[pltpu.VMEM(rows.shape, F32)],
        ),
        compiler_params=params(8),
    )(table, *args)


def exchange_edges(near, farther):
    size = lax.axis_size("cols")
    inner = [(i, i ^ 1) for i in range(size)]
    outer = [(i, i + 1 if i % 2 else i - 1) for i in range(1, size - 1)]
    return lax.ppermute(near, "cols", inner), lax.ppermute(farther, "cols", outer)


def local(
    clip_tokens,
    cotangent,
    gain_attn,
    w_query,
    w_key,
    w_value,
    w_out,
    gain_first,
    conv_first,
    gain_second,
    conv_second,
    matching,
    block_lists,
    counts,
):
    views, nr, tw, width = clip_tokens.shape
    head = width // HEADS
    n_cols = lax.axis_size("cols")
    own_index = lax.axis_index("cols").astype(jnp.int32)
    own = own_index.reshape(1)
    total = views * nr * tw
    blk = nr * tw
    flat = (total, width)
    slabs = (tw, views, nr, width)
    gain_attn = gain_attn.reshape(1, width)
    gain_first = gain_first.reshape(1, width)
    gain_second = gain_second.reshape(1, width)

    clip_t = jnp.transpose(clip_tokens, (2, 0, 1, 3))
    cot_t = jnp.transpose(cotangent, (2, 0, 1, 3))
    odd = own_index % 2
    last = (tw - 1) * (1 - odd)
    cot_near = lax.dynamic_index_in_dim(cot_t, last, 0, keepdims=False).reshape(-1, width)
    cot_far = lax.dynamic_index_in_dim(cot_t, tw - 1 - last, 0, keepdims=False).reshape(-1, width)

    rows, send = prep(n_cols, own, matching, block_lists, counts, clip_t, gain_attn)
    cot_near, cot_far = exchange_edges(cot_near, cot_far)
    arrived = lax.all_to_all(send, "cols", split_axis=0, concat_axis=0, tiled=True)
    rows, w_value, lists, live = lax.optimization_barrier((rows, w_value, block_lists, counts))
    w_value_t = w_value.T
    slots = jnp.arange(lists.shape[2], dtype=jnp.int32)
    asks = (lists == own_index) & (slots[None, None, :] < live[:, :, None])
    table = jnp.sum(jnp.where(asks, matching[:, None, None] + 1, 0), axis=(0, 2)) - 1
    q, k, v, vt, rq, rk = project(rows.reshape(flat), w_query, w_key, w_value, w_value_t, head, blk)
    q, k, v, rq, rk = (a.reshape(views, blk, width) for a in (q, k, v, rq, rk))
    arrived, q, k, v, vt, rq, rk = lax.optimization_barrier((arrived, q, k, v, vt, rq, rk))
    lifted, act_one, near, farther, kf, rf, e, row, col, mixed = attend(
        own, block_lists, counts, arrived, q, k, vt, clip_t, w_key, w_value_t, w_out, gain_first, head
    )
    edge = (views * nr, width)
    near, farther = exchange_edges(near.reshape(edge), farther.reshape(edge))
    (d_act_two,) = conv_call(
        "grad_two", grad_two_body, own, cot_t.reshape(flat), cot_near, cot_far, conv_second,
        (), (pltpu.VMEM(flat, F32),), nr, True,
    )
    flat_bf = pltpu.VMEM(flat, BF16)
    edge_bf = jax.ShapeDtypeStruct(edge, BF16)
    act_two, act_near, act_far, d_conv, d_near, d_far = conv_call(
        "conv_one", conv_one_body, own, act_one.reshape(flat), near, farther, conv_first,
        (d_act_two, gain_second),
        (flat_bf, edge_bf, edge_bf, flat_bf, edge_bf, edge_bf), nr, False,
    )
    d_near, d_far = exchange_edges(d_near, d_far)
    vf = far_values(arrived.reshape(-1, width), w_value)
    d_near, d_far, vf = lax.optimization_barrier((d_near, d_far, vf))
    vf = vf.reshape(arrived.shape)
    d_lifted, d_mixed = conv_call(
        "grad_one", grad_one_body, own, d_conv, d_near, d_far, conv_first,
        (lifted.reshape(flat), cot_t.reshape(flat), gain_first, w_out),
        (pltpu.VMEM(flat, F32), flat_bf), nr, True,
    )
    d_mixed, act_near, act_far = lax.optimization_barrier((d_mixed, act_near, act_far))
    d_mixed = d_mixed.reshape(slabs)
    act_near, act_far = exchange_edges(act_near, act_far)
    send_back = far_grads(
        own, block_lists, counts, n_cols, q, vf, e, d_mixed, mixed, row, col, kf, rf, w_key, w_value, head
    )
    send_back, act_near, act_far = lax.optimization_barrier((send_back, act_near, act_far))
    back = lax.all_to_all(send_back, "cols", split_axis=0, concat_axis=0, tiled=True)
    (result,) = conv_call(
        "conv_two", conv_two_body, own, act_two, act_near, act_far, conv_second,
        (lifted.reshape(flat),), (jax.ShapeDtypeStruct(flat, BF16),), nr, False,
    )
    d_rows = own_grads(
        own, block_lists, q, k, v, rq, rk, vf, e, d_mixed, mixed, row, col, kf, w_query, w_key, w_value, head
    )
    d_clip = final(table, back, d_rows, clip_t, d_lifted.reshape(slabs), gain_attn)
    return (
        jnp.transpose(result.reshape(slabs), (1, 2, 0, 3)),
        jnp.transpose(d_clip, (1, 2, 0, 3)),
    )


def solution(mesh):
    tiles = P("groups", None, "cols", None)
    in_specs = (tiles, tiles) + (P(),) * 12
    return jax.shard_map(
        local, mesh=mesh, in_specs=in_specs, out_specs=(tiles, tiles), check_vma=False
    )
```

```python
import functools

import jax
import jax.numpy as jnp
from jax import lax
from jax.experimental import pallas as pl
from jax.experimental.pallas import tpu as pltpu
from jax.sharding import PartitionSpec as P

HEADS = 8
EPSILON = 1e-06
F32 = jnp.float32
BF16 = jnp.bfloat16


def mm(a, b):
    return lax.dot_general(a, b, (((1,), (0,)), ((), ())), preferred_element_type=F32)


def mm_t(a, b):
    return lax.dot_general(a, b, (((1,), (1,)), ((), ())), preferred_element_type=F32)


def params(mib):
    return pltpu.CompilerParams(vmem_limit_bytes=mib * 1024 * 1024)


def hbm(x):
    return pltpu.with_memory_space_constraint(x, pltpu.HBM)


def vmem(x):
    return pltpu.with_memory_space_constraint(x, pltpu.VMEM)


def whole(shape):
    zeros = (0,) * len(shape)
    return pl.BlockSpec(shape, lambda *_: zeros)


def rms(values):
    return lax.rsqrt(jnp.mean(values * values, axis=-1, keepdims=True) + EPSILON)


def silu_parts(u):
    sigmoid = 0.5 + 0.5 * jnp.tanh(0.5 * u)
    return u * sigmoid, sigmoid * (1.0 + u * (1.0 - sigmoid))


def head_ones(width, head):
    rows = lax.broadcasted_iota(jnp.int32, (width, width), 0) // head
    cols = lax.broadcasted_iota(jnp.int32, (width, width), 1) // head
    return jnp.where(rows == cols, 1.0, 0.0).astype(BF16)


def head_mean(values, ones, head):
    width = ones.shape[0]
    parts = [
        mm(values[:, i : i + width].astype(BF16), ones)
        for i in range(0, values.shape[1], width)
    ]
    return jnp.concatenate(parts, axis=1) * (1.0 / head)


def prep_kernel(n_cols, own_s, match_s, lists_s, counts_s, clip_ref, gain_ref, rows_ref, send_ref, sem):
    cams = match_s.shape[0]
    picks = lists_s.shape[1]
    own = own_s[0]
    tw, _, nr, width = clip_ref.shape
    for c in range(cams):
        x = clip_ref[:, c].reshape(tw * nr, width).astype(F32)
        rows_ref[c] = (x * rms(x) * gain_ref[...]).astype(BF16)

    def copy(i):
        cam = jnp.int32(0)
        for c in range(cams):
            for s in range(picks):
                hit = (lists_s[c, s, i] == own) & (s < counts_s[c, i])
                cam = jnp.where(hit, match_s[c], cam)
        pltpu.make_async_copy(rows_ref.at[cam], send_ref.at[i], sem.at[i]).start()

    def start(i, carry):
        copy(i)
        return carry

    lax.fori_loop(0, n_cols, start, 0)

    def wait(i, carry):
        pltpu.make_async_copy(rows_ref.at[0], send_ref.at[i], sem.at[i]).wait()
        return carry

    lax.fori_loop(0, n_cols, wait, 0)


def prep(n_cols, own, matching, lists, counts, clip_t, gain):
    tw, cams, nr, width = clip_t.shape
    blk = tw * nr
    return pl.pallas_call(
        functools.partial(prep_kernel, n_cols),
        name="prep",
        out_shape=(
            jax.ShapeDtypeStruct((cams, blk, width), BF16),
            pltpu.HBM((n_cols, blk, width), BF16),
        ),
        grid_spec=pltpu.PrefetchScalarGridSpec(
            num_scalar_prefetch=4,
            grid=(1,),
            in_specs=[whole(clip_t.shape), whole((1, width))],
            out_specs=[whole((cams, blk, width)), pl.BlockSpec(memory_space=pltpu.HBM)],
            scratch_shapes=[pltpu.SemaphoreType.DMA((n_cols,))],
        ),
        compiler_params=params(8),
    )(own, hbm(matching), lists, hbm(counts), clip_t, hbm(gain))


def project_kernel(head, blk, rows_ref, wq_ref, wk_ref, wv_ref, wvt_ref, q_ref, k_ref, v_ref, vt_ref, rq_ref, rk_ref):
    rows = rows_ref[...]
    total, width = rows.shape
    half = width // 2
    ones = head_ones(half, head)
    for n in range(2):
        cols = slice(n * half, (n + 1) * half)
        for w_ref, o_ref, r_ref, scale in (
            (wq_ref, q_ref, rq_ref, head ** (-0.5)),
            (wk_ref, k_ref, rk_ref, 1.0),
        ):
            pre = mm(rows, w_ref[:, cols])
            r = lax.rsqrt(head_mean(pre * pre, ones, head) + EPSILON)
            o_ref[:, cols] = (pre * r * scale).astype(BF16)
            r_ref[:, cols] = r
        v_ref[:, cols] = mm(rows, wv_ref[:, cols]).astype(BF16)
    for c in range(total // blk):
        vt_ref[c] = mm_t(wvt_ref[...], rows_ref[c * blk : (c + 1) * blk]).astype(BF16)


def project(rows, wq, wk, wv, wvt, head, blk):
    total, width = rows.shape
    full = (total, width)
    return pl.pallas_call(
        functools.partial(project_kernel, head, blk),
        name="project",
        out_shape=(
            pltpu.HBM(full, BF16),
            pltpu.HBM(full, BF16),
            pltpu.HBM(full, BF16),
            pltpu.HBM((total // blk, width, blk), BF16),
            pltpu.HBM(full, F32),
            pltpu.HBM(full, F32),
        ),
        compiler_params=params(12),
        cost_estimate=pl.CostEstimate(
            flops=8 * total * width * width, bytes_accessed=20 * total * width, transcendentals=0
        ),
    )(rows, wq, wk, wv, wvt)


def pair_rows(x, low):
    zero = jnp.zeros_like(x)
    return jnp.concatenate([jnp.where(low, x, zero), jnp.where(low, zero, x)], axis=0)


PAD = 16


def attend_kernel(head, picks, own_s, lists_s, counts_s, *refs):
    (arrived_ref, q_ref, k_ref, vt_ref, clip_ref, wk_ref, wvt_ref, wo_ref, gain_ref,
     lifted_ref, act_ref, near_ref, farther_ref, kf_ref, rf_ref, e_ref, row_ref, col_ref,
     mixed_ref, kcat, vcat) = refs
    c = pl.program_id(0)
    near_ref, farther_ref, kf_ref, rf_ref, e_ref, row_ref, col_ref = (
        r.at[pl.ds(c, 1)] for r in (near_ref, farther_ref, kf_ref, rf_ref, e_ref, row_ref, col_ref)
    )
    lifted_ref, act_ref = (r.at[:, pl.ds(c, 1)] for r in (lifted_ref, act_ref))
    own = own_s[0]
    count = counts_s[c, own]
    blk, width = q_ref.shape[1:]
    half = width // 2
    keys = (1 + picks) * blk
    pairs = width // 128

    @pl.when(c == 0)
    def _():
        vcat[:, 128:] = jnp.ones((pairs, PAD, keys), BF16)

    ones_h = head_ones(half, head)
    rows = jnp.concatenate([arrived_ref[lists_s[c, s, own]] for s in range(picks)], axis=0)
    kcat[:blk] = k_ref[0]
    vcat[:, :128, :blk] = vt_ref[0].reshape(pairs, 128, blk)
    vcat[:, :128, blk:] = mm_t(wvt_ref[...], rows).astype(BF16).reshape(pairs, 128, keys - blk)
    for n in range(2):
        cols = slice(n * half, (n + 1) * half)
        pre = mm(rows, wk_ref[:, cols])
        r = lax.rsqrt(head_mean(pre * pre, ones_h, head) + EPSILON)
        k = (pre * r).astype(BF16)
        kcat[blk:, cols] = k
        kf_ref[0, :, cols] = k
        rf_ref[0, :, cols] = r
    low = lax.broadcasted_iota(jnp.int32, (blk, 128), 1) < head
    live = [jnp.where(s < count, 1.0, 0.0) for s in range(picks)]
    mixed = []
    inverses = []
    for p in range(pairs):
        cols = slice(128 * p, 128 * (p + 1))
        q2 = pair_rows(q_ref[0, :, cols], low)
        grown = jnp.exp(mm_t(kcat[:, cols], q2))
        e_ref[0, p, :blk] = grown[:blk].astype(BF16)
        for s in range(picks):
            part = slice((1 + s) * blk, (2 + s) * blk)
            e_ref[0, p, part] = (grown[part] * live[s]).astype(BF16)
        out = mm(vcat[p], e_ref[0, p])
        inverse = 1.0 / out[128:129]
        inverses += [inverse[:, :blk], inverse[:, blk:]]
        out = out[:128] * inverse
        out = jnp.concatenate([out[:head, :blk], out[head:, blk:]], axis=0)
        mixed.append(jnp.transpose(out).astype(BF16))
    inverses = jnp.concatenate(inverses, axis=0)
    row_ref[0] = inverses
    spread = jnp.concatenate([inverses, jnp.zeros((128 - HEADS, blk), F32)], axis=0)
    col_ref[0] = jnp.transpose(spread)
    mixed = jnp.concatenate(mixed, axis=1)
    mixed_ref[c] = mixed
    clip = clip_ref[:, 0].reshape(blk, width).astype(F32)
    lifted = (clip + mm(mixed, wo_ref[...])).astype(BF16)
    lifted_f = lifted.astype(F32)
    act, _ = silu_parts(lifted_f * rms(lifted_f) * gain_ref[...])
    slabs = (clip_ref.shape[0], clip_ref.shape[2], width)
    lifted_ref[:, 0] = lifted.reshape(slabs)
    act = act.astype(BF16).reshape(slabs)
    act_ref[:, 0] = act
    even = lax.rem(own, 2) == 0
    near_ref[0] = jnp.where(even, act[-1], act[0])
    farther_ref[0] = jnp.where(even, act[0], act[-1])


def per_camera(x):
    zeros = (0,) * (x.ndim - 1)
    return pl.BlockSpec((1,) + x.shape[1:], lambda c, *_: (c,) + zeros)


def attend(own, lists, counts, arrived, q, k, vt, clip_t, wk, wvt, wo, gain, head):
    tw, cams, nr, width = clip_t.shape
    blk = tw * nr
    picks = lists.shape[1]
    keys = (1 + picks) * blk
    pairs = width // 128
    slab = pl.BlockSpec((tw, 1, nr, width), lambda c, *_: (0, c, 0, 0))
    outs = (
        pltpu.VMEM(clip_t.shape, BF16),
        pltpu.VMEM(clip_t.shape, BF16),
        jax.ShapeDtypeStruct((cams, nr, width), BF16),
        jax.ShapeDtypeStruct((cams, nr, width), BF16),
        pltpu.VMEM((cams, picks * blk, width), BF16),
        pltpu.VMEM((cams, picks * blk, width), F32),
        pltpu.VMEM((cams, pairs, keys, 2 * blk), BF16),
        pltpu.VMEM((cams, HEADS, blk), F32),
        pltpu.VMEM((cams, blk, 128), F32),
        pltpu.VMEM((cams, blk, width), BF16),
    )
    weights = (wk, hbm(wvt), hbm(wo), gain)
    return pl.pallas_call(
        functools.partial(attend_kernel, head, picks),
        name="attend",
        out_shape=outs,
        grid_spec=pltpu.PrefetchScalarGridSpec(
            num_scalar_prefetch=3,
            grid=(cams,),
            in_specs=[whole(arrived.shape), per_camera(q), per_camera(k), per_camera(vt), slab]
            + [whole(x.shape) for x in weights],
            out_specs=[whole(x.shape) for x in outs],
            scratch_shapes=[
                pltpu.VMEM((keys, width), BF16),
                pltpu.VMEM((pairs, 128 + PAD, keys), BF16),
            ],
        ),
        compiler_params=params(10 + picks),
    )(own, lists, counts, arrived, hbm(q), hbm(k), hbm(vt), hbm(clip_t), *weights)


def far_values_kernel(arrived_ref, w_ref, out_ref):
    out_ref[...] = mm(arrived_ref[...], w_ref[...]).astype(BF16)


def far_values(arrived, w):
    total, width = arrived.shape
    return pl.pallas_call(
        far_values_kernel,
        name="far_values",
        out_shape=pltpu.VMEM((total, width), BF16),
        grid=(total // 512,),
        in_specs=[pl.BlockSpec((512, width), lambda i: (i, 0)), whole(w.shape)],
        out_specs=pl.BlockSpec((512, width), lambda i: (i, 0)),
        compiler_params=params(6),
        cost_estimate=pl.CostEstimate(
            flops=2 * total * width * width, bytes_accessed=4 * total * width, transcendentals=0
        ),
    )(arrived, w)


def fill_windows(own_s, act_ref, near_ref, farther_ref, x_ref, edge, total):
    width = act_ref.shape[1]
    even = lax.rem(own_s[0], 2) == 0
    near = near_ref[...]
    farther = farther_ref[...]
    x_ref[:edge, :width] = jnp.where(even, farther, near)
    x_ref[edge:, :width] = act_ref[: total - edge]
    x_ref[:, width : 2 * width] = act_ref[...]
    x_ref[: total - edge, 2 * width :] = act_ref[edge:]
    x_ref[total - edge :, 2 * width :] = jnp.where(even, near, farther)


def conv_step(w_ref, x_ref, y_ref, step, transposed):
    width = w_ref.shape[2]
    if transposed:
        total = None
        for q in range(3):
            cols = slice((2 - q) * width, (3 - q) * width)
            part = mm_t(x_ref[:, cols], w_ref[0, q])
            total = part if total is None else total + part
        y_ref[step] = total
    else:
        y_ref[step] = mm(x_ref[...], w_ref[0].reshape(3 * width, width))


def conv_rows(y_ref, start, size, nr, transposed):
    rows = pl.ds(start, size)
    before, centre, after = (2, 1, 0) if transposed else (0, 1, 2)
    place = lax.broadcasted_iota(jnp.int32, (size, 1), 0) % nr
    up = pltpu.roll(y_ref[before, rows, :], 1, 0)
    down = pltpu.roll(y_ref[after, rows, :], size - 1, 0)
    return (
        jnp.where(place == 0, 0.0, up)
        + y_ref[centre, rows, :]
        + jnp.where(place == nr - 1, 0.0, down)
    )


def conv_kernel(body, n_extra, transposed, nr, own_s, act_ref, near_ref, farther_ref, w_ref, *refs):
    extra, outs, (x_ref, y_ref) = refs[:n_extra], refs[n_extra:-2], refs[-2:]
    step = pl.program_id(0)
    total = act_ref.shape[0]
    edge = near_ref.shape[0]

    @pl.when(step == 0)
    def _():
        fill_windows(own_s, act_ref, near_ref, farther_ref, x_ref, edge, total)

    conv_step(w_ref, x_ref, y_ref, step, transposed)

    @pl.when(step == 2)
    def _():
        even = lax.rem(own_s[0], 2) == 0
        body(lambda start, size: conv_rows(y_ref, start, size, nr, transposed), even, edge, extra, outs)


def conv_call(name, body, own, act, near, farther, weights, extra, outs, nr, transposed):
    total, width = act.shape
    edge = near.shape[0]
    return pl.pallas_call(
        functools.partial(conv_kernel, body, len(extra), transposed, nr),
        name=name,
        out_shape=outs,
        grid_spec=pltpu.PrefetchScalarGridSpec(
            num_scalar_prefetch=1,
            grid=(3,),
            in_specs=[
                whole((total, width)),
                whole((edge, width)),
                whole((edge, width)),
                pl.BlockSpec((1, 3, width, width), lambda p, *_: (p, 0, 0, 0)),
            ]
            + [whole(e.shape) for e in extra],
            out_specs=[whole(o.shape) for o in outs],
            scratch_shapes=[
                pltpu.VMEM((total, 3 * width), BF16),
                pltpu.VMEM((3, total, width), F32),
            ],
        ),
        compiler_params=params(14),
        cost_estimate=pl.CostEstimate(
            flops=18 * total * width * width, bytes_accessed=18 * width * width, transcendentals=0
        ),
    )(own, act, near, farther, weights, *extra)


CHUNK = 128


def chunks(total, fn):
    def step(i, carry):
        fn(pl.multiple_of(i * CHUNK, CHUNK))
        return carry

    lax.fori_loop(0, total // CHUNK, step, 0)


def grad_two_body(rows_of, even, edge, extra, outs):
    (out,) = outs

    def one(start):
        out[pl.ds(start, CHUNK), :] = rows_of(start, CHUNK)

    chunks(out.shape[0], one)


def copy_edges(even, edge, full, near, farther):
    total = full.shape[0]
    first = full[:edge]
    last = full[total - edge :]
    near[...] = jnp.where(even, last, first)
    farther[...] = jnp.where(even, first, last)


def conv_one_body(rows_of, even, edge, extra, outs):
    grad_ref, gain_ref = extra
    act_ref, act_near, act_far, d_ref, d_near, d_far = outs
    total = act_ref.shape[0]
    gain = gain_ref[...]

    def one(start):
        rows = pl.ds(start, CHUNK)
        conv = rows_of(start, CHUNK)
        r = rms(conv)
        hat = conv * r
        act, slope = silu_parts(hat * gain)
        act_ref[rows, :] = act.astype(BF16)
        g = grad_ref[rows, :] * slope * gain
        d_ref[rows, :] = (r * (g - hat * jnp.mean(g * hat, axis=-1, keepdims=True))).astype(BF16)

    chunks(total, one)
    copy_edges(even, edge, act_ref, act_near, act_far)
    copy_edges(even, edge, d_ref, d_near, d_far)


def conv_two_body(rows_of, even, edge, extra, outs):
    (lifted_ref,) = extra
    (out,) = outs

    def one(start):
        rows = pl.ds(start, CHUNK)
        out[rows, :] = (lifted_ref[rows, :].astype(F32) + rows_of(start, CHUNK)).astype(BF16)

    chunks(out.shape[0], one)


def grad_main_kernel(edge, act_ref, w_ref, y_ref, x_ref):
    step = pl.program_id(0)
    total, width = act_ref.shape

    @pl.when(step == 0)
    def _():
        blank = jnp.zeros((edge, width), BF16)
        x_ref[:edge, :width] = blank
        x_ref[edge:, :width] = act_ref[: total - edge]
        x_ref[:, width : 2 * width] = act_ref[...]
        x_ref[: total - edge, 2 * width :] = act_ref[edge:]
        x_ref[total - edge :, 2 * width :] = blank

    conv_step(w_ref, x_ref, y_ref, step, True)


def grad_main(act, weights, edge):
    total, width = act.shape
    return pl.pallas_call(
        functools.partial(grad_main_kernel, edge),
        name="grad_main",
        out_shape=pltpu.VMEM((3, total, width), F32),
        grid_spec=pltpu.PrefetchScalarGridSpec(
            num_scalar_prefetch=0,
            grid=(3,),
            in_specs=[
                whole((total, width)),
                pl.BlockSpec((1, 3, width, width), lambda p, *_: (p, 0, 0, 0)),
            ],
            out_specs=whole((3, total, width)),
            scratch_shapes=[pltpu.VMEM((total, 3 * width), BF16)],
        ),
        compiler_params=params(14),
        cost_estimate=pl.CostEstimate(
            flops=18 * total * width * width, bytes_accessed=18 * width * width, transcendentals=0
        ),
    )(act, weights)


def grad_tail_kernel(nr, own_s, near_ref, farther_ref, w_ref, y_ref, lifted_ref, cot_ref, gain_ref,
                     wo_ref, d_lifted_ref, d_mixed_ref, z_ref):
    edge = near_ref.shape[0]
    total = d_lifted_ref.shape[0]
    even = lax.rem(own_s[0], 2) == 0
    near = near_ref[...]
    farther = farther_ref[...]
    left = jnp.where(even, farther, near)
    right = jnp.where(even, near, farther)
    for p in range(3):
        z_ref[0, p] = mm_t(left, w_ref[p, 2])
        z_ref[1, p] = mm_t(right, w_ref[p, 0])
    gain = gain_ref[...]
    split = (edge // nr + 1) // 2 * nr
    for start in range(0, total, edge):
        for first, last in ((0, split), (split, edge)):
            size = last - first
            rows = slice(start + first, start + last)
            taps = []
            for p in range(3):
                tap = y_ref[p, rows]
                if start == 0:
                    tap = tap + z_ref[0, p, first:last]
                if start == total - edge:
                    tap = tap + z_ref[1, p, first:last]
                taps.append(tap)
            place = lax.broadcasted_iota(jnp.int32, (size, 1), 0) % nr
            conv = (
                jnp.where(place == 0, 0.0, pltpu.roll(taps[2], 1, 0))
                + taps[1]
                + jnp.where(place == nr - 1, 0.0, pltpu.roll(taps[0], size - 1, 0))
            )
            lifted = lifted_ref[rows].astype(F32)
            r = rms(lifted)
            hat = lifted * r
            _, slope = silu_parts(hat * gain)
            g = conv * slope * gain
            back = r * (g - hat * jnp.mean(g * hat, axis=-1, keepdims=True))
            d_lifted_ref[rows] = cot_ref[rows].astype(F32) + back
    d_mixed_ref[...] = mm_t(d_lifted_ref[...].astype(BF16), wo_ref[...]).astype(BF16)


def grad_tail(own, near, farther, weights, y, lifted, cot, gain, wo, nr):
    args = (near, farther, weights, y, lifted, cot, gain, wo)
    edge, width = near.shape
    outs = (pltpu.VMEM(lifted.shape, F32), pltpu.VMEM(lifted.shape, BF16))
    return pl.pallas_call(
        functools.partial(grad_tail_kernel, nr),
        name="grad_tail",
        out_shape=outs,
        grid_spec=pltpu.PrefetchScalarGridSpec(
            num_scalar_prefetch=1,
            grid=(1,),
            in_specs=[whole(x.shape) for x in args],
            out_specs=[whole(x.shape) for x in outs],
            scratch_shapes=[pltpu.VMEM((2, 3, edge, width), F32)],
        ),
        compiler_params=params(14),
    )(own, *args)


def head_norm_back(grad, hat, r, ones, head):
    hat = hat.astype(F32)
    return r * (grad - hat * head_mean(grad * hat, ones, head))


def drift_rows(head, dm, mixed, row):
    width = dm.shape[1]
    lanes = lax.broadcasted_iota(jnp.int32, (PAD, width), 1) // head
    picked = (lanes == lax.broadcasted_iota(jnp.int32, (PAD, width), 0)).astype(BF16)
    product = (dm.astype(F32) * mixed.astype(F32)).astype(BF16)
    return mm_t(picked, product)[:HEADS] * row


def pair_queries(p, q, dm, col, drift, low):
    cols = slice(128 * p, 128 * (p + 1))
    spread = jnp.where(low, col[:, 2 * p : 2 * p + 1], col[:, 2 * p + 1 : 2 * p + 2])
    q2 = pair_rows(q[:, cols], low)
    dm2 = pair_rows((dm[:, cols].astype(F32) * spread).astype(BF16), low)
    shift = jnp.concatenate([drift[2 * p : 2 * p + 1], drift[2 * p + 1 : 2 * p + 2]], axis=1)
    return q2, dm2, shift


def far_grads_kernel(head, picks, own_s, lists_s, counts_s, q_ref, vf_ref, e_ref, dm_ref, mixed_ref,
                     row_ref, col_ref, kf_ref, rf_ref, wk_ref, wv_ref, send_ref, kgrad, vgrad, shares, sems):
    c = pl.program_id(0)
    own = own_s[0]
    cams, blk, width = mixed_ref.shape
    low = lax.broadcasted_iota(jnp.int32, (blk, 128), 1) < head
    q = q_ref[0]
    dm = dm_ref[:, c].reshape(blk, width)
    drift = drift_rows(head, dm, mixed_ref[c], row_ref[c])
    col = col_ref[c]
    for p in range(width // 128):
        cols = slice(128 * p, 128 * (p + 1))
        q2, dm2, shift = pair_queries(p, q, dm, col, drift, low)
        far_v = jnp.concatenate([vf_ref[lists_s[c, s, own], :, cols] for s in range(picks)], axis=0)
        e = e_ref[c, p, blk:]
        d_scaled = (e.astype(F32) * (mm_t(far_v, dm2) - shift)).astype(BF16)
        kgrad[c, :, cols] = mm(d_scaled, q2)
        vgrad[c, :, cols] = mm(e, dm2).astype(BF16)

    @pl.when(c == cams - 1)
    def _():
        ones_h = head_ones(width // 2, head)

        def back(i, carry):
            grad = head_norm_back(kgrad[i], kf_ref[i], rf_ref[i], ones_h, head)
            shares[i] = grad.astype(BF16)
            return carry

        lax.fori_loop(0, cams, back, 0)
        shape = (picks * blk, width)
        for first, last in ((0, (cams + 1) // 2), ((cams + 1) // 2, cams)):
            count = last - first
            share = mm_t(shares[first:last].reshape(count * shape[0], width), wk_ref[...])
            share = share + mm_t(vgrad[first:last].reshape(count * shape[0], width), wv_ref[...])
            shares[first:last] = share.astype(BF16).reshape((count,) + shape)
            for i in range(first, last):
                for s in range(picks):
                    pltpu.make_async_copy(
                        shares.at[i, pl.ds(s * blk, blk)],
                        send_ref.at[lists_s[i, s, own]],
                        sems.at[i, s],
                    ).start()
        for i in range(cams):
            for s in range(picks):
                pltpu.make_async_copy(
                    shares.at[i, pl.ds(s * blk, blk)], send_ref.at[0], sems.at[i, s]
                ).wait()


def far_grads(own, lists, counts, n_cols, q, vf, e, dm_t, mixed, row, col, kf, rf, wk, wv, head):
    cams, blk, width = mixed.shape
    picks = lists.shape[1]
    args = (vf, e, dm_t, mixed, row, col, kf, rf, wk, wv)
    return pl.pallas_call(
        functools.partial(far_grads_kernel, head, picks),
        name="far_grads",
        out_shape=pltpu.HBM((n_cols, blk, width), BF16),
        grid_spec=pltpu.PrefetchScalarGridSpec(
            num_scalar_prefetch=3,
            grid=(cams,),
            in_specs=[per_camera(q)] + [whole(x.shape) for x in args],
            out_specs=pl.BlockSpec(memory_space=pltpu.HBM),
            scratch_shapes=[
                pltpu.VMEM((cams, picks * blk, width), F32),
                pltpu.VMEM((cams, picks * blk, width), BF16),
                pltpu.VMEM((cams, picks * blk, width), BF16),
                pltpu.SemaphoreType.DMA((cams, picks)),
            ],
        ),
        compiler_params=params(4 + 6 * picks),
    )(own, lists, counts, hbm(q), *args)


def own_grads_kernel(head, picks, own_s, lists_s, q_ref, k_ref, v_ref, rq_ref, rk_ref, vf_ref, e_ref, dm_ref,
                     mixed_ref, row_ref, col_ref, kf_ref, wq_ref, wk_ref, wv_ref, out_ref):
    c = pl.program_id(0)
    own = own_s[0]
    cams, blk, width = mixed_ref.shape
    low = lax.broadcasted_iota(jnp.int32, (blk, 128), 1) < head
    ones_h = head_ones(width // 2, head)
    scale = head ** (-0.5)
    q = q_ref[0]
    dm = dm_ref[:, c].reshape(blk, width)
    drift = drift_rows(head, dm, mixed_ref[c], row_ref[c])
    col = col_ref[c]
    listed = [lists_s[c, s, own] for s in range(picks)]
    dq, dk, dv = [], [], []
    for p in range(width // 128):
        cols = slice(128 * p, 128 * (p + 1))
        q2, dm2, shift = pair_queries(p, q, dm, col, drift, low)
        all_v = jnp.concatenate([v_ref[0, :, cols]] + [vf_ref[i, :, cols] for i in listed], axis=0)
        all_k = jnp.concatenate([k_ref[0, :, cols], kf_ref[c, :, cols]], axis=0)
        e = e_ref[c, p]
        d_scaled = (e.astype(F32) * (mm_t(all_v, dm2) - shift)).astype(BF16)
        dk.append(mm(d_scaled[:blk], q2))
        dv.append(mm(e[:blk], dm2).astype(BF16))
        both = mm(jnp.transpose(d_scaled), all_k)
        dq.append(jnp.where(low, both[:blk], both[blk:]) * scale)
    dq, dk, dv = (jnp.concatenate(parts, axis=1) for parts in (dq, dk, dv))
    q_hat = q.astype(F32) * (1.0 / scale)
    dq = head_norm_back(dq, q_hat, rq_ref[0], ones_h, head).astype(BF16)
    dk = head_norm_back(dk, k_ref[0], rk_ref[0], ones_h, head).astype(BF16)
    out_ref[0] = mm_t(dq, wq_ref[...]) + mm_t(dk, wk_ref[...]) + mm_t(dv, wv_ref[...])


def own_grads(own, lists, q, k, v, rq, rk, vf, e, dm_t, mixed, row, col, kf, wq, wk, wv, head):
    cams, blk, width = mixed.shape
    picks = lists.shape[1]
    windows = (q, k, v, rq, rk)
    args = (vf, e, dm_t, mixed, row, col, kf, wq, wk, wv)
    return pl.pallas_call(
        functools.partial(own_grads_kernel, head, picks),
        name="own_grads",
        out_shape=pltpu.HBM((cams, blk, width), F32),
        grid_spec=pltpu.PrefetchScalarGridSpec(
            num_scalar_prefetch=2,
            grid=(cams,),
            in_specs=[per_camera(x) for x in windows] + [whole(x.shape) for x in args],
            out_specs=per_camera(mixed),
        ),
        compiler_params=params(6 + picks),
        cost_estimate=pl.CostEstimate(
            flops=20 * cams * blk * width * width, bytes_accessed=4 * e.size, transcendentals=0
        ),
    )(own, lists, *map(hbm, windows), *args)


def final_kernel(table_s, back_ref, rows_ref, clip_ref, dl_ref, gain_ref, out_ref, acc):
    tw, cams, nr, width = clip_ref.shape
    blk = tw * nr
    acc[...] = rows_ref[...]

    def add(i, carry):
        cam = table_s[i]

        @pl.when(cam >= 0)
        def _():
            acc[cam] += back_ref[i].astype(F32)

        return carry

    lax.fori_loop(0, back_ref.shape[0], add, 0)
    gain = gain_ref[...]

    def one(c, carry):
        x = clip_ref[:, c].reshape(blk, width).astype(F32)
        r = rms(x)
        hat = x * r
        g = acc[c] * gain
        d = dl_ref[:, c].reshape(blk, width) + r * (
            g - hat * jnp.mean(g * hat, axis=-1, keepdims=True)
        )
        out_ref[:, c] = d.astype(BF16).reshape(tw, nr, width)
        return carry

    lax.fori_loop(0, cams, one, 0)


def final(table, back, rows, clip_t, d_lifted, gain):
    args = (back, rows, clip_t, d_lifted, gain)
    return pl.pallas_call(
        final_kernel,
        name="final",
        out_shape=jax.ShapeDtypeStruct(clip_t.shape, BF16),
        grid_spec=pltpu.PrefetchScalarGridSpec(
            num_scalar_prefetch=1,
            grid=(1,),
            in_specs=[whole(x.shape) for x in args],
            out_specs=whole(clip_t.shape),
            scratch_shapes=[pltpu.VMEM(rows.shape, F32)],
        ),
        compiler_params=params(8),
    )(table, *args)


def exchange_edges(near, farther):
    size = lax.axis_size("cols")
    inner = [(i, i ^ 1) for i in range(size)]
    outer = [(i, i + 1 if i % 2 else i - 1) for i in range(1, size - 1)]
    return lax.ppermute(near, "cols", inner), lax.ppermute(farther, "cols", outer)


def local(
    clip_tokens,
    cotangent,
    gain_attn,
    w_query,
    w_key,
    w_value,
    w_out,
    gain_first,
    conv_first,
    gain_second,
    conv_second,
    matching,
    block_lists,
    counts,
):
    views, nr, tw, width = clip_tokens.shape
    head = width // HEADS
    n_cols = lax.axis_size("cols")
    own_index = lax.axis_index("cols").astype(jnp.int32)
    own = own_index.reshape(1)
    total = views * nr * tw
    blk = nr * tw
    flat = (total, width)
    slabs = (tw, views, nr, width)
    block_lists = jnp.transpose(block_lists, (0, 2, 1))
    gain_attn = gain_attn.reshape(1, width)
    gain_first = gain_first.reshape(1, width)
    gain_second = gain_second.reshape(1, width)

    clip_t = jnp.transpose(clip_tokens, (2, 0, 1, 3))
    cot_t = jnp.transpose(cotangent, (2, 0, 1, 3))
    odd = own_index % 2
    last = (tw - 1) * (1 - odd)
    cot_near = lax.dynamic_index_in_dim(cot_t, last, 0, keepdims=False).reshape(-1, width)
    cot_far = lax.dynamic_index_in_dim(cot_t, tw - 1 - last, 0, keepdims=False).reshape(-1, width)

    rows, send = prep(n_cols, own, matching, block_lists, counts, clip_t, gain_attn)
    cot_near, cot_far = exchange_edges(cot_near, cot_far)
    arrived = lax.all_to_all(send, "cols", split_axis=0, concat_axis=0, tiled=True)
    rows, w_value, lists, live = lax.optimization_barrier((rows, w_value, block_lists, counts))
    w_value_t = w_value.T
    slots = jnp.arange(lists.shape[1], dtype=jnp.int32)
    asks = (lists == own_index) & (slots[None, :, None] < live[:, None, :])
    table = jnp.sum(jnp.where(asks, matching[:, None, None] + 1, 0), axis=(0, 1)) - 1
    q, k, v, vt, rq, rk = project(rows.reshape(flat), w_query, w_key, w_value, w_value_t, head, blk)
    q, k, v, rq, rk = (a.reshape(views, blk, width) for a in (q, k, v, rq, rk))
    arrived, q, k, v, vt, rq, rk = lax.optimization_barrier((arrived, q, k, v, vt, rq, rk))
    lifted, act_one, near, farther, kf, rf, e, row, col, mixed = attend(
        own, block_lists, counts, arrived, q, k, vt, clip_t, w_key, w_value_t, w_out, gain_first, head
    )
    edge = (views * nr, width)
    near, farther = exchange_edges(near.reshape(edge), farther.reshape(edge))
    (d_act_two,) = conv_call(
        "grad_two", grad_two_body, own, cot_t.reshape(flat), cot_near, cot_far, conv_second,
        (), (pltpu.VMEM(flat, F32),), nr, True,
    )
    flat_bf = pltpu.VMEM(flat, BF16)
    edge_bf = jax.ShapeDtypeStruct(edge, BF16)
    act_two, act_near, act_far, d_conv, d_near, d_far = conv_call(
        "conv_one", conv_one_body, own, act_one.reshape(flat), near, farther, conv_first,
        (d_act_two, gain_second),
        (flat_bf, edge_bf, edge_bf, flat_bf, edge_bf, edge_bf), nr, False,
    )
    d_near, d_far = exchange_edges(d_near, d_far)
    vf = far_values(arrived.reshape(-1, width), w_value)
    y_grad = grad_main(d_conv, conv_first, views * nr)
    d_near, d_far, vf, y_grad = lax.optimization_barrier((d_near, d_far, vf, y_grad))
    vf = vf.reshape(arrived.shape)
    d_lifted, d_mixed = grad_tail(
        own, d_near, d_far, conv_first, y_grad, lifted.reshape(flat), cot_t.reshape(flat), gain_first, w_out, nr
    )
    d_mixed, act_near, act_far = lax.optimization_barrier((d_mixed, act_near, act_far))
    d_mixed = d_mixed.reshape(slabs)
    act_near, act_far = exchange_edges(act_near, act_far)
    send_back = far_grads(
        own, block_lists, counts, n_cols, q, vf, e, d_mixed, mixed, row, col, kf, rf, w_key, w_value, head
    )
    send_back, act_near, act_far = lax.optimization_barrier((send_back, act_near, act_far))
    back = lax.all_to_all(send_back, "cols", split_axis=0, concat_axis=0, tiled=True)
    (result,) = conv_call(
        "conv_two", conv_two_body, own, act_two, act_near, act_far, conv_second,
        (lifted.reshape(flat),), (jax.ShapeDtypeStruct(flat, BF16),), nr, False,
    )
    d_rows = own_grads(
        own, block_lists, q, k, v, rq, rk, vf, e, d_mixed, mixed, row, col, kf, w_query, w_key, w_value, head
    )
    d_clip = final(table, back, d_rows, clip_t, d_lifted.reshape(slabs), gain_attn)
    return (
        jnp.transpose(result.reshape(slabs), (1, 2, 0, 3)),
        jnp.transpose(d_clip, (1, 2, 0, 3)),
    )


def solution(mesh):
    tiles = P("groups", None, "cols", None)
    in_specs = (tiles, tiles) + (P(),) * 12
    return jax.shard_map(
        local, mesh=mesh, in_specs=in_specs, out_specs=(tiles, tiles), check_vma=False
    )
```

```python
import functools

import jax
import jax.numpy as jnp
from jax import lax
from jax.experimental import pallas as pl
from jax.experimental.pallas import tpu as pltpu
from jax.sharding import PartitionSpec as P

HEADS = 8
EPSILON = 1e-06
F32 = jnp.float32
BF16 = jnp.bfloat16


def mm(a, b):
    return lax.dot_general(a, b, (((1,), (0,)), ((), ())), preferred_element_type=F32)


def mm_t(a, b):
    return lax.dot_general(a, b, (((1,), (1,)), ((), ())), preferred_element_type=F32)


def params(mib):
    return pltpu.CompilerParams(vmem_limit_bytes=mib * 1024 * 1024)


def hbm(x):
    return pltpu.with_memory_space_constraint(x, pltpu.HBM)


def vmem(x):
    return pltpu.with_memory_space_constraint(x, pltpu.VMEM)


def whole(shape):
    zeros = (0,) * len(shape)
    return pl.BlockSpec(shape, lambda *_: zeros)


def rms(values):
    return lax.rsqrt(jnp.mean(values * values, axis=-1, keepdims=True) + EPSILON)


def silu_parts(u):
    sigmoid = 0.5 + 0.5 * jnp.tanh(0.5 * u)
    return u * sigmoid, sigmoid * (1.0 + u * (1.0 - sigmoid))


def head_ones(width, head):
    rows = lax.broadcasted_iota(jnp.int32, (width, width), 0) // head
    cols = lax.broadcasted_iota(jnp.int32, (width, width), 1) // head
    return jnp.where(rows == cols, 1.0, 0.0).astype(BF16)


def head_mean(values, ones, head):
    width = ones.shape[0]
    parts = [
        mm(values[:, i : i + width].astype(BF16), ones)
        for i in range(0, values.shape[1], width)
    ]
    return jnp.concatenate(parts, axis=1) * (1.0 / head)


def prep_kernel(n_cols, own_s, match_s, lists_s, counts_s, clip_ref, gain_ref, rows_ref, send_ref, sem):
    cams = match_s.shape[0]
    picks = lists_s.shape[1]
    own = own_s[0]
    tw, _, nr, width = clip_ref.shape
    for c in range(cams):
        x = clip_ref[:, c].reshape(tw * nr, width).astype(F32)
        rows_ref[c] = (x * rms(x) * gain_ref[...]).astype(BF16)

    def copy(i):
        cam = jnp.int32(0)
        for c in range(cams):
            for s in range(picks):
                hit = (lists_s[c, s, i] == own) & (s < counts_s[c, i])
                cam = jnp.where(hit, match_s[c], cam)
        pltpu.make_async_copy(rows_ref.at[cam], send_ref.at[i], sem.at[i]).start()

    def start(i, carry):
        copy(i)
        return carry

    lax.fori_loop(0, n_cols, start, 0)

    def wait(i, carry):
        pltpu.make_async_copy(rows_ref.at[0], send_ref.at[i], sem.at[i]).wait()
        return carry

    lax.fori_loop(0, n_cols, wait, 0)


def prep(n_cols, own, matching, lists, counts, clip_t, gain):
    tw, cams, nr, width = clip_t.shape
    blk = tw * nr
    return pl.pallas_call(
        functools.partial(prep_kernel, n_cols),
        name="prep",
        out_shape=(
            jax.ShapeDtypeStruct((cams, blk, width), BF16),
            pltpu.HBM((n_cols, blk, width), BF16),
        ),
        grid_spec=pltpu.PrefetchScalarGridSpec(
            num_scalar_prefetch=4,
            grid=(1,),
            in_specs=[whole(clip_t.shape), whole((1, width))],
            out_specs=[whole((cams, blk, width)), pl.BlockSpec(memory_space=pltpu.HBM)],
            scratch_shapes=[pltpu.SemaphoreType.DMA((n_cols,))],
        ),
        compiler_params=params(8),
    )(own, hbm(matching), lists, hbm(counts), clip_t, hbm(gain))


def project_kernel(head, blk, rows_ref, wq_ref, wk_ref, wv_ref, wvt_ref, q_ref, k_ref, v_ref, vt_ref, rq_ref, rk_ref):
    rows = rows_ref[...]
    total, width = rows.shape
    half = width // 2
    ones = head_ones(half, head)
    for n in range(2):
        cols = slice(n * half, (n + 1) * half)
        for w_ref, o_ref, r_ref, scale in (
            (wq_ref, q_ref, rq_ref, head ** (-0.5)),
            (wk_ref, k_ref, rk_ref, 1.0),
        ):
            pre = mm(rows, w_ref[:, cols])
            r = lax.rsqrt(head_mean(pre * pre, ones, head) + EPSILON)
            o_ref[:, cols] = (pre * r * scale).astype(BF16)
            r_ref[:, cols] = r
        v_ref[:, cols] = mm(rows, wv_ref[:, cols]).astype(BF16)
    for c in range(total // blk):
        vt_ref[c] = mm_t(wvt_ref[...], rows_ref[c * blk : (c + 1) * blk]).astype(BF16)


def project(rows, wq, wk, wv, wvt, head, blk):
    total, width = rows.shape
    full = (total, width)
    return pl.pallas_call(
        functools.partial(project_kernel, head, blk),
        name="project",
        out_shape=(
            pltpu.HBM(full, BF16),
            pltpu.HBM(full, BF16),
            pltpu.HBM(full, BF16),
            pltpu.HBM((total // blk, width, blk), BF16),
            pltpu.HBM(full, F32),
            pltpu.HBM(full, F32),
        ),
        compiler_params=params(12),
        cost_estimate=pl.CostEstimate(
            flops=8 * total * width * width, bytes_accessed=20 * total * width, transcendentals=0
        ),
    )(rows, wq, wk, wv, wvt)


def pair_rows(x, low):
    zero = jnp.zeros_like(x)
    return jnp.concatenate([jnp.where(low, x, zero), jnp.where(low, zero, x)], axis=0)


PAD = 16


def attend_kernel(head, picks, own_s, lists_s, counts_s, *refs):
    (arrived_ref, q_ref, k_ref, vt_ref, clip_ref, wk_ref, wvt_ref, wo_ref, gain_ref,
     lifted_ref, act_ref, near_ref, farther_ref, kf_ref, rf_ref, e_ref, row_ref, col_ref,
     mixed_ref, kcat, vcat) = refs
    c = pl.program_id(0)
    near_ref, farther_ref, kf_ref, rf_ref, e_ref, row_ref, col_ref = (
        r.at[pl.ds(c, 1)] for r in (near_ref, farther_ref, kf_ref, rf_ref, e_ref, row_ref, col_ref)
    )
    lifted_ref, act_ref = (r.at[:, pl.ds(c, 1)] for r in (lifted_ref, act_ref))
    own = own_s[0]
    count = counts_s[c, own]
    blk, width = q_ref.shape[1:]
    half = width // 2
    keys = (1 + picks) * blk
    pairs = width // 128

    @pl.when(c == 0)
    def _():
        vcat[:, 128:] = jnp.ones((pairs, PAD, keys), BF16)

    ones_h = head_ones(half, head)
    rows = jnp.concatenate([arrived_ref[lists_s[c, s, own]] for s in range(picks)], axis=0)
    kcat[:blk] = k_ref[0]
    vcat[:, :128, :blk] = vt_ref[0].reshape(pairs, 128, blk)
    vcat[:, :128, blk:] = mm_t(wvt_ref[...], rows).astype(BF16).reshape(pairs, 128, keys - blk)
    for n in range(2):
        cols = slice(n * half, (n + 1) * half)
        pre = mm(rows, wk_ref[:, cols])
        r = lax.rsqrt(head_mean(pre * pre, ones_h, head) + EPSILON)
        k = (pre * r).astype(BF16)
        kcat[blk:, cols] = k
        kf_ref[0, :, cols] = k
        rf_ref[0, :, cols] = r
    low = lax.broadcasted_iota(jnp.int32, (blk, 128), 1) < head
    live = [jnp.where(s < count, 1.0, 0.0) for s in range(picks)]
    mixed = []
    inverses = []
    for p in range(pairs):
        cols = slice(128 * p, 128 * (p + 1))
        q2 = pair_rows(q_ref[0, :, cols], low)
        grown = jnp.exp(mm_t(kcat[:, cols], q2))
        e_ref[0, p, :blk] = grown[:blk].astype(BF16)
        for s in range(picks):
            part = slice((1 + s) * blk, (2 + s) * blk)
            e_ref[0, p, part] = (grown[part] * live[s]).astype(BF16)
        out = mm(vcat[p], e_ref[0, p])
        inverse = 1.0 / out[128:129]
        inverses += [inverse[:, :blk], inverse[:, blk:]]
        out = out[:128] * inverse
        out = jnp.concatenate([out[:head, :blk], out[head:, blk:]], axis=0)
        mixed.append(jnp.transpose(out).astype(BF16))
    inverses = jnp.concatenate(inverses, axis=0)
    row_ref[0] = inverses
    spread = jnp.concatenate([inverses, jnp.zeros((128 - HEADS, blk), F32)], axis=0)
    col_ref[0] = jnp.transpose(spread)
    mixed = jnp.concatenate(mixed, axis=1)
    mixed_ref[c] = mixed
    clip = clip_ref[:, 0].reshape(blk, width).astype(F32)
    lifted = (clip + mm(mixed, wo_ref[...])).astype(BF16)
    lifted_f = lifted.astype(F32)
    act, _ = silu_parts(lifted_f * rms(lifted_f) * gain_ref[...])
    slabs = (clip_ref.shape[0], clip_ref.shape[2], width)
    lifted_ref[:, 0] = lifted.reshape(slabs)
    act = act.astype(BF16).reshape(slabs)
    act_ref[:, 0] = act
    even = lax.rem(own, 2) == 0
    near_ref[0] = jnp.where(even, act[-1], act[0])
    farther_ref[0] = jnp.where(even, act[0], act[-1])


def per_camera(x):
    zeros = (0,) * (x.ndim - 1)
    return pl.BlockSpec((1,) + x.shape[1:], lambda c, *_: (c,) + zeros)


def attend(own, lists, counts, arrived, q, k, vt, clip_t, wk, wvt, wo, gain, head):
    tw, cams, nr, width = clip_t.shape
    blk = tw * nr
    picks = lists.shape[1]
    keys = (1 + picks) * blk
    pairs = width // 128
    slab = pl.BlockSpec((tw, 1, nr, width), lambda c, *_: (0, c, 0, 0))
    outs = (
        pltpu.VMEM(clip_t.shape, BF16),
        pltpu.VMEM(clip_t.shape, BF16),
        jax.ShapeDtypeStruct((cams, nr, width), BF16),
        jax.ShapeDtypeStruct((cams, nr, width), BF16),
        pltpu.VMEM((cams, picks * blk, width), BF16),
        pltpu.VMEM((cams, picks * blk, width), F32),
        pltpu.VMEM((cams, pairs, keys, 2 * blk), BF16),
        pltpu.VMEM((cams, HEADS, blk), F32),
        pltpu.VMEM((cams, blk, 128), F32),
        pltpu.VMEM((cams, blk, width), BF16),
    )
    weights = (wk, hbm(wvt), hbm(wo), gain)
    return pl.pallas_call(
        functools.partial(attend_kernel, head, picks),
        name="attend",
        out_shape=outs,
        grid_spec=pltpu.PrefetchScalarGridSpec(
            num_scalar_prefetch=3,
            grid=(cams,),
            in_specs=[whole(arrived.shape), per_camera(q), per_camera(k), per_camera(vt), slab]
            + [whole(x.shape) for x in weights],
            out_specs=[whole(x.shape) for x in outs],
            scratch_shapes=[
                pltpu.VMEM((keys, width), BF16),
                pltpu.VMEM((pairs, 128 + PAD, keys), BF16),
            ],
        ),
        compiler_params=params(10 + picks),
    )(own, lists, counts, arrived, hbm(q), hbm(k), hbm(vt), hbm(clip_t), *weights)


def far_values_kernel(arrived_ref, w_ref, out_ref):
    out_ref[...] = mm(arrived_ref[...], w_ref[...]).astype(BF16)


def far_values(arrived, w):
    total, width = arrived.shape
    return pl.pallas_call(
        far_values_kernel,
        name="far_values",
        out_shape=pltpu.VMEM((total, width), BF16),
        grid=(total // 512,),
        in_specs=[pl.BlockSpec((512, width), lambda i: (i, 0)), whole(w.shape)],
        out_specs=pl.BlockSpec((512, width), lambda i: (i, 0)),
        compiler_params=params(6),
        cost_estimate=pl.CostEstimate(
            flops=2 * total * width * width, bytes_accessed=4 * total * width, transcendentals=0
        ),
    )(arrived, w)


def fill_windows(own_s, act_ref, near_ref, farther_ref, x_ref, edge, total):
    width = act_ref.shape[1]
    even = lax.rem(own_s[0], 2) == 0
    near = near_ref[...]
    farther = farther_ref[...]
    x_ref[:edge, :width] = jnp.where(even, farther, near)
    x_ref[edge:, :width] = act_ref[: total - edge]
    x_ref[:, width : 2 * width] = act_ref[...]
    x_ref[: total - edge, 2 * width :] = act_ref[edge:]
    x_ref[total - edge :, 2 * width :] = jnp.where(even, near, farther)


def conv_step(w_ref, x_ref, y_ref, step, transposed):
    width = w_ref.shape[2]
    if transposed:
        total = None
        for q in range(3):
            cols = slice((2 - q) * width, (3 - q) * width)
            part = mm_t(x_ref[:, cols], w_ref[0, q])
            total = part if total is None else total + part
        y_ref[step] = total
    else:
        y_ref[step] = mm(x_ref[...], w_ref[0].reshape(3 * width, width))


def conv_rows(y_ref, start, size, nr, transposed):
    rows = pl.ds(start, size)
    before, centre, after = (2, 1, 0) if transposed else (0, 1, 2)
    place = lax.broadcasted_iota(jnp.int32, (size, 1), 0) % nr
    up = pltpu.roll(y_ref[before, rows, :], 1, 0)
    down = pltpu.roll(y_ref[after, rows, :], size - 1, 0)
    return (
        jnp.where(place == 0, 0.0, up)
        + y_ref[centre, rows, :]
        + jnp.where(place == nr - 1, 0.0, down)
    )


def conv_kernel(body, n_extra, transposed, nr, own_s, act_ref, near_ref, farther_ref, w_ref, *refs):
    extra, outs, (x_ref, y_ref) = refs[:n_extra], refs[n_extra:-2], refs[-2:]
    step = pl.program_id(0)
    total = act_ref.shape[0]
    edge = near_ref.shape[0]

    @pl.when(step == 0)
    def _():
        fill_windows(own_s, act_ref, near_ref, farther_ref, x_ref, edge, total)

    conv_step(w_ref, x_ref, y_ref, step, transposed)

    @pl.when(step == 2)
    def _():
        even = lax.rem(own_s[0], 2) == 0
        body(lambda start, size: conv_rows(y_ref, start, size, nr, transposed), even, edge, extra, outs)


def conv_call(name, body, own, act, near, farther, weights, extra, outs, nr, transposed):
    total, width = act.shape
    edge = near.shape[0]
    return pl.pallas_call(
        functools.partial(conv_kernel, body, len(extra), transposed, nr),
        name=name,
        out_shape=outs,
        grid_spec=pltpu.PrefetchScalarGridSpec(
            num_scalar_prefetch=1,
            grid=(3,),
            in_specs=[
                whole((total, width)),
                whole((edge, width)),
                whole((edge, width)),
                pl.BlockSpec((1, 3, width, width), lambda p, *_: (p, 0, 0, 0)),
            ]
            + [whole(e.shape) for e in extra],
            out_specs=[whole(o.shape) for o in outs],
            scratch_shapes=[
                pltpu.VMEM((total, 3 * width), BF16),
                pltpu.VMEM((3, total, width), F32),
            ],
        ),
        compiler_params=params(14),
        cost_estimate=pl.CostEstimate(
            flops=18 * total * width * width, bytes_accessed=18 * width * width, transcendentals=0
        ),
    )(own, act, near, farther, weights, *extra)


CHUNK = 128


def chunks(total, fn):
    def step(i, carry):
        fn(pl.multiple_of(i * CHUNK, CHUNK))
        return carry

    lax.fori_loop(0, total // CHUNK, step, 0)


def grad_two_body(rows_of, even, edge, extra, outs):
    (out,) = outs

    def one(start):
        out[pl.ds(start, CHUNK), :] = rows_of(start, CHUNK)

    chunks(out.shape[0], one)


def copy_edges(even, edge, full, near, farther):
    total = full.shape[0]
    first = full[:edge]
    last = full[total - edge :]
    near[...] = jnp.where(even, last, first)
    farther[...] = jnp.where(even, first, last)


def conv_one_body(rows_of, even, edge, extra, outs):
    grad_ref, gain_ref = extra
    act_ref, act_near, act_far, d_ref, d_near, d_far = outs
    total = act_ref.shape[0]
    gain = gain_ref[...]

    def one(start):
        rows = pl.ds(start, CHUNK)
        conv = rows_of(start, CHUNK)
        r = rms(conv)
        hat = conv * r
        act, slope = silu_parts(hat * gain)
        act_ref[rows, :] = act.astype(BF16)
        g = grad_ref[rows, :] * slope * gain
        d_ref[rows, :] = (r * (g - hat * jnp.mean(g * hat, axis=-1, keepdims=True))).astype(BF16)

    chunks(total, one)
    copy_edges(even, edge, act_ref, act_near, act_far)
    copy_edges(even, edge, d_ref, d_near, d_far)


def conv_two_body(rows_of, even, edge, extra, outs):
    (lifted_ref,) = extra
    (out,) = outs

    def one(start):
        rows = pl.ds(start, CHUNK)
        out[rows, :] = (lifted_ref[rows, :].astype(F32) + rows_of(start, CHUNK)).astype(BF16)

    chunks(out.shape[0], one)


def grad_main_kernel(edge, act_ref, w_ref, y_ref, x_ref):
    step = pl.program_id(0)
    total, width = act_ref.shape

    @pl.when(step == 0)
    def _():
        blank = jnp.zeros((edge, width), BF16)
        x_ref[:edge, :width] = blank
        x_ref[edge:, :width] = act_ref[: total - edge]
        x_ref[:, width : 2 * width] = act_ref[...]
        x_ref[: total - edge, 2 * width :] = act_ref[edge:]
        x_ref[total - edge :, 2 * width :] = blank

    conv_step(w_ref, x_ref, y_ref, step, True)


def grad_main(act, weights, edge):
    total, width = act.shape
    return pl.pallas_call(
        functools.partial(grad_main_kernel, edge),
        name="grad_main",
        out_shape=pltpu.VMEM((3, total, width), F32),
        grid_spec=pltpu.PrefetchScalarGridSpec(
            num_scalar_prefetch=0,
            grid=(3,),
            in_specs=[
                whole((total, width)),
                pl.BlockSpec((1, 3, width, width), lambda p, *_: (p, 0, 0, 0)),
            ],
            out_specs=whole((3, total, width)),
            scratch_shapes=[pltpu.VMEM((total, 3 * width), BF16)],
        ),
        compiler_params=params(14),
        cost_estimate=pl.CostEstimate(
            flops=18 * total * width * width, bytes_accessed=18 * width * width, transcendentals=0
        ),
    )(act, weights)


def grad_tail_kernel(nr, own_s, near_ref, farther_ref, w_ref, y_ref, lifted_ref, cot_ref, gain_ref,
                     wo_ref, d_lifted_ref, d_mixed_ref, z_ref):
    edge = near_ref.shape[0]
    total = d_lifted_ref.shape[0]
    even = lax.rem(own_s[0], 2) == 0
    near = near_ref[...]
    farther = farther_ref[...]
    left = jnp.where(even, farther, near)
    right = jnp.where(even, near, farther)
    for p in range(3):
        z_ref[0, p] = mm_t(left, w_ref[p, 2])
        z_ref[1, p] = mm_t(right, w_ref[p, 0])
    gain = gain_ref[...]
    split = (edge // nr + 1) // 2 * nr
    for start in range(0, total, edge):
        for first, last in ((0, split), (split, edge)):
            size = last - first
            rows = slice(start + first, start + last)
            taps = []
            for p in range(3):
                tap = y_ref[p, rows]
                if start == 0:
                    tap = tap + z_ref[0, p, first:last]
                if start == total - edge:
                    tap = tap + z_ref[1, p, first:last]
                taps.append(tap)
            place = lax.broadcasted_iota(jnp.int32, (size, 1), 0) % nr
            conv = (
                jnp.where(place == 0, 0.0, pltpu.roll(taps[2], 1, 0))
                + taps[1]
                + jnp.where(place == nr - 1, 0.0, pltpu.roll(taps[0], size - 1, 0))
            )
            lifted = lifted_ref[rows].astype(F32)
            r = rms(lifted)
            hat = lifted * r
            _, slope = silu_parts(hat * gain)
            g = conv * slope * gain
            back = r * (g - hat * jnp.mean(g * hat, axis=-1, keepdims=True))
            d_lifted_ref[rows] = cot_ref[rows].astype(F32) + back
    d_mixed_ref[...] = mm_t(d_lifted_ref[...].astype(BF16), wo_ref[...]).astype(BF16)


def grad_tail(own, near, farther, weights, y, lifted, cot, gain, wo, nr):
    args = (near, farther, weights, y, lifted, cot, gain, wo)
    edge, width = near.shape
    outs = (pltpu.VMEM(lifted.shape, F32), pltpu.VMEM(lifted.shape, BF16))
    return pl.pallas_call(
        functools.partial(grad_tail_kernel, nr),
        name="grad_tail",
        out_shape=outs,
        grid_spec=pltpu.PrefetchScalarGridSpec(
            num_scalar_prefetch=1,
            grid=(1,),
            in_specs=[whole(x.shape) for x in args],
            out_specs=[whole(x.shape) for x in outs],
            scratch_shapes=[pltpu.VMEM((2, 3, edge, width), F32)],
        ),
        compiler_params=params(14),
    )(own, *args)


def head_norm_back(grad, hat, r, ones, head):
    hat = hat.astype(F32)
    return r * (grad - hat * head_mean(grad * hat, ones, head))


def drift_rows(head, dm, mixed, row):
    width = dm.shape[1]
    lanes = lax.broadcasted_iota(jnp.int32, (PAD, width), 1) // head
    picked = (lanes == lax.broadcasted_iota(jnp.int32, (PAD, width), 0)).astype(BF16)
    product = (dm.astype(F32) * mixed.astype(F32)).astype(BF16)
    return mm_t(picked, product)[:HEADS] * row


def pair_queries(p, q, dm, col, drift, low):
    cols = slice(128 * p, 128 * (p + 1))
    spread = jnp.where(low, col[:, 2 * p : 2 * p + 1], col[:, 2 * p + 1 : 2 * p + 2])
    q2 = pair_rows(q[:, cols], low)
    dm2 = pair_rows((dm[:, cols].astype(F32) * spread).astype(BF16), low)
    shift = jnp.concatenate([drift[2 * p : 2 * p + 1], drift[2 * p + 1 : 2 * p + 2]], axis=1)
    return q2, dm2, shift


def far_grads_kernel(head, picks, own_s, lists_s, counts_s, q_ref, vf_ref, e_ref, dm_ref, mixed_ref,
                     row_ref, col_ref, kf_ref, rf_ref, wk_ref, wv_ref, send_ref, kgrad, vgrad, shares, sems):
    c = pl.program_id(0)
    own = own_s[0]
    cams, blk, width = mixed_ref.shape
    low = lax.broadcasted_iota(jnp.int32, (blk, 128), 1) < head
    q = q_ref[0]
    dm = dm_ref[:, c].reshape(blk, width)
    drift = drift_rows(head, dm, mixed_ref[c], row_ref[c])
    col = col_ref[c]
    for p in range(width // 128):
        cols = slice(128 * p, 128 * (p + 1))
        q2, dm2, shift = pair_queries(p, q, dm, col, drift, low)
        far_v = jnp.concatenate([vf_ref[lists_s[c, s, own], :, cols] for s in range(picks)], axis=0)
        e = e_ref[c, p, blk:]
        d_scaled = (e.astype(F32) * (mm_t(far_v, dm2) - shift)).astype(BF16)
        kgrad[c, :, cols] = mm(d_scaled, q2)
        vgrad[c, :, cols] = mm(e, dm2).astype(BF16)

    @pl.when(c == cams - 1)
    def _():
        ones_h = head_ones(width // 2, head)

        def back(i, carry):
            grad = head_norm_back(kgrad[i], kf_ref[i], rf_ref[i], ones_h, head)
            shares[i] = grad.astype(BF16)
            return carry

        lax.fori_loop(0, cams, back, 0)
        shape = (picks * blk, width)
        for first, last in ((0, (cams + 1) // 2), ((cams + 1) // 2, cams)):
            count = last - first
            share = mm_t(shares[first:last].reshape(count * shape[0], width), wk_ref[...])
            share = share + mm_t(vgrad[first:last].reshape(count * shape[0], width), wv_ref[...])
            shares[first:last] = share.astype(BF16).reshape((count,) + shape)
            for i in range(first, last):
                for s in range(picks):
                    pltpu.make_async_copy(
                        shares.at[i, pl.ds(s * blk, blk)],
                        send_ref.at[lists_s[i, s, own]],
                        sems.at[i, s],
                    ).start()
        for i in range(cams):
            for s in range(picks):
                pltpu.make_async_copy(
                    shares.at[i, pl.ds(s * blk, blk)], send_ref.at[0], sems.at[i, s]
                ).wait()


def far_grads(own, lists, counts, n_cols, q, vf, e, dm_t, mixed, row, col, kf, rf, wk, wv, head):
    cams, blk, width = mixed.shape
    picks = lists.shape[1]
    args = (vf, e, dm_t, mixed, row, col, kf, rf, wk, wv)
    return pl.pallas_call(
        functools.partial(far_grads_kernel, head, picks),
        name="far_grads",
        out_shape=pltpu.HBM((n_cols, blk, width), BF16),
        grid_spec=pltpu.PrefetchScalarGridSpec(
            num_scalar_prefetch=3,
            grid=(cams,),
            in_specs=[per_camera(q)] + [whole(x.shape) for x in args],
            out_specs=pl.BlockSpec(memory_space=pltpu.HBM),
            scratch_shapes=[
                pltpu.VMEM((cams, picks * blk, width), F32),
                pltpu.VMEM((cams, picks * blk, width), BF16),
                pltpu.VMEM((cams, picks * blk, width), BF16),
                pltpu.SemaphoreType.DMA((cams, picks)),
            ],
        ),
        compiler_params=params(4 + 6 * picks),
    )(own, lists, counts, hbm(q), *args)


def own_grads_kernel(head, picks, own_s, lists_s, q_ref, k_ref, v_ref, rq_ref, rk_ref, vf_ref, e_ref, dm_ref,
                     mixed_ref, row_ref, col_ref, kf_ref, wq_ref, wk_ref, wv_ref, out_ref):
    c = pl.program_id(0)
    own = own_s[0]
    cams, blk, width = mixed_ref.shape
    low = lax.broadcasted_iota(jnp.int32, (blk, 128), 1) < head
    ones_h = head_ones(width // 2, head)
    scale = head ** (-0.5)
    q = q_ref[0]
    dm = dm_ref[:, c].reshape(blk, width)
    drift = drift_rows(head, dm, mixed_ref[c], row_ref[c])
    col = col_ref[c]
    listed = [lists_s[c, s, own] for s in range(picks)]
    dq, dk, dv = [], [], []
    for p in range(width // 128):
        cols = slice(128 * p, 128 * (p + 1))
        q2, dm2, shift = pair_queries(p, q, dm, col, drift, low)
        all_v = jnp.concatenate([v_ref[0, :, cols]] + [vf_ref[i, :, cols] for i in listed], axis=0)
        all_k = jnp.concatenate([k_ref[0, :, cols], kf_ref[c, :, cols]], axis=0)
        e = e_ref[c, p]
        d_scaled = (e.astype(F32) * (mm_t(all_v, dm2) - shift)).astype(BF16)
        dk.append(mm(d_scaled[:blk], q2))
        dv.append(mm(e[:blk], dm2).astype(BF16))
        both = mm(jnp.transpose(d_scaled), all_k)
        dq.append(jnp.where(low, both[:blk], both[blk:]) * scale)
    dq, dk, dv = (jnp.concatenate(parts, axis=1) for parts in (dq, dk, dv))
    q_hat = q.astype(F32) * (1.0 / scale)
    dq = head_norm_back(dq, q_hat, rq_ref[0], ones_h, head).astype(BF16)
    dk = head_norm_back(dk, k_ref[0], rk_ref[0], ones_h, head).astype(BF16)
    out_ref[0] = mm_t(dq, wq_ref[...]) + mm_t(dk, wk_ref[...]) + mm_t(dv, wv_ref[...])


def own_grads(own, lists, q, k, v, rq, rk, vf, e, dm_t, mixed, row, col, kf, wq, wk, wv, head):
    cams, blk, width = mixed.shape
    picks = lists.shape[1]
    windows = (q, k, v, rq, rk)
    args = (vf, e, dm_t, mixed, row, col, kf, wq, wk, wv)
    return pl.pallas_call(
        functools.partial(own_grads_kernel, head, picks),
        name="own_grads",
        out_shape=pltpu.HBM((cams, blk, width), F32),
        grid_spec=pltpu.PrefetchScalarGridSpec(
            num_scalar_prefetch=2,
            grid=(cams,),
            in_specs=[per_camera(x) for x in windows] + [whole(x.shape) for x in args],
            out_specs=per_camera(mixed),
        ),
        compiler_params=params(6 + picks),
        cost_estimate=pl.CostEstimate(
            flops=20 * cams * blk * width * width, bytes_accessed=4 * e.size, transcendentals=0
        ),
    )(own, lists, *map(hbm, windows), *args)


def final_kernel(table_s, back_ref, rows_ref, clip_ref, dl_ref, gain_ref, out_ref, acc):
    tw, cams, nr, width = clip_ref.shape
    blk = tw * nr
    acc[...] = rows_ref[...]

    def add(i, carry):
        cam = table_s[i]

        @pl.when(cam >= 0)
        def _():
            acc[cam] += back_ref[i].astype(F32)

        return carry

    lax.fori_loop(0, back_ref.shape[0], add, 0)
    gain = gain_ref[...]

    def one(c, carry):
        x = clip_ref[:, c].reshape(blk, width).astype(F32)
        r = rms(x)
        hat = x * r
        g = acc[c] * gain
        d = dl_ref[:, c].reshape(blk, width) + r * (
            g - hat * jnp.mean(g * hat, axis=-1, keepdims=True)
        )
        out_ref[:, c] = d.astype(BF16).reshape(tw, nr, width)
        return carry

    lax.fori_loop(0, cams, one, 0)


def final(table, back, rows, clip_t, d_lifted, gain):
    args = (back, rows, clip_t, d_lifted, gain)
    return pl.pallas_call(
        final_kernel,
        name="final",
        out_shape=jax.ShapeDtypeStruct(clip_t.shape, BF16),
        grid_spec=pltpu.PrefetchScalarGridSpec(
            num_scalar_prefetch=1,
            grid=(1,),
            in_specs=[whole(x.shape) for x in args],
            out_specs=whole(clip_t.shape),
            scratch_shapes=[pltpu.VMEM(rows.shape, F32)],
        ),
        compiler_params=params(8),
    )(table, *args)


def exchange_edges(near, farther):
    size = lax.axis_size("cols")
    inner = [(i, i ^ 1) for i in range(size)]
    outer = [(i, i + 1 if i % 2 else i - 1) for i in range(1, size - 1)]
    return lax.ppermute(near, "cols", inner), lax.ppermute(farther, "cols", outer)


def local(
    clip_tokens,
    cotangent,
    gain_attn,
    w_query,
    w_key,
    w_value,
    w_out,
    gain_first,
    conv_first,
    gain_second,
    conv_second,
    matching,
    block_lists,
    counts,
):
    views, nr, tw, width = clip_tokens.shape
    head = width // HEADS
    n_cols = lax.axis_size("cols")
    own_index = lax.axis_index("cols").astype(jnp.int32)
    own = own_index.reshape(1)
    total = views * nr * tw
    blk = nr * tw
    flat = (total, width)
    slabs = (tw, views, nr, width)
    block_lists = jnp.transpose(block_lists, (0, 2, 1))
    gain_attn = gain_attn.reshape(1, width)
    gain_first = gain_first.reshape(1, width)
    gain_second = gain_second.reshape(1, width)

    clip_t = jnp.transpose(clip_tokens, (2, 0, 1, 3))
    cot_t = jnp.transpose(cotangent, (2, 0, 1, 3))
    odd = own_index % 2
    last = (tw - 1) * (1 - odd)
    cot_near = lax.dynamic_index_in_dim(cot_t, last, 0, keepdims=False).reshape(-1, width)
    cot_far = lax.dynamic_index_in_dim(cot_t, tw - 1 - last, 0, keepdims=False).reshape(-1, width)

    rows, send = prep(n_cols, own, matching, block_lists, counts, clip_t, gain_attn)
    cot_near, cot_far = exchange_edges(cot_near, cot_far)
    arrived = lax.all_to_all(send, "cols", split_axis=0, concat_axis=0, tiled=True)
    rows, w_value, lists, live = lax.optimization_barrier((rows, w_value, block_lists, counts))
    w_value_t = w_value.T
    slots = jnp.arange(lists.shape[1], dtype=jnp.int32)
    asks = (lists == own_index) & (slots[None, :, None] < live[:, None, :])
    table = jnp.sum(jnp.where(asks, matching[:, None, None] + 1, 0), axis=(0, 1)) - 1
    q, k, v, vt, rq, rk = project(rows.reshape(flat), w_query, w_key, w_value, w_value_t, head, blk)
    q, k, v, rq, rk = (a.reshape(views, blk, width) for a in (q, k, v, rq, rk))
    arrived, q, k, v, vt, rq, rk = lax.optimization_barrier((arrived, q, k, v, vt, rq, rk))
    lifted, act_one, near, farther, kf, rf, e, row, col, mixed = attend(
        own, block_lists, counts, arrived, q, k, vt, clip_t, w_key, w_value_t, w_out, gain_first, head
    )
    edge = (views * nr, width)
    near, farther = exchange_edges(near.reshape(edge), farther.reshape(edge))
    (d_act_two,) = conv_call(
        "grad_two", grad_two_body, own, cot_t.reshape(flat), cot_near, cot_far, conv_second,
        (), (pltpu.VMEM(flat, F32),), nr, True,
    )
    flat_bf = pltpu.VMEM(flat, BF16)
    edge_bf = jax.ShapeDtypeStruct(edge, BF16)
    act_two, act_near, act_far, d_conv, d_near, d_far = conv_call(
        "conv_one", conv_one_body, own, act_one.reshape(flat), near, farther, conv_first,
        (d_act_two, gain_second),
        (flat_bf, edge_bf, edge_bf, flat_bf, edge_bf, edge_bf), nr, False,
    )
    d_near, d_far = exchange_edges(d_near, d_far)
    d_conv, fetched = lax.optimization_barrier((d_conv, arrived))
    vf = far_values(fetched.reshape(-1, width), w_value)
    y_grad = grad_main(d_conv, conv_first, views * nr)
    d_near, d_far, vf, y_grad = lax.optimization_barrier((d_near, d_far, vf, y_grad))
    vf = vf.reshape(arrived.shape)
    d_lifted, d_mixed = grad_tail(
        own, d_near, d_far, conv_first, y_grad, lifted.reshape(flat), cot_t.reshape(flat), gain_first, w_out, nr
    )
    d_mixed, act_near, act_far = lax.optimization_barrier((d_mixed, act_near, act_far))
    d_mixed = d_mixed.reshape(slabs)
    act_near, act_far = exchange_edges(act_near, act_far)
    send_back = far_grads(
        own, block_lists, counts, n_cols, q, vf, e, d_mixed, mixed, row, col, kf, rf, w_key, w_value, head
    )
    send_back, act_near, act_far = lax.optimization_barrier((send_back, act_near, act_far))
    back = lax.all_to_all(send_back, "cols", split_axis=0, concat_axis=0, tiled=True)
    (result,) = conv_call(
        "conv_two", conv_two_body, own, act_two, act_near, act_far, conv_second,
        (lifted.reshape(flat),), (jax.ShapeDtypeStruct(flat, BF16),), nr, False,
    )
    d_rows = own_grads(
        own, block_lists, q, k, v, rq, rk, vf, e, d_mixed, mixed, row, col, kf, w_query, w_key, w_value, head
    )
    d_clip = final(table, back, d_rows, clip_t, d_lifted.reshape(slabs), gain_attn)
    return (
        jnp.transpose(result.reshape(slabs), (1, 2, 0, 3)),
        jnp.transpose(d_clip, (1, 2, 0, 3)),
    )


def solution(mesh):
    tiles = P("groups", None, "cols", None)
    in_specs = (tiles, tiles) + (P(),) * 12
    return jax.shard_map(
        local, mesh=mesh, in_specs=in_specs, out_specs=(tiles, tiles), check_vma=False
    )
```

```python
import functools

import jax
import jax.numpy as jnp
from jax import lax
from jax.experimental import pallas as pl
from jax.experimental.pallas import tpu as pltpu
from jax.sharding import PartitionSpec as P

HEADS = 8
EPSILON = 1e-06
F32 = jnp.float32
BF16 = jnp.bfloat16


def mm(a, b):
    return lax.dot_general(a, b, (((1,), (0,)), ((), ())), preferred_element_type=F32)


def mm_t(a, b):
    return lax.dot_general(a, b, (((1,), (1,)), ((), ())), preferred_element_type=F32)


def params(mib):
    return pltpu.CompilerParams(vmem_limit_bytes=mib * 1024 * 1024)


def hbm(x):
    return pltpu.with_memory_space_constraint(x, pltpu.HBM)


def vmem(x):
    return pltpu.with_memory_space_constraint(x, pltpu.VMEM)


def whole(shape):
    zeros = (0,) * len(shape)
    return pl.BlockSpec(shape, lambda *_: zeros)


def rms(values):
    return lax.rsqrt(jnp.mean(values * values, axis=-1, keepdims=True) + EPSILON)


def silu_parts(u):
    sigmoid = 0.5 + 0.5 * jnp.tanh(0.5 * u)
    return u * sigmoid, sigmoid * (1.0 + u * (1.0 - sigmoid))


def head_ones(width, head):
    rows = lax.broadcasted_iota(jnp.int32, (width, width), 0) // head
    cols = lax.broadcasted_iota(jnp.int32, (width, width), 1) // head
    return jnp.where(rows == cols, 1.0, 0.0).astype(BF16)


def head_mean(values, ones, head):
    width = ones.shape[0]
    parts = [
        mm(values[:, i : i + width].astype(BF16), ones)
        for i in range(0, values.shape[1], width)
    ]
    return jnp.concatenate(parts, axis=1) * (1.0 / head)


def prep_kernel(n_cols, own_s, match_s, lists_s, counts_s, clip_ref, gain_ref, rows_ref, send_ref, sem):
    cams = match_s.shape[0]
    picks = lists_s.shape[1]
    own = own_s[0]
    tw, _, nr, width = clip_ref.shape
    for c in range(cams):
        x = clip_ref[:, c].reshape(tw * nr, width).astype(F32)
        rows_ref[c] = (x * rms(x) * gain_ref[...]).astype(BF16)

    def copy(i):
        cam = jnp.int32(0)
        for c in range(cams):
            for s in range(picks):
                hit = (lists_s[c, s, i] == own) & (s < counts_s[c, i])
                cam = jnp.where(hit, match_s[c], cam)
        pltpu.make_async_copy(rows_ref.at[cam], send_ref.at[i], sem.at[i]).start()

    def start(i, carry):
        copy(i)
        return carry

    lax.fori_loop(0, n_cols, start, 0)

    def wait(i, carry):
        pltpu.make_async_copy(rows_ref.at[0], send_ref.at[i], sem.at[i]).wait()
        return carry

    lax.fori_loop(0, n_cols, wait, 0)


def prep(n_cols, own, matching, lists, counts, clip_t, gain):
    tw, cams, nr, width = clip_t.shape
    blk = tw * nr
    return pl.pallas_call(
        functools.partial(prep_kernel, n_cols),
        name="prep",
        out_shape=(
            jax.ShapeDtypeStruct((cams, blk, width), BF16),
            pltpu.HBM((n_cols, blk, width), BF16),
        ),
        grid_spec=pltpu.PrefetchScalarGridSpec(
            num_scalar_prefetch=4,
            grid=(1,),
            in_specs=[whole(clip_t.shape), whole((1, width))],
            out_specs=[whole((cams, blk, width)), pl.BlockSpec(memory_space=pltpu.HBM)],
            scratch_shapes=[pltpu.SemaphoreType.DMA((n_cols,))],
        ),
        compiler_params=params(8),
    )(own, hbm(matching), lists, hbm(counts), clip_t, hbm(gain))


def project_kernel(head, blk, rows_ref, wq_ref, wk_ref, wv_ref, wvt_ref, q_ref, k_ref, v_ref, vt_ref, rq_ref, rk_ref):
    rows = rows_ref[...]
    total, width = rows.shape
    half = width // 2
    ones = head_ones(half, head)
    for n in range(2):
        cols = slice(n * half, (n + 1) * half)
        for w_ref, o_ref, r_ref, scale in (
            (wq_ref, q_ref, rq_ref, head ** (-0.5)),
            (wk_ref, k_ref, rk_ref, 1.0),
        ):
            pre = mm(rows, w_ref[:, cols])
            r = lax.rsqrt(head_mean(pre * pre, ones, head) + EPSILON)
            o_ref[:, cols] = (pre * r * scale).astype(BF16)
            r_ref[:, cols] = r
        v_ref[:, cols] = mm(rows, wv_ref[:, cols]).astype(BF16)
    for c in range(total // blk):
        vt_ref[c] = mm_t(wvt_ref[...], rows_ref[c * blk : (c + 1) * blk]).astype(BF16)


def project(rows, wq, wk, wv, wvt, head, blk):
    total, width = rows.shape
    full = (total, width)
    return pl.pallas_call(
        functools.partial(project_kernel, head, blk),
        name="project",
        out_shape=(
            pltpu.HBM(full, BF16),
            pltpu.HBM(full, BF16),
            pltpu.HBM(full, BF16),
            pltpu.HBM((total // blk, width, blk), BF16),
            pltpu.HBM(full, F32),
            pltpu.HBM(full, F32),
        ),
        compiler_params=params(12),
        cost_estimate=pl.CostEstimate(
            flops=8 * total * width * width, bytes_accessed=20 * total * width, transcendentals=0
        ),
    )(rows, wq, wk, wv, wvt)


def pair_rows(x, low):
    zero = jnp.zeros_like(x)
    return jnp.concatenate([jnp.where(low, x, zero), jnp.where(low, zero, x)], axis=0)


PAD = 16


def attend_kernel(head, picks, own_s, lists_s, counts_s, *refs):
    (arrived_ref, q_ref, k_ref, vt_ref, clip_ref, wk_ref, wvt_ref, wo_ref, gain_ref,
     lifted_ref, act_ref, near_ref, farther_ref, kf_ref, rf_ref, e_ref, row_ref, col_ref,
     mixed_ref, kcat, vcat) = refs
    c = pl.program_id(0)
    near_ref, farther_ref, kf_ref, rf_ref, e_ref, row_ref, col_ref = (
        r.at[pl.ds(c, 1)] for r in (near_ref, farther_ref, kf_ref, rf_ref, e_ref, row_ref, col_ref)
    )
    lifted_ref, act_ref = (r.at[:, pl.ds(c, 1)] for r in (lifted_ref, act_ref))
    own = own_s[0]
    count = counts_s[c, own]
    blk, width = q_ref.shape[1:]
    half = width // 2
    keys = (1 + picks) * blk
    pairs = width // 128

    @pl.when(c == 0)
    def _():
        vcat[:, 128:] = jnp.ones((pairs, PAD, keys), BF16)

    ones_h = head_ones(half, head)
    rows = jnp.concatenate([arrived_ref[lists_s[c, s, own]] for s in range(picks)], axis=0)
    kcat[:blk] = k_ref[0]
    vcat[:, :128, :blk] = vt_ref[0].reshape(pairs, 128, blk)
    vcat[:, :128, blk:] = mm_t(wvt_ref[...], rows).astype(BF16).reshape(pairs, 128, keys - blk)
    for n in range(2):
        cols = slice(n * half, (n + 1) * half)
        pre = mm(rows, wk_ref[:, cols])
        r = lax.rsqrt(head_mean(pre * pre, ones_h, head) + EPSILON)
        k = (pre * r).astype(BF16)
        kcat[blk:, cols] = k
        kf_ref[0, :, cols] = k
        rf_ref[0, :, cols] = r
    low = lax.broadcasted_iota(jnp.int32, (blk, 128), 1) < head
    live = [jnp.where(s < count, 1.0, 0.0) for s in range(picks)]
    mixed = []
    inverses = []
    for p in range(pairs):
        cols = slice(128 * p, 128 * (p + 1))
        q2 = pair_rows(q_ref[0, :, cols], low)
        grown = jnp.exp(mm_t(kcat[:, cols], q2))
        e_ref[0, p, :blk] = grown[:blk].astype(BF16)
        for s in range(picks):
            part = slice((1 + s) * blk, (2 + s) * blk)
            e_ref[0, p, part] = (grown[part] * live[s]).astype(BF16)
        out = mm(vcat[p], e_ref[0, p])
        inverse = 1.0 / out[128:129]
        inverses += [inverse[:, :blk], inverse[:, blk:]]
        out = out[:128] * inverse
        out = jnp.concatenate([out[:head, :blk], out[head:, blk:]], axis=0)
        mixed.append(jnp.transpose(out).astype(BF16))
    inverses = jnp.concatenate(inverses, axis=0)
    row_ref[0] = inverses
    spread = jnp.concatenate([inverses, jnp.zeros((128 - HEADS, blk), F32)], axis=0)
    col_ref[0] = jnp.transpose(spread)
    mixed = jnp.concatenate(mixed, axis=1)
    mixed_ref[c] = mixed
    clip = clip_ref[:, 0].reshape(blk, width).astype(F32)
    lifted = (clip + mm(mixed, wo_ref[...])).astype(BF16)
    lifted_f = lifted.astype(F32)
    act, _ = silu_parts(lifted_f * rms(lifted_f) * gain_ref[...])
    slabs = (clip_ref.shape[0], clip_ref.shape[2], width)
    lifted_ref[:, 0] = lifted.reshape(slabs)
    act = act.astype(BF16).reshape(slabs)
    act_ref[:, 0] = act
    even = lax.rem(own, 2) == 0
    near_ref[0] = jnp.where(even, act[-1], act[0])
    farther_ref[0] = jnp.where(even, act[0], act[-1])


def per_camera(x):
    zeros = (0,) * (x.ndim - 1)
    return pl.BlockSpec((1,) + x.shape[1:], lambda c, *_: (c,) + zeros)


def attend(own, lists, counts, arrived, q, k, vt, clip_t, wk, wvt, wo, gain, head):
    tw, cams, nr, width = clip_t.shape
    blk = tw * nr
    picks = lists.shape[1]
    keys = (1 + picks) * blk
    pairs = width // 128
    slab = pl.BlockSpec((tw, 1, nr, width), lambda c, *_: (0, c, 0, 0))
    outs = (
        pltpu.VMEM(clip_t.shape, BF16),
        pltpu.VMEM(clip_t.shape, BF16),
        jax.ShapeDtypeStruct((cams, nr, width), BF16),
        jax.ShapeDtypeStruct((cams, nr, width), BF16),
        pltpu.VMEM((cams, picks * blk, width), BF16),
        pltpu.VMEM((cams, picks * blk, width), F32),
        pltpu.VMEM((cams, pairs, keys, 2 * blk), BF16),
        pltpu.VMEM((cams, HEADS, blk), F32),
        pltpu.VMEM((cams, blk, 128), F32),
        pltpu.VMEM((cams, blk, width), BF16),
    )
    weights = (wk, hbm(wvt), hbm(wo), gain)
    return pl.pallas_call(
        functools.partial(attend_kernel, head, picks),
        name="attend",
        out_shape=outs,
        grid_spec=pltpu.PrefetchScalarGridSpec(
            num_scalar_prefetch=3,
            grid=(cams,),
            in_specs=[whole(arrived.shape), per_camera(q), per_camera(k), per_camera(vt), slab]
            + [whole(x.shape) for x in weights],
            out_specs=[whole(x.shape) for x in outs],
            scratch_shapes=[
                pltpu.VMEM((keys, width), BF16),
                pltpu.VMEM((pairs, 128 + PAD, keys), BF16),
            ],
        ),
        compiler_params=params(10 + picks),
    )(own, lists, counts, arrived, hbm(q), hbm(k), hbm(vt), hbm(clip_t), *weights)


def far_values_kernel(arrived_ref, w_ref, out_ref):
    out_ref[...] = mm(arrived_ref[...], w_ref[...]).astype(BF16)


def far_values(arrived, w):
    total, width = arrived.shape
    return pl.pallas_call(
        far_values_kernel,
        name="far_values",
        out_shape=pltpu.VMEM((total, width), BF16),
        grid=(total // 512,),
        in_specs=[pl.BlockSpec((512, width), lambda i: (i, 0)), whole(w.shape)],
        out_specs=pl.BlockSpec((512, width), lambda i: (i, 0)),
        compiler_params=params(6),
        cost_estimate=pl.CostEstimate(
            flops=2 * total * width * width, bytes_accessed=4 * total * width, transcendentals=0
        ),
    )(arrived, w)


def fill_windows(own_s, act_ref, near_ref, farther_ref, x_ref, edge, total):
    width = act_ref.shape[1]
    even = lax.rem(own_s[0], 2) == 0
    near = near_ref[...]
    farther = farther_ref[...]
    x_ref[:edge, :width] = jnp.where(even, farther, near)
    x_ref[edge:, :width] = act_ref[: total - edge]
    x_ref[:, width : 2 * width] = act_ref[...]
    x_ref[: total - edge, 2 * width :] = act_ref[edge:]
    x_ref[total - edge :, 2 * width :] = jnp.where(even, near, farther)


def conv_step(w_ref, x_ref, y_ref, step, transposed):
    width = w_ref.shape[2]
    if transposed:
        total = None
        for q in range(3):
            cols = slice((2 - q) * width, (3 - q) * width)
            part = mm_t(x_ref[:, cols], w_ref[0, q])
            total = part if total is None else total + part
        y_ref[step] = total
    else:
        y_ref[step] = mm(x_ref[...], w_ref[0].reshape(3 * width, width))


def conv_rows(y_ref, start, size, nr, transposed):
    rows = pl.ds(start, size)
    before, centre, after = (2, 1, 0) if transposed else (0, 1, 2)
    place = lax.broadcasted_iota(jnp.int32, (size, 1), 0) % nr
    up = pltpu.roll(y_ref[before, rows, :], 1, 0)
    down = pltpu.roll(y_ref[after, rows, :], size - 1, 0)
    return (
        jnp.where(place == 0, 0.0, up)
        + y_ref[centre, rows, :]
        + jnp.where(place == nr - 1, 0.0, down)
    )


def conv_kernel(body, n_extra, transposed, nr, own_s, act_ref, near_ref, farther_ref, w_ref, *refs):
    extra, outs, (x_ref, y_ref) = refs[:n_extra], refs[n_extra:-2], refs[-2:]
    step = pl.program_id(0)
    total = act_ref.shape[0]
    edge = near_ref.shape[0]

    @pl.when(step == 0)
    def _():
        fill_windows(own_s, act_ref, near_ref, farther_ref, x_ref, edge, total)

    conv_step(w_ref, x_ref, y_ref, step, transposed)

    @pl.when(step == 2)
    def _():
        even = lax.rem(own_s[0], 2) == 0
        body(lambda start, size: conv_rows(y_ref, start, size, nr, transposed), even, edge, extra, outs)


def conv_call(name, body, own, act, near, farther, weights, extra, outs, nr, transposed):
    total, width = act.shape
    edge = near.shape[0]
    return pl.pallas_call(
        functools.partial(conv_kernel, body, len(extra), transposed, nr),
        name=name,
        out_shape=outs,
        grid_spec=pltpu.PrefetchScalarGridSpec(
            num_scalar_prefetch=1,
            grid=(3,),
            in_specs=[
                whole((total, width)),
                whole((edge, width)),
                whole((edge, width)),
                pl.BlockSpec((1, 3, width, width), lambda p, *_: (p, 0, 0, 0)),
            ]
            + [whole(e.shape) for e in extra],
            out_specs=[whole(o.shape) for o in outs],
            scratch_shapes=[
                pltpu.VMEM((total, 3 * width), BF16),
                pltpu.VMEM((3, total, width), F32),
            ],
        ),
        compiler_params=params(14),
        cost_estimate=pl.CostEstimate(
            flops=18 * total * width * width, bytes_accessed=18 * width * width, transcendentals=0
        ),
    )(own, act, near, farther, weights, *extra)


CHUNK = 128


def chunks(total, fn):
    def step(i, carry):
        fn(pl.multiple_of(i * CHUNK, CHUNK))
        return carry

    lax.fori_loop(0, total // CHUNK, step, 0)


def grad_two_body(rows_of, even, edge, extra, outs):
    (out,) = outs

    def one(start):
        out[pl.ds(start, CHUNK), :] = rows_of(start, CHUNK)

    chunks(out.shape[0], one)


def copy_edges(even, edge, full, near, farther):
    total = full.shape[0]
    first = full[:edge]
    last = full[total - edge :]
    near[...] = jnp.where(even, last, first)
    farther[...] = jnp.where(even, first, last)


def conv_one_body(rows_of, even, edge, extra, outs):
    grad_ref, gain_ref = extra
    act_ref, act_near, act_far, d_ref, d_near, d_far = outs
    total = act_ref.shape[0]
    gain = gain_ref[...]

    def one(start):
        rows = pl.ds(start, CHUNK)
        conv = rows_of(start, CHUNK)
        r = rms(conv)
        hat = conv * r
        act, slope = silu_parts(hat * gain)
        act_ref[rows, :] = act.astype(BF16)
        g = grad_ref[rows, :] * slope * gain
        d_ref[rows, :] = (r * (g - hat * jnp.mean(g * hat, axis=-1, keepdims=True))).astype(BF16)

    chunks(total, one)
    copy_edges(even, edge, act_ref, act_near, act_far)
    copy_edges(even, edge, d_ref, d_near, d_far)


def conv_two_body(rows_of, even, edge, extra, outs):
    (lifted_ref,) = extra
    (out,) = outs

    def one(start):
        rows = pl.ds(start, CHUNK)
        out[rows, :] = (lifted_ref[rows, :].astype(F32) + rows_of(start, CHUNK)).astype(BF16)

    chunks(out.shape[0], one)


def grad_main_kernel(edge, act_ref, w_ref, y_ref, x_ref):
    step = pl.program_id(0)
    total, width = act_ref.shape

    @pl.when(step == 0)
    def _():
        blank = jnp.zeros((edge, width), BF16)
        x_ref[:edge, :width] = blank
        x_ref[edge:, :width] = act_ref[: total - edge]
        x_ref[:, width : 2 * width] = act_ref[...]
        x_ref[: total - edge, 2 * width :] = act_ref[edge:]
        x_ref[total - edge :, 2 * width :] = blank

    conv_step(w_ref, x_ref, y_ref, step, True)


def grad_main(act, weights, edge):
    total, width = act.shape
    return pl.pallas_call(
        functools.partial(grad_main_kernel, edge),
        name="grad_main",
        out_shape=pltpu.VMEM((3, total, width), F32),
        grid_spec=pltpu.PrefetchScalarGridSpec(
            num_scalar_prefetch=0,
            grid=(3,),
            in_specs=[
                whole((total, width)),
                pl.BlockSpec((1, 3, width, width), lambda p, *_: (p, 0, 0, 0)),
            ],
            out_specs=whole((3, total, width)),
            scratch_shapes=[pltpu.VMEM((total, 3 * width), BF16)],
        ),
        compiler_params=params(14),
        cost_estimate=pl.CostEstimate(
            flops=18 * total * width * width, bytes_accessed=18 * width * width, transcendentals=0
        ),
    )(act, weights)


def grad_tail_kernel(nr, own_s, near_ref, farther_ref, w_ref, y_ref, lifted_ref, cot_ref, gain_ref,
                     wo_ref, d_lifted_ref, d_mixed_ref, z_ref):
    edge = near_ref.shape[0]
    total = d_lifted_ref.shape[0]
    even = lax.rem(own_s[0], 2) == 0
    near = near_ref[...]
    farther = farther_ref[...]
    left = jnp.where(even, farther, near)
    right = jnp.where(even, near, farther)
    for p in range(3):
        z_ref[0, p] = mm_t(left, w_ref[p, 2])
        z_ref[1, p] = mm_t(right, w_ref[p, 0])
    gain = gain_ref[...]
    split = (edge // nr + 1) // 2 * nr
    for start in range(0, total, edge):
        for first, last in ((0, split), (split, edge)):
            size = last - first
            rows = slice(start + first, start + last)
            taps = []
            for p in range(3):
                tap = y_ref[p, rows]
                if start == 0:
                    tap = tap + z_ref[0, p, first:last]
                if start == total - edge:
                    tap = tap + z_ref[1, p, first:last]
                taps.append(tap)
            place = lax.broadcasted_iota(jnp.int32, (size, 1), 0) % nr
            conv = (
                jnp.where(place == 0, 0.0, pltpu.roll(taps[2], 1, 0))
                + taps[1]
                + jnp.where(place == nr - 1, 0.0, pltpu.roll(taps[0], size - 1, 0))
            )
            lifted = lifted_ref[rows].astype(F32)
            r = rms(lifted)
            hat = lifted * r
            _, slope = silu_parts(hat * gain)
            g = conv * slope * gain
            back = r * (g - hat * jnp.mean(g * hat, axis=-1, keepdims=True))
            d_lifted_ref[rows] = cot_ref[rows].astype(F32) + back
    d_mixed_ref[...] = mm_t(d_lifted_ref[...].astype(BF16), wo_ref[...]).astype(BF16)


def grad_tail(own, near, farther, weights, y, lifted, cot, gain, wo, nr):
    args = (near, farther, weights, y, lifted, cot, gain, wo)
    edge, width = near.shape
    outs = (pltpu.VMEM(lifted.shape, F32), pltpu.VMEM(lifted.shape, BF16))
    return pl.pallas_call(
        functools.partial(grad_tail_kernel, nr),
        name="grad_tail",
        out_shape=outs,
        grid_spec=pltpu.PrefetchScalarGridSpec(
            num_scalar_prefetch=1,
            grid=(1,),
            in_specs=[whole(x.shape) for x in args],
            out_specs=[whole(x.shape) for x in outs],
            scratch_shapes=[pltpu.VMEM((2, 3, edge, width), F32)],
        ),
        compiler_params=params(14),
    )(own, *args)


def head_norm_back(grad, hat, r, ones, head):
    hat = hat.astype(F32)
    return r * (grad - hat * head_mean(grad * hat, ones, head))


def drift_rows(head, dm, mixed, row):
    width = dm.shape[1]
    lanes = lax.broadcasted_iota(jnp.int32, (PAD, width), 1) // head
    picked = (lanes == lax.broadcasted_iota(jnp.int32, (PAD, width), 0)).astype(BF16)
    product = (dm.astype(F32) * mixed.astype(F32)).astype(BF16)
    return mm_t(picked, product)[:HEADS] * row


def pair_queries(p, q, dm, col, drift, low):
    cols = slice(128 * p, 128 * (p + 1))
    spread = jnp.where(low, col[:, 2 * p : 2 * p + 1], col[:, 2 * p + 1 : 2 * p + 2])
    q2 = pair_rows(q[:, cols], low)
    dm2 = pair_rows((dm[:, cols].astype(F32) * spread).astype(BF16), low)
    shift = jnp.concatenate([drift[2 * p : 2 * p + 1], drift[2 * p + 1 : 2 * p + 2]], axis=1)
    return q2, dm2, shift


def far_grads_kernel(head, picks, own_s, lists_s, counts_s, q_ref, vf_ref, e_ref, dm_ref, mixed_ref,
                     row_ref, col_ref, kf_ref, rf_ref, wk_ref, wv_ref, send_ref, kgrad, vgrad, shares, sems):
    c = pl.program_id(0)
    own = own_s[0]
    cams, blk, width = mixed_ref.shape
    low = lax.broadcasted_iota(jnp.int32, (blk, 128), 1) < head
    q = q_ref[0]
    dm = dm_ref[:, c].reshape(blk, width)
    drift = drift_rows(head, dm, mixed_ref[c], row_ref[c])
    col = col_ref[c]
    for p in range(width // 128):
        cols = slice(128 * p, 128 * (p + 1))
        q2, dm2, shift = pair_queries(p, q, dm, col, drift, low)
        far_v = jnp.concatenate([vf_ref[lists_s[c, s, own], :, cols] for s in range(picks)], axis=0)
        e = e_ref[c, p, blk:]
        d_scaled = (e.astype(F32) * (mm_t(far_v, dm2) - shift)).astype(BF16)
        kgrad[c, :, cols] = mm(d_scaled, q2)
        vgrad[c, :, cols] = mm(e, dm2).astype(BF16)

    @pl.when(c == cams - 1)
    def _():
        ones_h = head_ones(width // 2, head)

        def back(i, carry):
            grad = head_norm_back(kgrad[i], kf_ref[i], rf_ref[i], ones_h, head)
            shares[i] = grad.astype(BF16)
            return carry

        lax.fori_loop(0, cams, back, 0)
        shape = (picks * blk, width)
        for first, last in ((0, (cams + 1) // 2), ((cams + 1) // 2, cams)):
            count = last - first
            share = mm_t(shares[first:last].reshape(count * shape[0], width), wk_ref[...])
            share = share + mm_t(vgrad[first:last].reshape(count * shape[0], width), wv_ref[...])
            shares[first:last] = share.astype(BF16).reshape((count,) + shape)
            for i in range(first, last):
                for s in range(picks):
                    pltpu.make_async_copy(
                        shares.at[i, pl.ds(s * blk, blk)],
                        send_ref.at[lists_s[i, s, own]],
                        sems.at[i, s],
                    ).start()
        for i in range(cams):
            for s in range(picks):
                pltpu.make_async_copy(
                    shares.at[i, pl.ds(s * blk, blk)], send_ref.at[0], sems.at[i, s]
                ).wait()


def far_grads(own, lists, counts, n_cols, q, vf, e, dm_t, mixed, row, col, kf, rf, wk, wv, head):
    cams, blk, width = mixed.shape
    picks = lists.shape[1]
    args = (vf, e, dm_t, mixed, row, col, kf, rf, wk, wv)
    return pl.pallas_call(
        functools.partial(far_grads_kernel, head, picks),
        name="far_grads",
        out_shape=pltpu.HBM((n_cols, blk, width), BF16),
        grid_spec=pltpu.PrefetchScalarGridSpec(
            num_scalar_prefetch=3,
            grid=(cams,),
            in_specs=[per_camera(q)] + [whole(x.shape) for x in args],
            out_specs=pl.BlockSpec(memory_space=pltpu.HBM),
            scratch_shapes=[
                pltpu.VMEM((cams, picks * blk, width), F32),
                pltpu.VMEM((cams, picks * blk, width), BF16),
                pltpu.VMEM((cams, picks * blk, width), BF16),
                pltpu.SemaphoreType.DMA((cams, picks)),
            ],
        ),
        compiler_params=params(4 + 6 * picks),
    )(own, lists, counts, hbm(q), *args)


def own_grads_kernel(head, picks, own_s, lists_s, q_ref, k_ref, v_ref, rq_ref, rk_ref, vf_ref, e_ref, dm_ref,
                     mixed_ref, row_ref, col_ref, kf_ref, wq_ref, wk_ref, wv_ref, out_ref):
    c = pl.program_id(0)
    own = own_s[0]
    cams, blk, width = mixed_ref.shape
    low = lax.broadcasted_iota(jnp.int32, (blk, 128), 1) < head
    ones_h = head_ones(width // 2, head)
    scale = head ** (-0.5)
    q = q_ref[0]
    dm = dm_ref[:, c].reshape(blk, width)
    drift = drift_rows(head, dm, mixed_ref[c], row_ref[c])
    col = col_ref[c]
    listed = [lists_s[c, s, own] for s in range(picks)]
    dq, dk, dv = [], [], []
    for p in range(width // 128):
        cols = slice(128 * p, 128 * (p + 1))
        q2, dm2, shift = pair_queries(p, q, dm, col, drift, low)
        all_v = jnp.concatenate([v_ref[0, :, cols]] + [vf_ref[i, :, cols] for i in listed], axis=0)
        all_k = jnp.concatenate([k_ref[0, :, cols], kf_ref[c, :, cols]], axis=0)
        e = e_ref[c, p]
        d_scaled = (e.astype(F32) * (mm_t(all_v, dm2) - shift)).astype(BF16)
        dk.append(mm(d_scaled[:blk], q2))
        dv.append(mm(e[:blk], dm2).astype(BF16))
        both = mm(jnp.transpose(d_scaled), all_k)
        dq.append(jnp.where(low, both[:blk], both[blk:]) * scale)
    dq, dk, dv = (jnp.concatenate(parts, axis=1) for parts in (dq, dk, dv))
    q_hat = q.astype(F32) * (1.0 / scale)
    dq = head_norm_back(dq, q_hat, rq_ref[0], ones_h, head).astype(BF16)
    dk = head_norm_back(dk, k_ref[0], rk_ref[0], ones_h, head).astype(BF16)
    out_ref[0] = mm_t(dq, wq_ref[...]) + mm_t(dk, wk_ref[...]) + mm_t(dv, wv_ref[...])


def own_grads(own, lists, q, k, v, rq, rk, vf, e, dm_t, mixed, row, col, kf, wq, wk, wv, head):
    cams, blk, width = mixed.shape
    picks = lists.shape[1]
    windows = (q, k, v, rq, rk)
    args = (vf, e, dm_t, mixed, row, col, kf, wq, wk, wv)
    return pl.pallas_call(
        functools.partial(own_grads_kernel, head, picks),
        name="own_grads",
        out_shape=pltpu.HBM((cams, blk, width), F32),
        grid_spec=pltpu.PrefetchScalarGridSpec(
            num_scalar_prefetch=2,
            grid=(cams,),
            in_specs=[per_camera(x) for x in windows] + [whole(x.shape) for x in args],
            out_specs=per_camera(mixed),
        ),
        compiler_params=params(6 + picks),
        cost_estimate=pl.CostEstimate(
            flops=20 * cams * blk * width * width, bytes_accessed=4 * e.size, transcendentals=0
        ),
    )(own, lists, *map(hbm, windows), *args)


def final_kernel(table_s, back_ref, rows_ref, clip_ref, dl_ref, gain_ref, out_ref, acc):
    tw, cams, nr, width = clip_ref.shape
    blk = tw * nr
    acc[...] = rows_ref[...]

    def add(i, carry):
        cam = table_s[i]

        @pl.when(cam >= 0)
        def _():
            acc[cam] += back_ref[i].astype(F32)

        return carry

    lax.fori_loop(0, back_ref.shape[0], add, 0)
    gain = gain_ref[...]

    def one(c, carry):
        x = clip_ref[:, c].reshape(blk, width).astype(F32)
        r = rms(x)
        hat = x * r
        g = acc[c] * gain
        d = dl_ref[:, c].reshape(blk, width) + r * (
            g - hat * jnp.mean(g * hat, axis=-1, keepdims=True)
        )
        out_ref[:, c] = d.astype(BF16).reshape(tw, nr, width)
        return carry

    lax.fori_loop(0, cams, one, 0)


def final(table, back, rows, clip_t, d_lifted, gain):
    args = (back, rows, clip_t, d_lifted, gain)
    return pl.pallas_call(
        final_kernel,
        name="final",
        out_shape=jax.ShapeDtypeStruct(clip_t.shape, BF16),
        grid_spec=pltpu.PrefetchScalarGridSpec(
            num_scalar_prefetch=1,
            grid=(1,),
            in_specs=[whole(x.shape) for x in args],
            out_specs=whole(clip_t.shape),
            scratch_shapes=[pltpu.VMEM(rows.shape, F32)],
        ),
        compiler_params=params(8),
    )(table, *args)


def exchange_edges(near, farther):
    size = lax.axis_size("cols")
    inner = [(i, i ^ 1) for i in range(size)]
    outer = [(i, i + 1 if i % 2 else i - 1) for i in range(1, size - 1)]
    return lax.ppermute(near, "cols", inner), lax.ppermute(farther, "cols", outer)


def local(
    clip_tokens,
    cotangent,
    gain_attn,
    w_query,
    w_key,
    w_value,
    w_out,
    gain_first,
    conv_first,
    gain_second,
    conv_second,
    matching,
    block_lists,
    counts,
):
    views, nr, tw, width = clip_tokens.shape
    head = width // HEADS
    n_cols = lax.axis_size("cols")
    own_index = lax.axis_index("cols").astype(jnp.int32)
    own = own_index.reshape(1)
    total = views * nr * tw
    blk = nr * tw
    flat = (total, width)
    slabs = (tw, views, nr, width)
    block_lists = jnp.transpose(block_lists, (0, 2, 1))
    gain_attn = gain_attn.reshape(1, width)
    gain_first = gain_first.reshape(1, width)
    gain_second = gain_second.reshape(1, width)

    clip_t = jnp.transpose(clip_tokens, (2, 0, 1, 3))
    cot_t = jnp.transpose(cotangent, (2, 0, 1, 3))
    odd = own_index % 2
    last = (tw - 1) * (1 - odd)
    cot_near = lax.dynamic_index_in_dim(cot_t, last, 0, keepdims=False).reshape(-1, width)
    cot_far = lax.dynamic_index_in_dim(cot_t, tw - 1 - last, 0, keepdims=False).reshape(-1, width)

    rows, send = prep(n_cols, own, matching, block_lists, counts, clip_t, gain_attn)
    cot_near, cot_far = exchange_edges(cot_near, cot_far)
    arrived = lax.all_to_all(send, "cols", split_axis=0, concat_axis=0, tiled=True)
    rows, w_value, lists, live = lax.optimization_barrier((rows, w_value, block_lists, counts))
    w_value_t = w_value.T
    slots = jnp.arange(lists.shape[1], dtype=jnp.int32)
    asks = (lists == own_index) & (slots[None, :, None] < live[:, None, :])
    table = jnp.sum(jnp.where(asks, matching[:, None, None] + 1, 0), axis=(0, 1)) - 1
    q, k, v, vt, rq, rk = project(rows.reshape(flat), w_query, w_key, w_value, w_value_t, head, blk)
    q, k, v, rq, rk = (a.reshape(views, blk, width) for a in (q, k, v, rq, rk))
    arrived, q, k, v, vt, rq, rk = lax.optimization_barrier((arrived, q, k, v, vt, rq, rk))
    lifted, act_one, near, farther, kf, rf, e, row, col, mixed = attend(
        own, block_lists, counts, arrived, q, k, vt, clip_t, w_key, w_value_t, w_out, gain_first, head
    )
    edge = (views * nr, width)
    near, farther = exchange_edges(near.reshape(edge), farther.reshape(edge))
    (d_act_two,) = conv_call(
        "grad_two", grad_two_body, own, cot_t.reshape(flat), cot_near, cot_far, hbm(conv_second),
        (), (pltpu.VMEM(flat, F32),), nr, True,
    )
    flat_bf = pltpu.VMEM(flat, BF16)
    edge_bf = jax.ShapeDtypeStruct(edge, BF16)
    act_two, act_near, act_far, d_conv, d_near, d_far = conv_call(
        "conv_one", conv_one_body, own, act_one.reshape(flat), near, farther, conv_first,
        (d_act_two, gain_second),
        (flat_bf, edge_bf, edge_bf, flat_bf, edge_bf, edge_bf), nr, False,
    )
    d_near, d_far = exchange_edges(d_near, d_far)
    d_conv, fetched = lax.optimization_barrier((d_conv, arrived))
    vf = far_values(fetched.reshape(-1, width), w_value)
    y_grad = grad_main(d_conv, conv_first, views * nr)
    d_near, d_far, vf, y_grad = lax.optimization_barrier((d_near, d_far, vf, y_grad))
    vf = vf.reshape(arrived.shape)
    d_lifted, d_mixed = grad_tail(
        own, d_near, d_far, conv_first, y_grad, lifted.reshape(flat), cot_t.reshape(flat), gain_first, w_out, nr
    )
    d_mixed, act_near, act_far = lax.optimization_barrier((d_mixed, act_near, act_far))
    d_mixed = d_mixed.reshape(slabs)
    act_near, act_far = exchange_edges(act_near, act_far)
    send_back = far_grads(
        own, block_lists, counts, n_cols, q, vf, e, d_mixed, mixed, row, col, kf, rf, w_key, w_value, head
    )
    send_back, act_near, act_far = lax.optimization_barrier((send_back, act_near, act_far))
    back = lax.all_to_all(send_back, "cols", split_axis=0, concat_axis=0, tiled=True)
    (result,) = conv_call(
        "conv_two", conv_two_body, own, act_two, act_near, act_far, conv_second,
        (lifted.reshape(flat),), (jax.ShapeDtypeStruct(flat, BF16),), nr, False,
    )
    d_rows = own_grads(
        own, block_lists, q, k, v, rq, rk, vf, e, d_mixed, mixed, row, col, kf, w_query, w_key, w_value, head
    )
    d_clip = final(table, back, d_rows, clip_t, d_lifted.reshape(slabs), gain_attn)
    return (
        jnp.transpose(result.reshape(slabs), (1, 2, 0, 3)),
        jnp.transpose(d_clip, (1, 2, 0, 3)),
    )


def solution(mesh):
    tiles = P("groups", None, "cols", None)
    in_specs = (tiles, tiles) + (P(),) * 12
    return jax.shard_map(
        local, mesh=mesh, in_specs=in_specs, out_specs=(tiles, tiles), check_vma=False
    )
```
